32 devices in a mesh: fsdp: 4 (over x, core), seq: 8 (over z, y).
Axes of the slice: x: 2, y: 2, z: 4, core: 2. Of those that a mesh axis runs over, the one named last changes fastest.
Arguments:
- tokens: bfloat16 [4, 2048, 2304], P('fsdp', 'seq'), may hold values from -6 to 6
- norm_gain: float32 [2304], replicated, may hold values from 0.5 to 1.5
- w_qkv: bfloat16 [3, 2304, 1152], P(None, 'seq', 'fsdp'), may hold values from -0.125 to 0.125
- q_gain: float32 [96], replicated, may hold values from 0.8 to 7, as said below
- k_gain: float32 [96], replicated, may hold values from 0.8 to 7, as said below
- img_blocks: int32 [4, 8], replicated, may hold values from 1 to 4, 16 in all within a row
- img_width: int32 [4, 8], replicated, may hold values from 8 to 32
Outputs:
- attended: bfloat16 [4, 2048, 1152], P('fsdp', 'seq')
The draws below stay inside these ranges and needn't reach their ends.
Inputs may be any that keep to these rules, and one draw needn't show every extreme that they name: `img_blocks`: row p lists the lengths, in blocks of 128 tokens, of the 8 images of pack p in order; they sum to 16, and the longest is 4 blocks. `q_gain`: the same for every head. `k_gain`: the same for every head.
All inputs are finite; a program needn't handle non-finite values.
Results may differ from the reference program's by a relative error of at most 0.0045.
The reference program's roundings to bfloat16 on the way count: a program that leaves them out, or rounds other values in their place, can miss the bound.
Values may be sent and summed in bfloat16 or wider, within the bound.
A program may use at most 64 MiB of HBM per device.

```python
import math
import jax
import jax.numpy as jnp
import numpy as np
from jax import lax

D = 2304
HEAD = 96
HEADS = 12
BLOCK = 128
MAXB = 4
TOK_DEV = 256
PACKS = 4
SEQLEN = 2048
HW = 1152
NBLK = 16
NIMG = 8
REACH = 2
N_SEQ = 8


def draw_gain_common(key, salt):
    inner = jax.random.fold_in(key, salt)
    return jax.random.uniform(inner, (HEAD,), jnp.float32, 0.8, 1.3)


def draw_q_gain(key, part):
    return draw_gain_common(key, 11)


def draw_k_gain(key, part):
    return draw_gain_common(key, 23)


def set_ends(array, own_key, least, top_value):
    dims = array.shape
    place = [jax.random.randint(jax.random.fold_in(own_key, axis), (), 0, dims[axis]) for axis in range(len(dims))]
    array = array.at[tuple(place)].set(least)
    longest = dims.index(max(dims))
    place[longest] = (place[longest] + 1) % dims[longest]
    return array.at[tuple(place)].set(top_value)


def block_scale(key, shape, shards, least, top_value):
    loudness = 1.0
    for axis_at, parts in shards:
        heights = jax.random.uniform(jax.random.fold_in(jax.random.fold_in(key, 6), axis_at), (parts,), jnp.float32, least / len(shards), top_value / len(shards))
        loudness = loudness * jnp.repeat(jnp.exp(heights), shape[axis_at] // parts).reshape((-1,) + (1,) * (len(shape) - 1 - axis_at))
    return loudness


def profile(count, total, bound, lean):
    portions = [(1 << 20) // math.isqrt(grade ** lean) + 1 for grade in range(2, count + 1)]
    spare, counts = total - bound - (count - 1), [1] * (count - 1)
    while spare > 0:
        candidates = [i for i in range(count - 1) if counts[i] < bound]
        pool, budget = sum([portions[i] for i in candidates]), spare
        for i in candidates:
            addition = min(bound - counts[i], max(1, budget * portions[i] // pool), spare)
            counts[i] = counts[i] + addition
            spare = spare - addition
    return np.array([bound] + counts)


def uneven_parts(stream_key, number_of, total, most, lean):
    if number_of == 2:
        one = jax.random.randint(stream_key, (), max(1, total - most), min(most, total - 1) + 1)
        return jnp.stack([one, total - one])
    lengths = jnp.asarray(profile(number_of, total, most, lean), jnp.int32)
    pairs = (number_of - 1) // 2
    giver, receiver = lengths[1:1 + 2 * pairs:2], lengths[2:2 + 2 * pairs:2]
    room = jnp.minimum(giver - 1, most - receiver)
    passed = jax.random.randint(jax.random.fold_in(stream_key, 1), (pairs,), 0, 1 << 20) % (room + 1)
    lengths = lengths.at[1:1 + 2 * pairs:2].set(giver - passed).at[2:2 + 2 * pairs:2].set(receiver + passed)
    return lengths[jax.random.permutation(jax.random.fold_in(stream_key, 2), number_of)]


def bell_draw(key, shape, width, reach, pieces=(), kind=jnp.bfloat16):
    drawn = jax.random.normal(key, shape, jnp.float32) * width
    if len(pieces) > 0:
        drawn = block_scale(key, shape, pieces, -0.22, 0.18) * drawn
    return jnp.clip(drawn, min=-reach, max=reach).astype(kind)


def setup_inputs(seed: int = 0) -> dict:
    seeds = jax.random.split(jax.random.key(seed), 8)
    return {
        "tokens": bell_draw(seeds[0], (PACKS, SEQLEN, D), 1.0, 6.0, ((0, 4), (1, 8))),
        "norm_gain": jnp.clip(1.0 + 0.1 * jax.random.normal(seeds[1], (D,), jnp.float32), 0.5, 1.5),
        "w_qkv": bell_draw(seeds[2], (3, D, HW), D ** -0.5, 0.125, ((1, 8), (2, 4))),
        "q_gain": draw_q_gain(jax.random.fold_in(seeds[7], 71), 0),
        "k_gain": draw_k_gain(jax.random.fold_in(seeds[7], 71), 0),
        "img_blocks": jax.vmap(lambda own: uneven_parts(own, NIMG, NBLK, MAXB, 2))(jax.random.split(seeds[5], PACKS)).reshape((PACKS, NIMG)).astype(jnp.int32),
        "img_width": set_ends(jax.random.randint(seeds[6], (PACKS, NIMG), 8, 33), jax.random.fold_in(seeds[6], 1), 8, 32).astype(jnp.int32),
    }


eps_model = 1e-06

def rms_norm(values, gain):
    return values * lax.rsqrt(lax.optimization_barrier(jnp.mean(values * values, axis=-1, keepdims=True)) + eps_model) * gain

def locate(blocks, widths, where, seq_total):
    starts = (jnp.cumsum(blocks, dtype=jnp.int32) - blocks) * BLOCK
    inside = (where[:, None] >= starts[None, :]).astype(jnp.int32)
    segment = lax.optimization_barrier(jnp.sum(inside, axis=1, dtype=jnp.int32)) - 1
    onehot = (segment[:, None] == jnp.arange(blocks.shape[0], dtype=jnp.int32)[None, :]).astype(jnp.int32)
    begin = lax.optimization_barrier(jnp.sum(onehot * starts[None, :], axis=1, dtype=jnp.int32))
    across = jnp.maximum(lax.optimization_barrier(jnp.sum(onehot * widths[None, :], axis=1, dtype=jnp.int32)), 1)
    offset = where - begin
    valid = (where >= 0) & (where < seq_total)
    return (jnp.where(valid, segment, -1), offset // across, offset % across)

def rotate(values, angle):
    pairs = angle.shape[-1]
    cosine = jnp.cos(angle)[..., None, :]
    sine = jnp.sin(angle)[..., None, :]
    first = values[..., :pairs]
    second = values[..., pairs:]
    return jnp.concatenate([first * cosine - second * sine, second * cosine + first * sine], axis=-1)

def rotary(values, row_pos, col_pos):
    half = values.shape[-1] // 2
    pairs = half // 2
    freq = 10000.0 ** (-jnp.arange(pairs, dtype=jnp.float32) / pairs)
    row_angle = row_pos.astype(jnp.float32)[..., None] * freq
    col_angle = col_pos.astype(jnp.float32)[..., None] * freq
    return jnp.concatenate([rotate(values[..., :half], row_angle), rotate(values[..., half:], col_angle)], axis=-1)

def softmax_mix(queries, key_rows, value_rows, seg_query, seg_key):
    scores = jnp.einsum('thd,shd->hts', queries.astype(jnp.float32), key_rows.astype(jnp.float32)) * HEAD ** (-0.5)
    mask = (seg_query[:, None] == seg_key[None, :])[None]
    top = lax.optimization_barrier(jnp.max(jnp.where(mask, scores, -1e+30), axis=-1, keepdims=True))
    expo = jnp.exp(jnp.where(mask, scores - top, -1e+30))
    weights = (expo / lax.optimization_barrier(jnp.sum(expo, axis=-1, keepdims=True))).astype(jnp.bfloat16)
    return jnp.einsum('hts,shd->thd', weights.astype(jnp.float32), value_rows.astype(jnp.float32)).astype(jnp.bfloat16)

def one_pack(tokens, norm_gain, w_qkv, q_gain, k_gain, blocks, widths):
    normed = rms_norm(tokens.astype(jnp.float32), norm_gain).astype(jnp.bfloat16)
    where = jnp.arange(SEQLEN, dtype=jnp.int32)
    segment, row_pos, col_pos = locate(blocks, widths, where, SEQLEN)
    head_shape = (SEQLEN, HEADS, HEAD)
    queries = jnp.dot(normed, w_qkv[0], preferred_element_type=jnp.float32).reshape(head_shape)
    queries = rotary(rms_norm(queries, q_gain), row_pos, col_pos).astype(jnp.bfloat16)
    key_rows = jnp.dot(normed, w_qkv[1], preferred_element_type=jnp.float32).reshape(head_shape)
    key_rows = rotary(rms_norm(key_rows, k_gain), row_pos, col_pos).astype(jnp.bfloat16)
    value_rows = jnp.dot(normed, w_qkv[2], preferred_element_type=jnp.float32).reshape(head_shape).astype(jnp.bfloat16)
    margin = REACH * TOK_DEV
    window = (2 * REACH + 1) * TOK_DEV
    padding = ((margin, margin), (0, 0), (0, 0))
    key_pad = jnp.pad(key_rows, padding)
    value_pad = jnp.pad(value_rows, padding)
    seg_pad = jnp.pad(segment, (margin, margin), constant_values=-1)

    def block_out(index):
        start = (index * TOK_DEV).astype(jnp.int32)
        query_block = lax.dynamic_slice_in_dim(queries, start, TOK_DEV, 0)
        seg_block = lax.dynamic_slice_in_dim(segment, start, TOK_DEV, 0)
        key_block = lax.dynamic_slice_in_dim(key_pad, start, window, 0)
        value_block = lax.dynamic_slice_in_dim(value_pad, start, window, 0)
        seg_keys = lax.dynamic_slice_in_dim(seg_pad, start, window, 0)
        return softmax_mix(query_block, key_block, value_block, seg_block, seg_keys)
    mixed = lax.map(block_out, jnp.arange(N_SEQ, dtype=jnp.int32))
    return mixed.reshape(SEQLEN, HEADS * HEAD)

def reference(tokens, norm_gain, w_qkv, q_gain, k_gain, img_blocks, img_width):
    outputs = []
    for pack_index in range(PACKS):
        outputs.append(one_pack(tokens[pack_index], norm_gain, w_qkv, q_gain, k_gain, img_blocks[pack_index], img_width[pack_index]))
    return jnp.stack(outputs)
```

```python
import functools

import jax
import jax.numpy as jnp
import numpy as np
from jax import lax
from jax.experimental import pallas as pl
from jax.experimental.pallas import tpu as pltpu
from jax.sharding import PartitionSpec as P

HEAD = 96
BLOCK = 128
HALO = 3 * BLOCK
MESH = pl.DeviceIdType.MESH

eps_model = 1e-06


def rms_norm(values, gain):
    return values * lax.rsqrt(jnp.mean(values * values, axis=-1, keepdims=True) + eps_model) * gain


def place():
    f = lax.axis_index("fsdp")
    s = lax.axis_index("seq")
    return f // 2, f % 2, s // 2, s % 2, f, s


def remote(src, dst, send, recv, f, s):
    return pltpu.make_async_remote_copy(
        src_ref=src, dst_ref=dst, send_sem=send, recv_sem=recv,
        device_id={"fsdp": f, "seq": s}, device_id_type=MESH,
    )


def signal(sem, f, s):
    pl.semaphore_signal(sem, inc=1, device_id={"fsdp": f, "seq": s}, device_id_type=MESH)


def gather_kernel(planes, raw_ref, gain_ref, parts_ref, blocks_ref, widths_ref, freq_ref,
                  t_ref, wall_ref, cos_ref, sin_ref,
                  tok_ref, w_ref, tok_send, tok_recv, w_send, w_recv, local_sem):
    x, c, a, b, f, s = place()
    rows = tok_ref.shape[0]
    half = rows // 2
    other = s + 1 - 2 * b
    home = c == b
    barrier = pltpu.get_barrier_semaphore()
    signal(barrier, 2 * x + 1 - c, s)
    for core in range(2):
        signal(barrier, 2 * (1 - x) + core, s)
        signal(barrier, 2 * x + core, other)

    @pl.when(a > 0)
    def _():
        signal(barrier, f, s - 2)

    @pl.when(a < planes - 1)
    def _():
        signal(barrier, f, s + 2)

    step = 32

    @pl.loop(0, rows // step)
    def _(i):
        at = pl.ds(pl.multiple_of(i * step, step), step)
        tok_ref[at] = rms_norm(raw_ref[0, at].astype(jnp.float32), gain_ref[...][None]).astype(jnp.bfloat16)

    spare = jnp.zeros((w_ref.shape[0], w_ref.shape[1] - 3 * parts_ref.shape[2]), jnp.bfloat16)
    w_ref[...] = jnp.concatenate([parts_ref[1], parts_ref[2], parts_ref[0], spare], axis=1)
    pl.semaphore_wait(barrier, 5 + (a > 0).astype(jnp.int32) + (a < planes - 1).astype(jnp.int32))

    def part(xx, yy, h):
        return t_ref.at[xx, yy, pl.ds(pl.multiple_of(h * half, half), half)]

    keep = pltpu.make_async_copy(tok_ref, t_ref.at[x, b], local_sem.at[0])
    whole = remote(tok_ref, t_ref.at[x, b], tok_send.at[0], tok_recv.at[6], 2 * x + 1 - c, s)
    along = [remote(tok_ref.at[pl.ds(h * half, half)], part(x, b, h), tok_send.at[1 + h], tok_recv.at[1],
                    2 * (1 - x) + h, s) for h in range(2)]
    across = [remote(tok_ref.at[pl.ds(h * half, half)], part(x, b, h), tok_send.at[1 + h], tok_recv.at[0],
                     2 * x + h, other) for h in range(2)]

    @pl.when(home)
    def _():
        for copy in along:
            copy.start()
        whole.start()
        keep.start()

    @pl.when(jnp.logical_not(home))
    def _():
        for copy in across:
            copy.start()

    keep_w = pltpu.make_async_copy(w_ref, wall_ref.at[s], local_sem.at[1])
    keep_w.start()

    def push(src, slot, way):
        target = (s + 2, s - 2, other)[way]
        return remote(src, wall_ref.at[slot], w_send.at[slot, way], w_recv.at[slot], f, target)

    def spread(src, slot, up, down):
        if up:
            @pl.when(a < planes - 1)
            def _():
                push(src, slot, 0).start()
        if down:
            @pl.when(a > 0)
            def _():
                push(src, slot, 1).start()

        @pl.when(crosses(slot // 2))
        def _():
            push(src, slot, 2).start()

    middle = planes // 2
    bottom, top = 1 - b, 2 * (planes - 1) + 1 - b
    lifts = jnp.logical_not(home) & (a >= middle - 1) & (a < planes - 1)
    drops = jnp.logical_not(home) & (a <= middle) & (a > 0)

    def crosses(k):
        skipped = ((k == 0) & (a >= middle)) | ((k == planes - 1) & (a < middle))
        return jnp.logical_not(home & skipped)

    spread(w_ref, s, True, True)

    size = cos_ref.shape[1]
    lane = lax.broadcasted_iota(jnp.int32, (size, HEAD), 1)
    where = a * size + lax.broadcasted_iota(jnp.int32, (size, HEAD), 0)
    by_row = lane < HEAD // 2
    low = (lane < HEAD // 4) | ((lane >= HEAD // 2) & (lane < 3 * HEAD // 4))
    for px in range(2):
        pack = 2 * px + b

        def image(j, carry):
            start, begin, wide = carry
            inside = where >= start
            begin = jnp.where(inside, start, begin)
            wide = jnp.where(inside, widths_ref[pack, j], wide)
            return start + blocks_ref[pack, j] * BLOCK, begin, wide

        zero = jnp.zeros((size, HEAD), jnp.int32)
        _, begin, wide = lax.fori_loop(0, blocks_ref.shape[1], image, (jnp.int32(0), zero, zero + 1))
        offset = (where - begin).astype(jnp.float32)
        wide = wide.astype(jnp.float32)
        row = jnp.floor((offset + 0.5) / wide)
        col = offset - row * wide
        angle = jnp.where(by_row, row, col) * freq_ref[...]
        cos_ref[px] = jnp.cos(angle)
        sine = jnp.sin(angle)
        sin_ref[px] = jnp.where(low, -sine, sine)

    mine = [(x, 1 - b), (1 - x, b), (1 - x, 1 - b)]

    def share(k):
        spot = part(mine[k][0], mine[k][1], c)
        return remote(spot, spot, tok_send.at[3 + k], tok_recv.at[3 + k], 2 * x + 1 - c, s)

    def landed(k):
        spot = part(mine[k][0], mine[k][1], c)
        return remote(spot, spot, tok_send.at[3 + k], tok_recv.at[k], 2 * x + 1 - c, s)

    spot = part(x, 1 - b, c)
    relay = remote(spot, spot, tok_send.at[6], tok_recv.at[2], 2 * (1 - x) + c, s)
    def hop(d, carry):
        lower = a - d
        upper = a + d

        @pl.when(lower >= 0)
        def _():
            slot = jnp.maximum(2 * lower + b, 0)
            push(wall_ref.at[slot], slot, 0).wait_recv()
            spread(wall_ref.at[slot], slot, True, False)

        @pl.when(upper < planes)
        def _():
            slot = jnp.minimum(2 * upper + b, 2 * planes - 1)
            push(wall_ref.at[slot], slot, 1).wait_recv()
            spread(wall_ref.at[slot], slot, False, True)

        return carry

    lax.fori_loop(1, 2, hop, 0)
    landed(0).wait_recv()
    relay.start()
    share(0).start()
    lax.fori_loop(2, 3, hop, 0)

    @pl.when(lifts)
    def _():
        push(wall_ref.at[bottom], bottom, 0).wait_recv()
        push(wall_ref.at[bottom], bottom, 0).start()

    @pl.when(drops)
    def _():
        push(wall_ref.at[top], top, 1).wait_recv()
        push(wall_ref.at[top], top, 1).start()

    lax.fori_loop(3, planes, hop, 0)
    landed(1).wait_recv()
    share(1).start()
    landed(2).wait_recv()
    share(2).start()

    def finish(k, carry):
        slot = 2 * k + 1 - b
        early = ((k == 0) & lifts) | ((k == planes - 1) & drops)

        @pl.when(jnp.logical_not(early))
        def _():
            push(wall_ref.at[slot], slot, 2).wait_recv()

        sent = 2 * k + b

        @pl.when(crosses(k))
        def _():
            push(wall_ref.at[sent], sent, 2).wait_send()

        @pl.when((k <= a) & (a < planes - 1))
        def _():
            push(wall_ref.at[sent], sent, 0).wait_send()

        @pl.when((k >= a) & (a > 0))
        def _():
            push(wall_ref.at[sent], sent, 1).wait_send()

        return carry

    lax.fori_loop(0, planes, finish, 0)

    @pl.when(lifts)
    def _():
        push(wall_ref.at[bottom], bottom, 0).wait_send()

    @pl.when(drops)
    def _():
        push(wall_ref.at[top], top, 1).wait_send()

    keep_w.wait()

    @pl.when(home)
    def _():
        for copy in along:
            copy.wait_send()
        whole.wait_send()
        keep.wait()

    @pl.when(jnp.logical_not(home))
    def _():
        for copy in across:
            copy.wait_send()
        whole.wait_recv()

    relay.wait_send()
    for k in range(3):
        share(k).wait_send()
        spot = part(mine[k][0], mine[k][1], 1 - c)
        remote(spot, spot, tok_send.at[3 + k], tok_recv.at[3 + k], 2 * x + 1 - c, s).wait_recv()


def turn(raw, gain, cosine, sine):
    parts = HEAD // 4
    n = rms_norm(raw, gain)
    swapped = jnp.concatenate(
        [n[:, parts:2 * parts], n[:, :parts], n[:, 3 * parts:], n[:, 2 * parts:3 * parts]], axis=1)
    return (n * cosine + swapped * sine).astype(jnp.bfloat16)


def attend_kernel(planes, t_ref, wall_ref, cos_ref, sin_ref, qg_ref, kg_ref, blocks_ref, o_ref,
                  x_ref, w_ref, q_ref, low_win, high_win, mixed, landed, halo_send, halo_recv, out_send, out_recv,
                  local_sem, load_sem):
    x, c, a, b, f, s = place()
    size, width = q_ref.shape[1], q_ref.shape[2]
    rows = size // 2
    inner = size - HALO
    span = HALO + BLOCK
    wins = (low_win, high_win)
    home = c == b
    load_w = pltpu.make_async_copy(wall_ref, w_ref, load_sem.at[2])
    loads = [pltpu.make_async_copy(t_ref.at[p], x_ref.at[p], load_sem.at[p]) for p in range(2)]
    load_w.start()
    for load in loads:
        load.start()
    barrier = pltpu.get_barrier_semaphore()
    has_down, has_up = a > 0, a < planes - 1
    for core in range(4):
        @pl.when(jnp.logical_or(b != c, f != core))
        def _():
            signal(barrier, core, 2 * a + c)

    @pl.when(has_down)
    def _():
        signal(barrier, f, s - 2)

    @pl.when(has_up)
    def _():
        signal(barrier, f, s + 2)

    count = 4 - home.astype(jnp.int32) + has_down.astype(jnp.int32) + has_up.astype(jnp.int32)
    pl.semaphore_wait(barrier, count)

    def upward(p):
        return remote(wins[p].at[pl.ds(HALO + inner, HALO)], wins[p].at[pl.ds(0, HALO)],
                      halo_send.at[p, 0], halo_recv.at[p, 0], f, s + 2)

    def downward(p):
        return remote(wins[p].at[pl.ds(HALO, HALO)], wins[p].at[pl.ds(HALO + size, HALO)],
                      halo_send.at[p, 1], halo_recv.at[p, 1], f, s - 2)

    blank = jnp.zeros((HALO, 2 * width), jnp.bfloat16)

    @pl.when(jnp.logical_not(has_down))
    def _():
        for win in wins:
            win[:HALO] = blank

    @pl.when(jnp.logical_not(has_up))
    def _():
        for win in wins:
            win[HALO + size:] = blank

    heads = width // HEAD
    shift_q = 2 * width // 128 * 128

    def make_keys(p, i):
        first = i * rows
        at = slice(first, first + rows)
        raw = jnp.dot(x_ref[p, at], w_ref[:, :pl.cdiv(2 * width, 128) * 128], preferred_element_type=jnp.float32)
        keys = [turn(raw[:, h * HEAD:(h + 1) * HEAD], kg_ref[...], cos_ref[p, at], sin_ref[p, at])
                for h in range(heads)]
        done = jnp.concatenate(keys + [raw[:, width:2 * width].astype(jnp.bfloat16)], axis=1)
        wins[p][HALO + first:HALO + first + rows] = done

    def make_queries(p, i):
        at = slice(i * rows, (i + 1) * rows)
        raw = jnp.dot(x_ref[p, at], w_ref[:, shift_q:], preferred_element_type=jnp.float32)
        raw = raw[:, 2 * width - shift_q:]
        q_ref[p, at] = jnp.concatenate(
            [turn(raw[:, h * HEAD:(h + 1) * HEAD], qg_ref[...], cos_ref[p, at], sin_ref[p, at])
             for h in range(heads)], axis=1)

    load_w.wait()
    for load in loads:
        load.wait()
    for p in range(2):
        for i in range(2):
            make_keys(p, i)

        make_queries(p, 0)

        @pl.when(has_up)
        def _():
            upward(p).start()

        @pl.when(has_down)
        def _():
            downward(p).start()

    for p in range(2):
        make_queries(p, 1)

    scale = HEAD ** (-0.5) * 1.4426950408889634

    def deliver(p, yy):
        return remote(mixed.at[p, pl.ds(yy * rows, rows)], landed.at[f],
                      out_send.at[p, yy], out_recv.at[f], 2 * p + b, 2 * a + yy)

    def to_self(p, yy):
        return pltpu.make_async_copy(mixed.at[p, pl.ds(yy * rows, rows)], landed.at[f], local_sem.at[2])

    def is_self(p, yy):
        return home & (p == x) & (yy == b)

    for p in range(2):
        pack = 2 * p + b

        @pl.when(has_down)
        def _():
            upward(p).wait_recv()

        @pl.when(has_up)
        def _():
            downward(p).wait_recv()

        def block(i, carry):
            first = pl.multiple_of(i * BLOCK, BLOCK)
            where_q = a * size + i * BLOCK

            def image(j, state):
                start, begin, length = state
                inside = where_q >= start
                blocks = blocks_ref[pack, j] * BLOCK
                return start + blocks, jnp.where(inside, start, begin), jnp.where(inside, blocks, length)

            _, begin, length = lax.fori_loop(0, blocks_ref.shape[1], image,
                                             (jnp.int32(0), jnp.int32(0), jnp.int32(0)))
            back = where_q - begin
            chosen = wins[p][pl.ds(pl.multiple_of(first + HALO, BLOCK), span)]
            for shift in range(BLOCK, HALO + 1, BLOCK):
                earlier = wins[p][pl.ds(pl.multiple_of(first + HALO - shift, BLOCK), span)]
                chosen = jnp.where(back == shift, earlier, chosen)
            mask = lax.broadcasted_iota(jnp.int32, (BLOCK, span), 1) < length
            queries = q_ref[p, pl.ds(first, BLOCK)]
            outs = []
            for h in range(width // HEAD):
                keys = chosen[:, h * HEAD:(h + 1) * HEAD]
                vals = chosen[:, width + h * HEAD:width + (h + 1) * HEAD]
                scores = lax.dot_general(queries[:, h * HEAD:(h + 1) * HEAD], keys, (((1,), (1,)), ((), ())),
                                         preferred_element_type=jnp.float32)
                scores = jnp.where(mask, scores, -1e30)
                top = jnp.max(scores, axis=-1, keepdims=True)
                expo = jnp.exp2((scores - top) * scale)
                norm = jnp.sum(expo, axis=-1, keepdims=True)
                probs = (expo * (1.0 / norm)).astype(jnp.bfloat16)
                outs.append(jnp.dot(probs, vals, preferred_element_type=jnp.float32).astype(jnp.bfloat16))
            mixed[p, pl.ds(first, BLOCK)] = jnp.concatenate(outs, axis=1)
            return carry

        lax.fori_loop(0, size // BLOCK, block, 0)
        for yy in range(2):
            @pl.when(is_self(p, yy))
            def _():
                to_self(p, yy).start()

            @pl.when(jnp.logical_not(is_self(p, yy)))
            def _():
                deliver(p, yy).start()

    for p in range(2):
        for yy in range(2):
            @pl.when(is_self(p, yy))
            def _():
                to_self(p, yy).wait()

            @pl.when(jnp.logical_not(is_self(p, yy)))
            def _():
                deliver(p, yy).wait_send()

        @pl.when(has_up)
        def _():
            upward(p).wait_send()

        @pl.when(has_down)
        def _():
            downward(p).wait_send()

    for core in range(4):
        @pl.when(jnp.logical_or(b != c, f != core))
        def _():
            remote(mixed.at[0, pl.ds(0, rows)], landed.at[core], out_send.at[0, 0], out_recv.at[core], f, s).wait_recv()

    o_ref[0] = jnp.concatenate([landed[core] for core in range(4)], axis=1)


def fused_kernel(planes, raw_ref, gain_ref, parts_ref, qg_ref, kg_ref, freq_ref, blocks_ref, widths_ref, o_ref,
                 own_ref, xa_ref, xb_ref, xd_ref, wkv_ref, wq_ref, okv_ref, oq_ref, cos_ref, sin_ref, q_ref, lead_ref, win_a, win_b, mixed,
                 landed, tok_send, tok_recv, w_send, w_recv, pass_send, halo_send, halo_recv, out_send, out_recv,
                 local_sem):
    x, c, a, b, f, s = place()
    rows = raw_ref.shape[1]
    depth, width = parts_ref.shape[1], parts_ref.shape[2]
    size = 2 * rows
    heads = width // HEAD
    wide = wkv_ref.shape[2]
    extra = wide - 2 * width
    wins = (win_a, win_b)
    span = HALO + BLOCK
    home = c == b
    has_down, has_up = a > 0, a < planes - 1
    mate = 2 * x + 1 - c
    beside = 2 * (1 - x) + c
    other = s + 1 - 2 * b
    packs = (2 * x + c, 2 * (1 - x) + c)
    cut = rows * 5 // 8 // 32 * 32

    barrier = pltpu.get_barrier_semaphore()
    signal(barrier, mate, s)
    signal(barrier, beside, s)
    signal(barrier, f, other)
    signal(barrier, beside, other)

    @pl.when(jnp.logical_not(home))
    def _():
        signal(barrier, mate, other)

    @pl.when(has_down)
    def _():
        signal(barrier, f, s - 2)

    @pl.when(has_up)
    def _():
        signal(barrier, f, s + 2)

    okv_ref[...] = jnp.concatenate([parts_ref[1], parts_ref[2], parts_ref[0, :, :extra]], axis=1)
    oq_ref[...] = jnp.concatenate(
        [parts_ref[0, :, extra:], jnp.zeros((depth, oq_ref.shape[1] - width + extra), jnp.bfloat16)], axis=1)
    count = 4 + jnp.logical_not(home).astype(jnp.int32) + has_down.astype(jnp.int32) + has_up.astype(jnp.int32)
    pl.semaphore_wait(barrier, count)


    def slot_of(plane):
        return 2 * plane + c

    def spot(slot, kind):
        return (wkv_ref, wq_ref)[kind].at[slot]

    def push(plane, kind, way, src=None):
        slot = slot_of(plane)
        target = ((f, s + 2), (f, s - 2), (mate, s))[way]
        return remote(spot(slot, kind) if src is None else src, spot(slot, kind), w_send.at[plane, kind, way], w_recv.at[slot, kind], *target)

    def pass_over(kind):
        return remote((okv_ref, oq_ref)[kind], spot(s, kind), pass_send.at[kind], w_recv.at[s, kind], mate, other)

    def spread(plane, kind, up, down, src=None):
        if up:
            @pl.when(has_up)
            def _():
                push(plane, kind, 0, src).start()
        if down:
            @pl.when(has_down)
            def _():
                push(plane, kind, 1, src).start()
        push(plane, kind, 2, src).start()

    def keep_own(kind):
        return pltpu.make_async_copy((okv_ref, oq_ref)[kind], spot(s, kind), local_sem.at[1 + kind])

    def begin_ring(kind):
        @pl.when(home)
        def _():
            spread(a, kind, True, True, (okv_ref, oq_ref)[kind])
            keep_own(kind).start()

        @pl.when(jnp.logical_not(home))
        def _():
            slot = slot_of(a)
            remote(spot(slot, kind), spot(slot, kind), pass_send.at[kind], w_recv.at[slot, kind], mate, other).wait_recv()
            spread(a, kind, True, True)

    def hop(d, kind):
        @pl.when(a >= d)
        def _():
            plane = jnp.maximum(a - d, 0)
            push(plane, kind, 0).wait_recv()
            spread(plane, kind, True, False)

        @pl.when(a + d < planes)
        def _():
            plane = jnp.minimum(a + d, planes - 1)
            push(plane, kind, 1).wait_recv()
            spread(plane, kind, False, True)

    def from_mate(kind):
        for plane in range(planes):
            slot = 2 * plane + 1 - c
            remote(spot(slot, kind), spot(slot, kind), w_send.at[plane, kind, 2], w_recv.at[slot, kind], mate, s).wait_recv()

    @pl.when(jnp.logical_not(home))
    def _():
        pass_over(0).start()
        pass_over(1).start()

    @pl.when(home)
    def _():
        spread(a, 0, True, True, okv_ref)
        keep_own(0).start()

    def piece(ref, k):
        first, length = ((0, cut), (cut, rows - cut))[k]
        return ref.at[pl.ds(first, length)]

    def along_x(k):
        return remote(piece(own_ref, k), piece(xb_ref, k), tok_send.at[0, k], tok_recv.at[0, k], beside, s)

    def along_y(k):
        return remote(piece(own_ref, k), piece(xa_ref, k), tok_send.at[1, k], tok_recv.at[1, k], f, other)

    def relay_x():
        return remote(piece(xa_ref, 0), piece(xd_ref, 0), tok_send.at[2, 0], tok_recv.at[2, 0], beside, s)

    def relay_y():
        return remote(piece(xb_ref, 1), piece(xd_ref, 1), tok_send.at[2, 1], tok_recv.at[2, 1], f, other)

    def shard_rows(p, mine, first, length):
        ref = ((xd_ref, xb_ref), (xa_ref, own_ref))[p == 0][mine]
        return ref[first:first + length]

    step = 32

    def normalize(i, carry):
        at = pl.ds(pl.multiple_of(i * step, step), step)
        own_ref[at] = rms_norm(raw_ref[0, at].astype(jnp.float32), gain_ref[...][None]).astype(jnp.bfloat16)
        return carry

    lax.fori_loop(0, cut // step, normalize, 0)
    along_y(0).start()
    lax.fori_loop(cut // step, rows // step, normalize, 0)
    along_x(1).start()
    along_x(0).start()
    along_y(1).start()

    lane = lax.broadcasted_iota(jnp.int32, (size, HEAD), 1)
    where = a * size + lax.broadcasted_iota(jnp.int32, (size, HEAD), 0)
    by_row = lane < HEAD // 2
    low = (lane < HEAD // 4) | ((lane >= HEAD // 2) & (lane < 3 * HEAD // 4))

    def tables(p):
        def image(j, carry):
            start, begin, columns = carry
            inside = where >= start
            begin = jnp.where(inside, start, begin)
            columns = jnp.where(inside, widths_ref[packs[p], j], columns)
            return start + blocks_ref[packs[p], j] * BLOCK, begin, columns

        zero = jnp.zeros((size, HEAD), jnp.int32)
        _, begin, columns = lax.fori_loop(0, blocks_ref.shape[1], image, (jnp.int32(0), zero, zero + 1))
        offset = (where - begin).astype(jnp.float32)
        columns = columns.astype(jnp.float32)
        row = jnp.floor((offset + 0.5) / columns)
        col = offset - row * columns
        angle = jnp.where(by_row, row, col) * freq_ref[...]
        cos_ref[p] = jnp.cos(angle)
        sine = jnp.sin(angle)
        sin_ref[p] = jnp.where(low, -sine, sine)

    @pl.when(jnp.logical_not(home))
    def _():
        slot = slot_of(a)
        remote(spot(slot, 0), spot(slot, 0), pass_send.at[0], w_recv.at[slot, 0], mate, other).wait_recv()
        spread(a, 0, True, True)

    tables(0)
    hop(1, 0)
    tables(1)

    blank = jnp.zeros((HALO, 2 * width), jnp.bfloat16)

    @pl.when(jnp.logical_not(has_down))
    def _():
        for win in wins:
            win[:HALO] = blank

    @pl.when(jnp.logical_not(has_up))
    def _():
        for win in wins:
            win[HALO + size:] = blank

    begin_ring(1)
    hop(2, 0)
    along_x(1).wait_recv()
    relay_y().start()
    hop(1, 1)
    along_y(0).wait_recv()
    relay_x().start()
    for d in range(3, planes):
        hop(d, 0)
        hop(d - 1, 1)
    from_mate(0)

    @pl.when(home)
    def _():
        keep_own(0).wait()
        keep_own(1).wait()

    wkv = lambda: wkv_ref[...].reshape(-1, wide)
    wq = lambda: wq_ref[...].reshape(-1, wq_ref.shape[2])

    def make_keys(p, mine, first, length):
        pos = b if mine else 1 - b
        at = pl.ds(pl.multiple_of(pos * rows + first, 16), length)
        raw = jnp.dot(shard_rows(p, mine, first, length), wkv(), preferred_element_type=jnp.float32)
        cosine, sine = cos_ref[p, at], sin_ref[p, at]
        keys = [turn(raw[:, h * HEAD:(h + 1) * HEAD], kg_ref[...], cosine, sine) for h in range(heads)]
        done = jnp.concatenate(keys + [raw[:, width:2 * width].astype(jnp.bfloat16)], axis=1)
        wins[p][pl.ds(pl.multiple_of(HALO + pos * rows + first, 16), length)] = done
        lead_ref[p, at] = raw[:, 2 * width:]

    def make_queries(p, mine, first, length):
        pos = b if mine else 1 - b
        at = pl.ds(pl.multiple_of(pos * rows + first, 16), length)
        raw = jnp.dot(shard_rows(p, mine, first, length), wq(), preferred_element_type=jnp.float32)
        raw = jnp.concatenate([lead_ref[p, at], raw[:, :width - extra]], axis=1)
        cosine, sine = cos_ref[p, at], sin_ref[p, at]
        q_ref[p, at] = jnp.concatenate(
            [turn(raw[:, h * HEAD:(h + 1) * HEAD], qg_ref[...], cosine, sine) for h in range(heads)], axis=1)

    def upward(p, k):
        return remote(wins[p].at[pl.ds(size + k * BLOCK, BLOCK)], wins[p].at[pl.ds(k * BLOCK, BLOCK)],
                      halo_send.at[p, 0, k], halo_recv.at[p, 0, k], f, s + 2)

    def downward(p, k):
        return remote(wins[p].at[pl.ds(HALO + k * BLOCK, BLOCK)], wins[p].at[pl.ds(HALO + size + k * BLOCK, BLOCK)],
                      halo_send.at[p, 1, k], halo_recv.at[p, 1, k], f, s - 2)

    per = rows // BLOCK
    reach = HALO // BLOCK
    total = size // BLOCK

    def send_block(p, i):
        if i >= total - reach:
            @pl.when(has_up)
            def _():
                upward(p, i - (total - reach)).start()
        if i < reach:
            @pl.when(has_down)
            def _():
                downward(p, i).start()

    def send_shard(p, pos):
        for q in range(2):
            @pl.when(pos == q)
            def _():
                for k in range(per):
                    send_block(p, q * per + k)

    make_keys(0, True, 0, rows)
    send_shard(0, b)
    hop(planes - 1, 1)
    along_y(1).wait_recv()
    make_keys(0, False, 0, rows)
    send_shard(0, 1 - b)
    along_x(0).wait_recv()
    make_keys(1, True, 0, rows)
    send_shard(1, b)
    from_mate(1)
    make_queries(0, True, 0, rows)
    make_queries(0, False, 0, rows)
    make_queries(1, True, 0, rows)

    scale = HEAD ** (-0.5) * 1.4426950408889634

    def attend_block(p, i):
        first = pl.multiple_of(i * BLOCK, BLOCK)
        where_q = a * size + i * BLOCK

        def image(j, state):
            start, begin, length = state
            inside = where_q >= start
            blocks = blocks_ref[packs[p], j] * BLOCK
            return start + blocks, jnp.where(inside, start, begin), jnp.where(inside, blocks, length)

        _, begin, length = lax.fori_loop(0, blocks_ref.shape[1], image, (jnp.int32(0), jnp.int32(0), jnp.int32(0)))
        back = where_q - begin
        chosen = wins[p][pl.ds(pl.multiple_of(first + HALO, BLOCK), span)]
        for shift in range(BLOCK, HALO + 1, BLOCK):
            earlier = wins[p][pl.ds(pl.multiple_of(first + HALO - shift, BLOCK), span)]
            chosen = jnp.where(back == shift, earlier, chosen)
        mask = lax.broadcasted_iota(jnp.int32, (span, BLOCK), 0) < length
        queries = q_ref[p, pl.ds(first, BLOCK)]
        outs = []
        for h in range(heads):
            keys = chosen[:, h * HEAD:(h + 1) * HEAD]
            vals = chosen[:, width + h * HEAD:width + (h + 1) * HEAD]
            scores = lax.dot_general(keys, queries[:, h * HEAD:(h + 1) * HEAD], (((1,), (1,)), ((), ())),
                                     preferred_element_type=jnp.float32)
            scores = jnp.where(mask, scores, -1e30)
            top = jnp.max(scores, axis=0, keepdims=True)
            expo = jnp.exp2((scores - top) * scale)
            norm = jnp.sum(expo, axis=0, keepdims=True)
            probs = (expo * (1.0 / norm)).astype(jnp.bfloat16)
            outs.append(lax.dot_general(probs, vals, (((0,), (0,)), ((), ())),
                                        preferred_element_type=jnp.float32).astype(jnp.bfloat16))
        mixed[p, pl.ds(first, BLOCK)] = jnp.concatenate(outs, axis=1)

    group = 2 * x + b

    def result(p, pos):
        return mixed.at[p, pl.ds(pl.multiple_of(pos * rows, 16), rows)]

    def deliver(p, k):
        pos, seat = (1 - b, other) if k == 0 else (b, s)
        owner = f if p == 0 else beside
        return remote(result(p, pos), landed.at[group], out_send.at[p, k], out_recv.at[group], owner, seat)

    keep = pltpu.make_async_copy(result(0, b), landed.at[group], local_sem.at[0])

    def attend(p, k):
        pos = 1 - b if k == 0 else b
        for i in range(per):
            attend_block(p, pos * per + i)
        if p == 0 and k == 1:
            keep.start()
        else:
            deliver(p, k).start()

    def halo_wait(p):
        @pl.when(has_down)
        def _():
            for k in range(reach):
                upward(p, k).wait_recv()

        @pl.when(has_up)
        def _():
            for k in range(reach):
                downward(p, k).wait_recv()

    relay_x().wait_recv()
    relay_y().wait_recv()
    make_keys(1, False, 0, rows)
    send_shard(1, 1 - b)
    halo_wait(0)
    attend(0, 0)
    attend(0, 1)
    make_queries(1, False, 0, rows)
    halo_wait(1)
    attend(1, 0)
    attend(1, 1)

    def drain(plane, carry):
        for kind in range(2):
            @pl.when((plane <= a) & has_up)
            def _():
                push(plane, kind, 0).wait_send()

            @pl.when((plane >= a) & has_down)
            def _():
                push(plane, kind, 1).wait_send()

            push(plane, kind, 2).wait_send()
        return carry

    lax.fori_loop(0, planes, drain, 0)

    @pl.when(jnp.logical_not(home))
    def _():
        pass_over(0).wait_send()
        pass_over(1).wait_send()

    for k in range(2):
        along_x(k).wait_send()
        along_y(k).wait_send()
    relay_x().wait_send()
    relay_y().wait_send()
    for p in range(2):
        for k in range(reach):
            @pl.when(has_up)
            def _():
                upward(p, k).wait_send()

            @pl.when(has_down)
            def _():
                downward(p, k).wait_send()

    keep.wait()
    deliver(0, 0).wait_send()
    deliver(1, 0).wait_send()
    deliver(1, 1).wait_send()
    for g in range(4):
        @pl.when(group != g)
        def _():
            remote(result(0, b), landed.at[g], out_send.at[0, 0], out_recv.at[g], mate, s).wait_recv()

    o_ref[0] = jnp.concatenate([landed[g] for g in range(4)], axis=1)


def fused(planes, tokens, norm_gain, w_qkv, q_gain, k_gain, img_blocks, img_width):
    row_count, model = tokens.shape[1], tokens.shape[2]
    depth, width = w_qkv.shape[1], w_qkv.shape[2]
    size = 2 * row_count
    wide = pl.cdiv(2 * width, 128) * 128
    tail = pl.cdiv(3 * width - wide, 128) * 128
    quarter = HEAD // 4
    freq = np.tile(np.float32(10000.0) ** (-np.arange(quarter, dtype=np.float32) / np.float32(quarter)), 4)[None]
    vmem = pl.BlockSpec(memory_space=pltpu.VMEM)
    smem = pl.BlockSpec(memory_space=pltpu.SMEM)
    dma = pltpu.SemaphoreType.DMA
    return pl.pallas_call(
        functools.partial(fused_kernel, planes),
        out_shape=jax.ShapeDtypeStruct((1, row_count, 4 * width), jnp.bfloat16),
        in_specs=[vmem] * 6 + [smem] * 2,
        out_specs=vmem,
        scratch_shapes=[
            pltpu.VMEM((row_count, model), jnp.bfloat16),
            pltpu.VMEM((row_count, model), jnp.bfloat16),
            pltpu.VMEM((row_count, model), jnp.bfloat16),
            pltpu.VMEM((row_count, model), jnp.bfloat16),
            pltpu.VMEM((2 * planes, depth, wide), jnp.bfloat16),
            pltpu.VMEM((2 * planes, depth, tail), jnp.bfloat16),
            pltpu.VMEM((depth, wide), jnp.bfloat16),
            pltpu.VMEM((depth, tail), jnp.bfloat16),
            pltpu.VMEM((2, size, HEAD), jnp.float32),
            pltpu.VMEM((2, size, HEAD), jnp.float32),
            pltpu.VMEM((2, size, width), jnp.bfloat16),
            pltpu.VMEM((2, size, wide - 2 * width), jnp.float32),
            pltpu.VMEM((size + 2 * HALO, 2 * width), jnp.bfloat16),
            pltpu.VMEM((size + 2 * HALO, 2 * width), jnp.bfloat16),
            pltpu.VMEM((2, size, width), jnp.bfloat16),
            pltpu.VMEM((4, row_count, width), jnp.bfloat16),
            dma((3, 2)),
            dma((3, 2)),
            dma((planes, 2, 3)),
            dma((2 * planes, 2)),
            dma((2,)),
            dma((2, 2, HALO // BLOCK)),
            dma((2, 2, HALO // BLOCK)),
            dma((2, 2)),
            dma((4,)),
            dma((3,)),
        ],
        compiler_params=pltpu.CompilerParams(
            collective_id=0, has_side_effects=True, vmem_limit_bytes=48 * 1024 * 1024),
        name="fused",
    )(tokens, norm_gain, w_qkv, q_gain[None], k_gain[None], jnp.asarray(freq), img_blocks, img_width)


def shards(planes, tokens, norm_gain, w_qkv, q_gain, k_gain, img_blocks, img_width):
    row_count, model = tokens.shape[1], tokens.shape[2]
    width = w_qkv.shape[2]
    size = 2 * row_count
    seqs = 2 * planes
    depth = w_qkv.shape[1]
    broad = pl.cdiv(3 * width, 128) * 128
    quarter = HEAD // 4
    freq = np.tile(np.float32(10000.0) ** (-np.arange(quarter, dtype=np.float32) / np.float32(quarter)), 4)[None]
    vmem = pl.BlockSpec(memory_space=pltpu.VMEM)
    smem = pl.BlockSpec(memory_space=pltpu.SMEM)
    anywhere = pl.BlockSpec(memory_space=pl.ANY)
    table = jax.ShapeDtypeStruct((2, size, HEAD), jnp.float32)
    gathered, weights, cosine, sine = pl.pallas_call(
        functools.partial(gather_kernel, planes),
        out_shape=(
            jax.ShapeDtypeStruct((2, 2, row_count, model), jnp.bfloat16),
            jax.ShapeDtypeStruct((seqs, depth, broad), jnp.bfloat16),
            table,
            table,
        ),
        in_specs=[vmem, vmem, vmem, smem, smem, vmem],
        out_specs=(anywhere, anywhere, vmem, vmem),
        scratch_shapes=[
            pltpu.VMEM((row_count, model), jnp.bfloat16),
            pltpu.VMEM((depth, broad), jnp.bfloat16),
            pltpu.SemaphoreType.DMA((7,)),
            pltpu.SemaphoreType.DMA((7,)),
            pltpu.SemaphoreType.DMA((seqs, 3)),
            pltpu.SemaphoreType.DMA((seqs,)),
            pltpu.SemaphoreType.DMA((2,)),
        ],
        compiler_params=pltpu.CompilerParams(collective_id=0, has_side_effects=True),
        name="gather",
    )(tokens, norm_gain, w_qkv, img_blocks, img_width, jnp.asarray(freq))
    attended = pl.pallas_call(
        functools.partial(attend_kernel, planes),
        out_shape=jax.ShapeDtypeStruct((1, row_count, 4 * width), jnp.bfloat16),
        in_specs=[anywhere, anywhere, vmem, vmem, vmem, vmem, smem],
        out_specs=vmem,
        scratch_shapes=[
            pltpu.VMEM((2, size, model), jnp.bfloat16),
            pltpu.VMEM((model, broad), jnp.bfloat16),
            pltpu.VMEM((2, size, width), jnp.bfloat16),
            pltpu.VMEM((size + 2 * HALO, 2 * width), jnp.bfloat16),
            pltpu.VMEM((size + 2 * HALO, 2 * width), jnp.bfloat16),
            pltpu.VMEM((2, size, width), jnp.bfloat16),
            pltpu.VMEM((4, row_count, width), jnp.bfloat16),
            pltpu.SemaphoreType.DMA((2, 2)),
            pltpu.SemaphoreType.DMA((2, 2)),
            pltpu.SemaphoreType.DMA((2, 2)),
            pltpu.SemaphoreType.DMA((4,)),
            pltpu.SemaphoreType.DMA((3,)),
            pltpu.SemaphoreType.DMA((3,)),
        ],
        compiler_params=pltpu.CompilerParams(collective_id=1, has_side_effects=True),
        name="attend",
    )(gathered.reshape(2, size, model), weights.reshape(model, broad), cosine, sine,
      q_gain[None], k_gain[None], img_blocks)
    return attended


def solution(mesh):
    assert mesh.shape["fsdp"] == 4 and mesh.shape["seq"] % 2 == 0
    planes = mesh.shape["seq"] // 2

    def body(tokens, norm_gain, w_qkv, *rest):
        whole_tiles = w_qkv.shape[1] % 16 == 0 and 2 * w_qkv.shape[2] % 128 != 0
        return (fused if whole_tiles else shards)(planes, tokens, norm_gain, w_qkv, *rest)

    return jax.shard_map(
        body,
        mesh=mesh,
        in_specs=(P("fsdp", "seq", None), P(), P(None, "seq", "fsdp"), P(), P(), P(), P()),
        out_specs=P("fsdp", "seq", None),
        check_vma=False,
    )
```

```python
import functools

import jax
import jax.numpy as jnp
import numpy as np
from jax import lax
from jax.experimental import pallas as pl
from jax.experimental.pallas import tpu as pltpu
from jax.sharding import PartitionSpec as P

HEAD = 96
BLOCK = 128
HALO = 3 * BLOCK
MESH = pl.DeviceIdType.MESH

eps_model = 1e-06


def rms_norm(values, gain):
    return values * lax.rsqrt(jnp.mean(values * values, axis=-1, keepdims=True) + eps_model) * gain


def place():
    f = lax.axis_index("fsdp")
    s = lax.axis_index("seq")
    return f // 2, f % 2, s // 2, s % 2, f, s


def remote(src, dst, send, recv, f, s):
    return pltpu.make_async_remote_copy(
        src_ref=src, dst_ref=dst, send_sem=send, recv_sem=recv,
        device_id={"fsdp": f, "seq": s}, device_id_type=MESH,
    )


def signal(sem, f, s):
    pl.semaphore_signal(sem, inc=1, device_id={"fsdp": f, "seq": s}, device_id_type=MESH)


def gather_kernel(planes, raw_ref, gain_ref, parts_ref, blocks_ref, widths_ref, freq_ref,
                  t_ref, wall_ref, cos_ref, sin_ref,
                  tok_ref, w_ref, tok_send, tok_recv, w_send, w_recv, local_sem):
    x, c, a, b, f, s = place()
    rows = tok_ref.shape[0]
    half = rows // 2
    other = s + 1 - 2 * b
    home = c == b
    barrier = pltpu.get_barrier_semaphore()
    signal(barrier, 2 * x + 1 - c, s)
    for core in range(2):
        signal(barrier, 2 * (1 - x) + core, s)
        signal(barrier, 2 * x + core, other)

    @pl.when(a > 0)
    def _():
        signal(barrier, f, s - 2)

    @pl.when(a < planes - 1)
    def _():
        signal(barrier, f, s + 2)

    step = 32

    @pl.loop(0, rows // step)
    def _(i):
        at = pl.ds(pl.multiple_of(i * step, step), step)
        tok_ref[at] = rms_norm(raw_ref[0, at].astype(jnp.float32), gain_ref[...][None]).astype(jnp.bfloat16)

    spare = jnp.zeros((w_ref.shape[0], w_ref.shape[1] - 3 * parts_ref.shape[2]), jnp.bfloat16)
    w_ref[...] = jnp.concatenate([parts_ref[1], parts_ref[2], parts_ref[0], spare], axis=1)
    pl.semaphore_wait(barrier, 5 + (a > 0).astype(jnp.int32) + (a < planes - 1).astype(jnp.int32))

    def part(xx, yy, h):
        return t_ref.at[xx, yy, pl.ds(pl.multiple_of(h * half, half), half)]

    keep = pltpu.make_async_copy(tok_ref, t_ref.at[x, b], local_sem.at[0])
    whole = remote(tok_ref, t_ref.at[x, b], tok_send.at[0], tok_recv.at[6], 2 * x + 1 - c, s)
    along = [remote(tok_ref.at[pl.ds(h * half, half)], part(x, b, h), tok_send.at[1 + h], tok_recv.at[1],
                    2 * (1 - x) + h, s) for h in range(2)]
    across = [remote(tok_ref.at[pl.ds(h * half, half)], part(x, b, h), tok_send.at[1 + h], tok_recv.at[0],
                     2 * x + h, other) for h in range(2)]

    @pl.when(home)
    def _():
        for copy in along:
            copy.start()
        whole.start()
        keep.start()

    @pl.when(jnp.logical_not(home))
    def _():
        for copy in across:
            copy.start()

    keep_w = pltpu.make_async_copy(w_ref, wall_ref.at[s], local_sem.at[1])
    keep_w.start()

    def push(src, slot, way):
        target = (s + 2, s - 2, other)[way]
        return remote(src, wall_ref.at[slot], w_send.at[slot, way], w_recv.at[slot], f, target)

    def spread(src, slot, up, down):
        if up:
            @pl.when(a < planes - 1)
            def _():
                push(src, slot, 0).start()
        if down:
            @pl.when(a > 0)
            def _():
                push(src, slot, 1).start()

        @pl.when(crosses(slot // 2))
        def _():
            push(src, slot, 2).start()

    middle = planes // 2
    bottom, top = 1 - b, 2 * (planes - 1) + 1 - b
    lifts = jnp.logical_not(home) & (a >= middle - 1) & (a < planes - 1)
    drops = jnp.logical_not(home) & (a <= middle) & (a > 0)

    def crosses(k):
        skipped = ((k == 0) & (a >= middle)) | ((k == planes - 1) & (a < middle))
        return jnp.logical_not(home & skipped)

    spread(w_ref, s, True, True)

    size = cos_ref.shape[1]
    lane = lax.broadcasted_iota(jnp.int32, (size, HEAD), 1)
    where = a * size + lax.broadcasted_iota(jnp.int32, (size, HEAD), 0)
    by_row = lane < HEAD // 2
    low = (lane < HEAD // 4) | ((lane >= HEAD // 2) & (lane < 3 * HEAD // 4))
    for px in range(2):
        pack = 2 * px + b

        def image(j, carry):
            start, begin, wide = carry
            inside = where >= start
            begin = jnp.where(inside, start, begin)
            wide = jnp.where(inside, widths_ref[pack, j], wide)
            return start + blocks_ref[pack, j] * BLOCK, begin, wide

        zero = jnp.zeros((size, HEAD), jnp.int32)
        _, begin, wide = lax.fori_loop(0, blocks_ref.shape[1], image, (jnp.int32(0), zero, zero + 1))
        offset = (where - begin).astype(jnp.float32)
        wide = wide.astype(jnp.float32)
        row = jnp.floor((offset + 0.5) / wide)
        col = offset - row * wide
        angle = jnp.where(by_row, row, col) * freq_ref[...]
        cos_ref[px] = jnp.cos(angle)
        sine = jnp.sin(angle)
        sin_ref[px] = jnp.where(low, -sine, sine)

    mine = [(x, 1 - b), (1 - x, b), (1 - x, 1 - b)]

    def share(k):
        spot = part(mine[k][0], mine[k][1], c)
        return remote(spot, spot, tok_send.at[3 + k], tok_recv.at[3 + k], 2 * x + 1 - c, s)

    def landed(k):
        spot = part(mine[k][0], mine[k][1], c)
        return remote(spot, spot, tok_send.at[3 + k], tok_recv.at[k], 2 * x + 1 - c, s)

    spot = part(x, 1 - b, c)
    relay = remote(spot, spot, tok_send.at[6], tok_recv.at[2], 2 * (1 - x) + c, s)
    def hop(d, carry):
        lower = a - d
        upper = a + d

        @pl.when(lower >= 0)
        def _():
            slot = jnp.maximum(2 * lower + b, 0)
            push(wall_ref.at[slot], slot, 0).wait_recv()
            spread(wall_ref.at[slot], slot, True, False)

        @pl.when(upper < planes)
        def _():
            slot = jnp.minimum(2 * upper + b, 2 * planes - 1)
            push(wall_ref.at[slot], slot, 1).wait_recv()
            spread(wall_ref.at[slot], slot, False, True)

        return carry

    lax.fori_loop(1, 2, hop, 0)
    landed(0).wait_recv()
    relay.start()
    share(0).start()
    lax.fori_loop(2, 3, hop, 0)

    @pl.when(lifts)
    def _():
        push(wall_ref.at[bottom], bottom, 0).wait_recv()
        push(wall_ref.at[bottom], bottom, 0).start()

    @pl.when(drops)
    def _():
        push(wall_ref.at[top], top, 1).wait_recv()
        push(wall_ref.at[top], top, 1).start()

    lax.fori_loop(3, planes, hop, 0)
    landed(1).wait_recv()
    share(1).start()
    landed(2).wait_recv()
    share(2).start()

    def finish(k, carry):
        slot = 2 * k + 1 - b
        early = ((k == 0) & lifts) | ((k == planes - 1) & drops)

        @pl.when(jnp.logical_not(early))
        def _():
            push(wall_ref.at[slot], slot, 2).wait_recv()

        sent = 2 * k + b

        @pl.when(crosses(k))
        def _():
            push(wall_ref.at[sent], sent, 2).wait_send()

        @pl.when((k <= a) & (a < planes - 1))
        def _():
            push(wall_ref.at[sent], sent, 0).wait_send()

        @pl.when((k >= a) & (a > 0))
        def _():
            push(wall_ref.at[sent], sent, 1).wait_send()

        return carry

    lax.fori_loop(0, planes, finish, 0)

    @pl.when(lifts)
    def _():
        push(wall_ref.at[bottom], bottom, 0).wait_send()

    @pl.when(drops)
    def _():
        push(wall_ref.at[top], top, 1).wait_send()

    keep_w.wait()

    @pl.when(home)
    def _():
        for copy in along:
            copy.wait_send()
        whole.wait_send()
        keep.wait()

    @pl.when(jnp.logical_not(home))
    def _():
        for copy in across:
            copy.wait_send()
        whole.wait_recv()

    relay.wait_send()
    for k in range(3):
        share(k).wait_send()
        spot = part(mine[k][0], mine[k][1], 1 - c)
        remote(spot, spot, tok_send.at[3 + k], tok_recv.at[3 + k], 2 * x + 1 - c, s).wait_recv()


def turn(raw, gain, cosine, sine):
    parts = HEAD // 4
    n = rms_norm(raw, gain)
    swapped = jnp.concatenate(
        [n[:, parts:2 * parts], n[:, :parts], n[:, 3 * parts:], n[:, 2 * parts:3 * parts]], axis=1)
    return (n * cosine + swapped * sine).astype(jnp.bfloat16)


def attend_kernel(planes, t_ref, wall_ref, cos_ref, sin_ref, qg_ref, kg_ref, blocks_ref, o_ref,
                  x_ref, w_ref, q_ref, low_win, high_win, mixed, landed, halo_send, halo_recv, out_send, out_recv,
                  local_sem, load_sem):
    x, c, a, b, f, s = place()
    size, width = q_ref.shape[1], q_ref.shape[2]
    rows = size // 2
    inner = size - HALO
    span = HALO + BLOCK
    wins = (low_win, high_win)
    home = c == b
    load_w = pltpu.make_async_copy(wall_ref, w_ref, load_sem.at[2])
    loads = [pltpu.make_async_copy(t_ref.at[p], x_ref.at[p], load_sem.at[p]) for p in range(2)]
    load_w.start()
    for load in loads:
        load.start()
    barrier = pltpu.get_barrier_semaphore()
    has_down, has_up = a > 0, a < planes - 1
    for core in range(4):
        @pl.when(jnp.logical_or(b != c, f != core))
        def _():
            signal(barrier, core, 2 * a + c)

    @pl.when(has_down)
    def _():
        signal(barrier, f, s - 2)

    @pl.when(has_up)
    def _():
        signal(barrier, f, s + 2)

    count = 4 - home.astype(jnp.int32) + has_down.astype(jnp.int32) + has_up.astype(jnp.int32)
    pl.semaphore_wait(barrier, count)

    def upward(p):
        return remote(wins[p].at[pl.ds(HALO + inner, HALO)], wins[p].at[pl.ds(0, HALO)],
                      halo_send.at[p, 0], halo_recv.at[p, 0], f, s + 2)

    def downward(p):
        return remote(wins[p].at[pl.ds(HALO, HALO)], wins[p].at[pl.ds(HALO + size, HALO)],
                      halo_send.at[p, 1], halo_recv.at[p, 1], f, s - 2)

    blank = jnp.zeros((HALO, 2 * width), jnp.bfloat16)

    @pl.when(jnp.logical_not(has_down))
    def _():
        for win in wins:
            win[:HALO] = blank

    @pl.when(jnp.logical_not(has_up))
    def _():
        for win in wins:
            win[HALO + size:] = blank

    heads = width // HEAD
    shift_q = 2 * width // 128 * 128

    def make_keys(p, i):
        first = i * rows
        at = slice(first, first + rows)
        raw = jnp.dot(x_ref[p, at], w_ref[:, :pl.cdiv(2 * width, 128) * 128], preferred_element_type=jnp.float32)
        keys = [turn(raw[:, h * HEAD:(h + 1) * HEAD], kg_ref[...], cos_ref[p, at], sin_ref[p, at])
                for h in range(heads)]
        done = jnp.concatenate(keys + [raw[:, width:2 * width].astype(jnp.bfloat16)], axis=1)
        wins[p][HALO + first:HALO + first + rows] = done

    def make_queries(p, i):
        at = slice(i * rows, (i + 1) * rows)
        raw = jnp.dot(x_ref[p, at], w_ref[:, shift_q:], preferred_element_type=jnp.float32)
        raw = raw[:, 2 * width - shift_q:]
        q_ref[p, at] = jnp.concatenate(
            [turn(raw[:, h * HEAD:(h + 1) * HEAD], qg_ref[...], cos_ref[p, at], sin_ref[p, at])
             for h in range(heads)], axis=1)

    load_w.wait()
    for load in loads:
        load.wait()
    for p in range(2):
        for i in range(2):
            make_keys(p, i)

        make_queries(p, 0)

        @pl.when(has_up)
        def _():
            upward(p).start()

        @pl.when(has_down)
        def _():
            downward(p).start()

    for p in range(2):
        make_queries(p, 1)

    scale = HEAD ** (-0.5) * 1.4426950408889634

    def deliver(p, yy):
        return remote(mixed.at[p, pl.ds(yy * rows, rows)], landed.at[f],
                      out_send.at[p, yy], out_recv.at[f], 2 * p + b, 2 * a + yy)

    def to_self(p, yy):
        return pltpu.make_async_copy(mixed.at[p, pl.ds(yy * rows, rows)], landed.at[f], local_sem.at[2])

    def is_self(p, yy):
        return home & (p == x) & (yy == b)

    for p in range(2):
        pack = 2 * p + b

        @pl.when(has_down)
        def _():
            upward(p).wait_recv()

        @pl.when(has_up)
        def _():
            downward(p).wait_recv()

        def block(i, carry):
            first = pl.multiple_of(i * BLOCK, BLOCK)
            where_q = a * size + i * BLOCK

            def image(j, state):
                start, begin, length = state
                inside = where_q >= start
                blocks = blocks_ref[pack, j] * BLOCK
                return start + blocks, jnp.where(inside, start, begin), jnp.where(inside, blocks, length)

            _, begin, length = lax.fori_loop(0, blocks_ref.shape[1], image,
                                             (jnp.int32(0), jnp.int32(0), jnp.int32(0)))
            back = where_q - begin
            chosen = wins[p][pl.ds(pl.multiple_of(first + HALO, BLOCK), span)]
            for shift in range(BLOCK, HALO + 1, BLOCK):
                earlier = wins[p][pl.ds(pl.multiple_of(first + HALO - shift, BLOCK), span)]
                chosen = jnp.where(back == shift, earlier, chosen)
            mask = lax.broadcasted_iota(jnp.int32, (BLOCK, span), 1) < length
            queries = q_ref[p, pl.ds(first, BLOCK)]
            outs = []
            for h in range(width // HEAD):
                keys = chosen[:, h * HEAD:(h + 1) * HEAD]
                vals = chosen[:, width + h * HEAD:width + (h + 1) * HEAD]
                scores = lax.dot_general(queries[:, h * HEAD:(h + 1) * HEAD], keys, (((1,), (1,)), ((), ())),
                                         preferred_element_type=jnp.float32)
                scores = jnp.where(mask, scores, -1e30)
                top = jnp.max(scores, axis=-1, keepdims=True)
                expo = jnp.exp2((scores - top) * scale)
                norm = jnp.sum(expo, axis=-1, keepdims=True)
                probs = (expo * (1.0 / norm)).astype(jnp.bfloat16)
                outs.append(jnp.dot(probs, vals, preferred_element_type=jnp.float32).astype(jnp.bfloat16))
            mixed[p, pl.ds(first, BLOCK)] = jnp.concatenate(outs, axis=1)
            return carry

        lax.fori_loop(0, size // BLOCK, block, 0)
        for yy in range(2):
            @pl.when(is_self(p, yy))
            def _():
                to_self(p, yy).start()

            @pl.when(jnp.logical_not(is_self(p, yy)))
            def _():
                deliver(p, yy).start()

    for p in range(2):
        for yy in range(2):
            @pl.when(is_self(p, yy))
            def _():
                to_self(p, yy).wait()

            @pl.when(jnp.logical_not(is_self(p, yy)))
            def _():
                deliver(p, yy).wait_send()

        @pl.when(has_up)
        def _():
            upward(p).wait_send()

        @pl.when(has_down)
        def _():
            downward(p).wait_send()

    for core in range(4):
        @pl.when(jnp.logical_or(b != c, f != core))
        def _():
            remote(mixed.at[0, pl.ds(0, rows)], landed.at[core], out_send.at[0, 0], out_recv.at[core], f, s).wait_recv()

    o_ref[0] = jnp.concatenate([landed[core] for core in range(4)], axis=1)


def fused_kernel(planes, raw_in, gain_in, parts_in, qg_in, kg_in, freq_in, blocks_ref, widths_ref, o_ref,
                 raw_ref, gain_ref, parts_ref, qg_ref, kg_ref, freq_ref, load_sem, own_ref, xa_ref, xb_ref, xd_ref, wkv_ref, wq_ref, okv_ref, oq_ref, cos_ref, sin_ref, q_ref, lead_ref, win_a, win_b, mixed,
                 landed, tok_send, tok_recv, w_send, w_recv, pass_send, halo_send, halo_recv, out_send, out_recv,
                 local_sem):
    x, c, a, b, f, s = place()
    loads = [pltpu.make_async_copy(src, dst, load_sem.at[i]) for i, (src, dst) in enumerate((
        (parts_in, parts_ref), (raw_in, raw_ref), (gain_in, gain_ref), (qg_in, qg_ref), (kg_in, kg_ref),
        (freq_in, freq_ref)))]
    for load in loads:
        load.start()
    rows = raw_ref.shape[1]
    depth, width = parts_ref.shape[1], parts_ref.shape[2]
    size = 2 * rows
    heads = width // HEAD
    wide = wkv_ref.shape[2]
    extra = wide - 2 * width
    wins = (win_a, win_b)
    span = HALO + BLOCK
    home = c == b
    has_down, has_up = a > 0, a < planes - 1
    mate = 2 * x + 1 - c
    beside = 2 * (1 - x) + c
    other = s + 1 - 2 * b
    packs = (2 * x + c, 2 * (1 - x) + c)
    cut = rows * 5 // 8 // 32 * 32

    barrier = pltpu.get_barrier_semaphore()
    signal(barrier, mate, s)
    signal(barrier, beside, s)
    signal(barrier, f, other)
    signal(barrier, beside, other)

    @pl.when(jnp.logical_not(home))
    def _():
        signal(barrier, mate, other)

    @pl.when(has_down)
    def _():
        signal(barrier, f, s - 2)

    @pl.when(has_up)
    def _():
        signal(barrier, f, s + 2)

    loads[0].wait()
    okv_ref[...] = jnp.concatenate([parts_ref[1], parts_ref[2], parts_ref[0, :, :extra]], axis=1)
    oq_ref[...] = jnp.concatenate(
        [parts_ref[0, :, extra:], jnp.zeros((depth, oq_ref.shape[1] - width + extra), jnp.bfloat16)], axis=1)
    count = 4 + jnp.logical_not(home).astype(jnp.int32) + has_down.astype(jnp.int32) + has_up.astype(jnp.int32)
    pl.semaphore_wait(barrier, count)


    def slot_of(plane):
        return 2 * plane + c

    def spot(slot, kind):
        return (wkv_ref, wq_ref)[kind].at[slot]

    def push(plane, kind, way, src=None):
        slot = slot_of(plane)
        target = ((f, s + 2), (f, s - 2), (mate, s))[way]
        return remote(spot(slot, kind) if src is None else src, spot(slot, kind), w_send.at[plane, kind, way], w_recv.at[slot, kind], *target)

    def pass_over(kind):
        return remote((okv_ref, oq_ref)[kind], spot(s, kind), pass_send.at[kind], w_recv.at[s, kind], mate, other)

    def spread(plane, kind, up, down, src=None):
        if up:
            @pl.when(has_up)
            def _():
                push(plane, kind, 0, src).start()
        if down:
            @pl.when(has_down)
            def _():
                push(plane, kind, 1, src).start()
        push(plane, kind, 2, src).start()

    def keep_own(kind):
        return pltpu.make_async_copy((okv_ref, oq_ref)[kind], spot(s, kind), local_sem.at[1 + kind])

    def begin_ring(kind):
        @pl.when(home)
        def _():
            spread(a, kind, True, True, (okv_ref, oq_ref)[kind])
            keep_own(kind).start()

        @pl.when(jnp.logical_not(home))
        def _():
            slot = slot_of(a)
            remote(spot(slot, kind), spot(slot, kind), pass_send.at[kind], w_recv.at[slot, kind], mate, other).wait_recv()
            spread(a, kind, True, True)

    def hop(d, kind):
        @pl.when(a >= d)
        def _():
            plane = jnp.maximum(a - d, 0)
            push(plane, kind, 0).wait_recv()
            spread(plane, kind, True, False)

        @pl.when(a + d < planes)
        def _():
            plane = jnp.minimum(a + d, planes - 1)
            push(plane, kind, 1).wait_recv()
            spread(plane, kind, False, True)

    def from_mate(kind):
        for plane in range(planes):
            slot = 2 * plane + 1 - c
            remote(spot(slot, kind), spot(slot, kind), w_send.at[plane, kind, 2], w_recv.at[slot, kind], mate, s).wait_recv()

    @pl.when(jnp.logical_not(home))
    def _():
        pass_over(0).start()
        pass_over(1).start()

    @pl.when(home)
    def _():
        spread(a, 0, True, True, okv_ref)
        keep_own(0).start()

    def piece(ref, k):
        first, length = ((0, cut), (cut, rows - cut))[k]
        return ref.at[pl.ds(first, length)]

    def along_x(k):
        return remote(piece(own_ref, k), piece(xb_ref, k), tok_send.at[0, k], tok_recv.at[0, k], beside, s)

    def along_y(k):
        return remote(piece(own_ref, k), piece(xa_ref, k), tok_send.at[1, k], tok_recv.at[1, k], f, other)

    def relay_x():
        return remote(piece(xa_ref, 0), piece(xd_ref, 0), tok_send.at[2, 0], tok_recv.at[2, 0], beside, s)

    def relay_y():
        return remote(piece(xb_ref, 1), piece(xd_ref, 1), tok_send.at[2, 1], tok_recv.at[2, 1], f, other)

    def shard_rows(p, mine, first, length):
        ref = ((xd_ref, xb_ref), (xa_ref, own_ref))[p == 0][mine]
        return ref[first:first + length]

    step = 32

    def normalize(i, carry):
        at = pl.ds(pl.multiple_of(i * step, step), step)
        own_ref[at] = rms_norm(raw_ref[0, at].astype(jnp.float32), gain_ref[...][None]).astype(jnp.bfloat16)
        return carry

    for load in loads[1:]:
        load.wait()
    lax.fori_loop(cut // step, rows // step, normalize, 0)
    along_x(1).start()
    lax.fori_loop(0, cut // step, normalize, 0)
    along_y(0).start()
    along_x(0).start()
    along_y(1).start()

    lane = lax.broadcasted_iota(jnp.int32, (size, HEAD), 1)
    where = a * size + lax.broadcasted_iota(jnp.int32, (size, HEAD), 0)
    by_row = lane < HEAD // 2
    low = (lane < HEAD // 4) | ((lane >= HEAD // 2) & (lane < 3 * HEAD // 4))

    def tables(p):
        def image(j, carry):
            start, begin, columns = carry
            inside = where >= start
            begin = jnp.where(inside, start, begin)
            columns = jnp.where(inside, widths_ref[packs[p], j], columns)
            return start + blocks_ref[packs[p], j] * BLOCK, begin, columns

        zero = jnp.zeros((size, HEAD), jnp.int32)
        _, begin, columns = lax.fori_loop(0, blocks_ref.shape[1], image, (jnp.int32(0), zero, zero + 1))
        offset = (where - begin).astype(jnp.float32)
        columns = columns.astype(jnp.float32)
        row = jnp.floor((offset + 0.5) / columns)
        col = offset - row * columns
        angle = jnp.where(by_row, row, col) * freq_ref[...]
        cos_ref[p] = jnp.cos(angle)
        sine = jnp.sin(angle)
        sin_ref[p] = jnp.where(low, -sine, sine)

    @pl.when(jnp.logical_not(home))
    def _():
        slot = slot_of(a)
        remote(spot(slot, 0), spot(slot, 0), pass_send.at[0], w_recv.at[slot, 0], mate, other).wait_recv()
        spread(a, 0, True, True)

    tables(0)
    hop(1, 0)
    tables(1)

    blank = jnp.zeros((HALO, 2 * width), jnp.bfloat16)

    @pl.when(jnp.logical_not(has_down))
    def _():
        for win in wins:
            win[:HALO] = blank

    @pl.when(jnp.logical_not(has_up))
    def _():
        for win in wins:
            win[HALO + size:] = blank

    begin_ring(1)
    hop(2, 0)
    along_x(1).wait_recv()
    relay_y().start()
    hop(1, 1)
    along_y(0).wait_recv()
    relay_x().start()
    for d in range(3, planes):
        hop(d, 0)
        hop(d - 1, 1)
    from_mate(0)

    @pl.when(home)
    def _():
        keep_own(0).wait()
        keep_own(1).wait()

    wkv = lambda: wkv_ref[...].reshape(-1, wide)
    wq = lambda: wq_ref[...].reshape(-1, wq_ref.shape[2])

    def make_keys(p, mine, first, length):
        pos = b if mine else 1 - b
        at = pl.ds(pl.multiple_of(pos * rows + first, 16), length)
        raw = jnp.dot(shard_rows(p, mine, first, length), wkv(), preferred_element_type=jnp.float32)
        cosine, sine = cos_ref[p, at], sin_ref[p, at]
        keys = [turn(raw[:, h * HEAD:(h + 1) * HEAD], kg_ref[...], cosine, sine) for h in range(heads)]
        done = jnp.concatenate(keys + [raw[:, width:2 * width].astype(jnp.bfloat16)], axis=1)
        wins[p][pl.ds(pl.multiple_of(HALO + pos * rows + first, 16), length)] = done
        lead_ref[p, at] = raw[:, 2 * width:]

    def make_queries(p, mine, first, length):
        pos = b if mine else 1 - b
        at = pl.ds(pl.multiple_of(pos * rows + first, 16), length)
        raw = jnp.dot(shard_rows(p, mine, first, length), wq(), preferred_element_type=jnp.float32)
        raw = jnp.concatenate([lead_ref[p, at], raw[:, :width - extra]], axis=1)
        cosine, sine = cos_ref[p, at], sin_ref[p, at]
        q_ref[p, at] = jnp.concatenate(
            [turn(raw[:, h * HEAD:(h + 1) * HEAD], qg_ref[...], cosine, sine) for h in range(heads)], axis=1)

    def upward(p, k):
        return remote(wins[p].at[pl.ds(size + k * BLOCK, BLOCK)], wins[p].at[pl.ds(k * BLOCK, BLOCK)],
                      halo_send.at[p, 0, k], halo_recv.at[p, 0, k], f, s + 2)

    def downward(p, k):
        return remote(wins[p].at[pl.ds(HALO + k * BLOCK, BLOCK)], wins[p].at[pl.ds(HALO + size + k * BLOCK, BLOCK)],
                      halo_send.at[p, 1, k], halo_recv.at[p, 1, k], f, s - 2)

    per = rows // BLOCK
    reach = HALO // BLOCK
    total = size // BLOCK

    def send_block(p, i):
        if i >= total - reach:
            @pl.when(has_up)
            def _():
                upward(p, i - (total - reach)).start()
        if i < reach:
            @pl.when(has_down)
            def _():
                downward(p, i).start()

    def send_shard(p, pos):
        for q in range(2):
            @pl.when(pos == q)
            def _():
                for k in range(per):
                    send_block(p, q * per + k)

    make_keys(0, True, 0, rows)
    send_shard(0, b)
    hop(planes - 1, 1)
    along_y(1).wait_recv()
    make_keys(0, False, 0, rows)
    send_shard(0, 1 - b)
    along_x(0).wait_recv()
    make_keys(1, True, 0, rows)
    send_shard(1, b)
    from_mate(1)
    make_queries(0, True, 0, rows)
    make_queries(0, False, 0, rows)
    make_queries(1, True, 0, rows)

    scale = HEAD ** (-0.5) * 1.4426950408889634

    def attend_block(p, pos, k):
        i = pos * per + k
        first = pl.multiple_of(i * BLOCK, BLOCK)
        where_q = a * size + i * BLOCK

        def image(j, state):
            start, begin, length = state
            inside = where_q >= start
            blocks = blocks_ref[packs[p], j] * BLOCK
            return start + blocks, jnp.where(inside, start, begin), jnp.where(inside, blocks, length)

        _, begin, length = lax.fori_loop(0, blocks_ref.shape[1], image, (jnp.int32(0), jnp.int32(0), jnp.int32(0)))
        back = where_q - begin
        chosen = wins[p][pl.ds(pl.multiple_of(first + HALO, BLOCK), span)]
        for shift in range(BLOCK, HALO + 1, BLOCK):
            earlier = wins[p][pl.ds(pl.multiple_of(first + HALO - shift, BLOCK), span)]
            chosen = jnp.where(back == shift, earlier, chosen)
        mask = lax.broadcasted_iota(jnp.int32, (span, BLOCK), 0) < length
        queries = q_ref[p, pl.ds(first, BLOCK)]
        outs = []
        for h in range(heads):
            keys = chosen[:, h * HEAD:(h + 1) * HEAD]
            vals = chosen[:, width + h * HEAD:width + (h + 1) * HEAD]
            scores = lax.dot_general(keys, queries[:, h * HEAD:(h + 1) * HEAD], (((1,), (1,)), ((), ())),
                                     preferred_element_type=jnp.float32)
            scores = jnp.where(mask, scores, -1e30)
            top = jnp.max(scores, axis=0, keepdims=True)
            expo = jnp.exp2((scores - top) * scale)
            norm = jnp.sum(expo, axis=0, keepdims=True)
            probs = (expo * (1.0 / norm)).astype(jnp.bfloat16)
            outs.append(lax.dot_general(vals, probs, (((0,), (0,)), ((), ())),
                                        preferred_element_type=jnp.float32).astype(jnp.bfloat16))
        mixed[p, pos, :, k * BLOCK:(k + 1) * BLOCK] = jnp.concatenate(outs, axis=0)

    group = 2 * x + b

    def result(p, pos):
        return mixed.at[p, pos]

    def deliver(p, k):
        pos, seat = (1 - b, other) if k == 0 else (b, s)
        owner = f if p == 0 else beside
        return remote(result(p, pos), landed.at[group], out_send.at[p, k], out_recv.at[group], owner, seat)

    keep = pltpu.make_async_copy(result(0, b), landed.at[group], local_sem.at[0])

    def attend(p, k):
        pos = 1 - b if k == 0 else b
        for i in range(per):
            attend_block(p, pos, i)
        if p == 0 and k == 1:
            keep.start()
        else:
            deliver(p, k).start()

    def halo_wait(p):
        @pl.when(has_down)
        def _():
            for k in range(reach):
                upward(p, k).wait_recv()

        @pl.when(has_up)
        def _():
            for k in range(reach):
                downward(p, k).wait_recv()

    relay_x().wait_recv()
    relay_y().wait_recv()
    make_keys(1, False, 0, rows)
    send_shard(1, 1 - b)
    halo_wait(0)
    attend(0, 0)
    attend(0, 1)
    make_queries(1, False, 0, rows)
    halo_wait(1)
    attend(1, 0)
    attend(1, 1)

    def drain(plane, carry):
        for kind in range(2):
            @pl.when((plane <= a) & has_up)
            def _():
                push(plane, kind, 0).wait_send()

            @pl.when((plane >= a) & has_down)
            def _():
                push(plane, kind, 1).wait_send()

            push(plane, kind, 2).wait_send()
        return carry

    lax.fori_loop(0, planes, drain, 0)

    @pl.when(jnp.logical_not(home))
    def _():
        pass_over(0).wait_send()
        pass_over(1).wait_send()

    for k in range(2):
        along_x(k).wait_send()
        along_y(k).wait_send()
    relay_x().wait_send()
    relay_y().wait_send()
    for p in range(2):
        for k in range(reach):
            @pl.when(has_up)
            def _():
                upward(p, k).wait_send()

            @pl.when(has_down)
            def _():
                downward(p, k).wait_send()

    keep.wait()
    deliver(0, 0).wait_send()
    deliver(1, 0).wait_send()
    deliver(1, 1).wait_send()
    for g in range(4):
        @pl.when(group != g)
        def _():
            remote(result(0, b), landed.at[g], out_send.at[0, 0], out_recv.at[g], mate, s).wait_recv()

    for g in range(4):
        o_ref[0, g * width:(g + 1) * width] = landed[g]


def fused(planes, tokens, norm_gain, w_qkv, q_gain, k_gain, img_blocks, img_width):
    row_count, model = tokens.shape[1], tokens.shape[2]
    depth, width = w_qkv.shape[1], w_qkv.shape[2]
    size = 2 * row_count
    wide = pl.cdiv(2 * width, 128) * 128
    tail = pl.cdiv(3 * width - wide, 128) * 128
    quarter = HEAD // 4
    freq = np.tile(np.float32(10000.0) ** (-np.arange(quarter, dtype=np.float32) / np.float32(quarter)), 4)[None]
    vmem = pl.BlockSpec(memory_space=pltpu.VMEM)
    smem = pl.BlockSpec(memory_space=pltpu.SMEM)
    anywhere = pl.BlockSpec(memory_space=pl.ANY)
    dma = pltpu.SemaphoreType.DMA
    across = pl.pallas_call(
        functools.partial(fused_kernel, planes),
        out_shape=jax.ShapeDtypeStruct((1, 4 * width, row_count), jnp.bfloat16),
        in_specs=[anywhere] * 6 + [smem] * 2,
        out_specs=vmem,
        scratch_shapes=[
            pltpu.VMEM(tokens.shape, jnp.bfloat16),
            pltpu.VMEM(norm_gain.shape, jnp.float32),
            pltpu.VMEM(w_qkv.shape, jnp.bfloat16),
            pltpu.VMEM((1, HEAD), jnp.float32),
            pltpu.VMEM((1, HEAD), jnp.float32),
            pltpu.VMEM((1, HEAD), jnp.float32),
            dma((6,)),
            pltpu.VMEM((row_count, model), jnp.bfloat16),
            pltpu.VMEM((row_count, model), jnp.bfloat16),
            pltpu.VMEM((row_count, model), jnp.bfloat16),
            pltpu.VMEM((row_count, model), jnp.bfloat16),
            pltpu.VMEM((2 * planes, depth, wide), jnp.bfloat16),
            pltpu.VMEM((2 * planes, depth, tail), jnp.bfloat16),
            pltpu.VMEM((depth, wide), jnp.bfloat16),
            pltpu.VMEM((depth, tail), jnp.bfloat16),
            pltpu.VMEM((2, size, HEAD), jnp.float32),
            pltpu.VMEM((2, size, HEAD), jnp.float32),
            pltpu.VMEM((2, size, width), jnp.bfloat16),
            pltpu.VMEM((2, size, wide - 2 * width), jnp.float32),
            pltpu.VMEM((size + 2 * HALO, 2 * width), jnp.bfloat16),
            pltpu.VMEM((size + 2 * HALO, 2 * width), jnp.bfloat16),
            pltpu.VMEM((2, 2, width, row_count), jnp.bfloat16),
            pltpu.VMEM((4, width, row_count), jnp.bfloat16),
            dma((3, 2)),
            dma((3, 2)),
            dma((planes, 2, 3)),
            dma((2 * planes, 2)),
            dma((2,)),
            dma((2, 2, HALO // BLOCK)),
            dma((2, 2, HALO // BLOCK)),
            dma((2, 2)),
            dma((4,)),
            dma((3,)),
        ],
        compiler_params=pltpu.CompilerParams(
            collective_id=0, has_side_effects=True, vmem_limit_bytes=60 * 1024 * 1024),
        name="fused",
    )(tokens, norm_gain, w_qkv, q_gain[None], k_gain[None], jnp.asarray(freq), img_blocks, img_width)
    return jnp.swapaxes(across, 1, 2)


def shards(planes, tokens, norm_gain, w_qkv, q_gain, k_gain, img_blocks, img_width):
    row_count, model = tokens.shape[1], tokens.shape[2]
    width = w_qkv.shape[2]
    size = 2 * row_count
    seqs = 2 * planes
    depth = w_qkv.shape[1]
    broad = pl.cdiv(3 * width, 128) * 128
    quarter = HEAD // 4
    freq = np.tile(np.float32(10000.0) ** (-np.arange(quarter, dtype=np.float32) / np.float32(quarter)), 4)[None]
    vmem = pl.BlockSpec(memory_space=pltpu.VMEM)
    smem = pl.BlockSpec(memory_space=pltpu.SMEM)
    anywhere = pl.BlockSpec(memory_space=pl.ANY)
    table = jax.ShapeDtypeStruct((2, size, HEAD), jnp.float32)
    gathered, weights, cosine, sine = pl.pallas_call(
        functools.partial(gather_kernel, planes),
        out_shape=(
            jax.ShapeDtypeStruct((2, 2, row_count, model), jnp.bfloat16),
            jax.ShapeDtypeStruct((seqs, depth, broad), jnp.bfloat16),
            table,
            table,
        ),
        in_specs=[vmem, vmem, vmem, smem, smem, vmem],
        out_specs=(anywhere, anywhere, vmem, vmem),
        scratch_shapes=[
            pltpu.VMEM((row_count, model), jnp.bfloat16),
            pltpu.VMEM((depth, broad), jnp.bfloat16),
            pltpu.SemaphoreType.DMA((7,)),
            pltpu.SemaphoreType.DMA((7,)),
            pltpu.SemaphoreType.DMA((seqs, 3)),
            pltpu.SemaphoreType.DMA((seqs,)),
            pltpu.SemaphoreType.DMA((2,)),
        ],
        compiler_params=pltpu.CompilerParams(collective_id=0, has_side_effects=True),
        name="gather",
    )(tokens, norm_gain, w_qkv, img_blocks, img_width, jnp.asarray(freq))
    attended = pl.pallas_call(
        functools.partial(attend_kernel, planes),
        out_shape=jax.ShapeDtypeStruct((1, row_count, 4 * width), jnp.bfloat16),
        in_specs=[anywhere, anywhere, vmem, vmem, vmem, vmem, smem],
        out_specs=vmem,
        scratch_shapes=[
            pltpu.VMEM((2, size, model), jnp.bfloat16),
            pltpu.VMEM((model, broad), jnp.bfloat16),
            pltpu.VMEM((2, size, width), jnp.bfloat16),
            pltpu.VMEM((size + 2 * HALO, 2 * width), jnp.bfloat16),
            pltpu.VMEM((size + 2 * HALO, 2 * width), jnp.bfloat16),
            pltpu.VMEM((2, size, width), jnp.bfloat16),
            pltpu.VMEM((4, row_count, width), jnp.bfloat16),
            pltpu.SemaphoreType.DMA((2, 2)),
            pltpu.SemaphoreType.DMA((2, 2)),
            pltpu.SemaphoreType.DMA((2, 2)),
            pltpu.SemaphoreType.DMA((4,)),
            pltpu.SemaphoreType.DMA((3,)),
            pltpu.SemaphoreType.DMA((3,)),
        ],
        compiler_params=pltpu.CompilerParams(collective_id=1, has_side_effects=True),
        name="attend",
    )(gathered.reshape(2, size, model), weights.reshape(model, broad), cosine, sine,
      q_gain[None], k_gain[None], img_blocks)
    return attended


def solution(mesh):
    assert mesh.shape["fsdp"] == 4 and mesh.shape["seq"] % 2 == 0
    planes = mesh.shape["seq"] // 2

    def body(tokens, norm_gain, w_qkv, *rest):
        whole_tiles = w_qkv.shape[1] % 16 == 0 and 2 * w_qkv.shape[2] % 128 != 0
        return (fused if whole_tiles else shards)(planes, tokens, norm_gain, w_qkv, *rest)

    return jax.shard_map(
        body,
        mesh=mesh,
        in_specs=(P("fsdp", "seq", None), P(), P(None, "seq", "fsdp"), P(), P(), P(), P()),
        out_specs=P("fsdp", "seq", None),
        check_vma=False,
    )
```

```python
import functools

import jax
import jax.numpy as jnp
import numpy as np
from jax import lax
from jax.experimental import pallas as pl
from jax.experimental.pallas import tpu as pltpu
from jax.sharding import PartitionSpec as P

HEAD = 96
BLOCK = 128
HALO = 3 * BLOCK
MESH = pl.DeviceIdType.MESH

eps_model = 1e-06


def rms_norm(values, gain):
    return values * lax.rsqrt(jnp.mean(values * values, axis=-1, keepdims=True) + eps_model) * gain


def place():
    f = lax.axis_index("fsdp")
    s = lax.axis_index("seq")
    return f // 2, f % 2, s // 2, s % 2, f, s


def remote(src, dst, send, recv, f, s):
    return pltpu.make_async_remote_copy(
        src_ref=src, dst_ref=dst, send_sem=send, recv_sem=recv,
        device_id={"fsdp": f, "seq": s}, device_id_type=MESH,
    )


def signal(sem, f, s):
    pl.semaphore_signal(sem, inc=1, device_id={"fsdp": f, "seq": s}, device_id_type=MESH)


def gather_kernel(planes, raw_ref, gain_ref, parts_ref, blocks_ref, widths_ref, freq_ref,
                  t_ref, wall_ref, cos_ref, sin_ref,
                  tok_ref, w_ref, tok_send, tok_recv, w_send, w_recv, local_sem):
    x, c, a, b, f, s = place()
    rows = tok_ref.shape[0]
    half = rows // 2
    other = s + 1 - 2 * b
    home = c == b
    barrier = pltpu.get_barrier_semaphore()
    signal(barrier, 2 * x + 1 - c, s)
    for core in range(2):
        signal(barrier, 2 * (1 - x) + core, s)
        signal(barrier, 2 * x + core, other)

    @pl.when(a > 0)
    def _():
        signal(barrier, f, s - 2)

    @pl.when(a < planes - 1)
    def _():
        signal(barrier, f, s + 2)

    step = 32

    @pl.loop(0, rows // step)
    def _(i):
        at = pl.ds(pl.multiple_of(i * step, step), step)
        tok_ref[at] = rms_norm(raw_ref[0, at].astype(jnp.float32), gain_ref[...][None]).astype(jnp.bfloat16)

    spare = jnp.zeros((w_ref.shape[0], w_ref.shape[1] - 3 * parts_ref.shape[2]), jnp.bfloat16)
    w_ref[...] = jnp.concatenate([parts_ref[1], parts_ref[2], parts_ref[0], spare], axis=1)
    pl.semaphore_wait(barrier, 5 + (a > 0).astype(jnp.int32) + (a < planes - 1).astype(jnp.int32))

    def part(xx, yy, h):
        return t_ref.at[xx, yy, pl.ds(pl.multiple_of(h * half, half), half)]

    keep = pltpu.make_async_copy(tok_ref, t_ref.at[x, b], local_sem.at[0])
    whole = remote(tok_ref, t_ref.at[x, b], tok_send.at[0], tok_recv.at[6], 2 * x + 1 - c, s)
    along = [remote(tok_ref.at[pl.ds(h * half, half)], part(x, b, h), tok_send.at[1 + h], tok_recv.at[1],
                    2 * (1 - x) + h, s) for h in range(2)]
    across = [remote(tok_ref.at[pl.ds(h * half, half)], part(x, b, h), tok_send.at[1 + h], tok_recv.at[0],
                     2 * x + h, other) for h in range(2)]

    @pl.when(home)
    def _():
        for copy in along:
            copy.start()
        whole.start()
        keep.start()

    @pl.when(jnp.logical_not(home))
    def _():
        for copy in across:
            copy.start()

    keep_w = pltpu.make_async_copy(w_ref, wall_ref.at[s], local_sem.at[1])
    keep_w.start()

    def push(src, slot, way):
        target = (s + 2, s - 2, other)[way]
        return remote(src, wall_ref.at[slot], w_send.at[slot, way], w_recv.at[slot], f, target)

    def spread(src, slot, up, down):
        if up:
            @pl.when(a < planes - 1)
            def _():
                push(src, slot, 0).start()
        if down:
            @pl.when(a > 0)
            def _():
                push(src, slot, 1).start()

        @pl.when(crosses(slot // 2))
        def _():
            push(src, slot, 2).start()

    middle = planes // 2
    bottom, top = 1 - b, 2 * (planes - 1) + 1 - b
    lifts = jnp.logical_not(home) & (a >= middle - 1) & (a < planes - 1)
    drops = jnp.logical_not(home) & (a <= middle) & (a > 0)

    def crosses(k):
        skipped = ((k == 0) & (a >= middle)) | ((k == planes - 1) & (a < middle))
        return jnp.logical_not(home & skipped)

    spread(w_ref, s, True, True)

    size = cos_ref.shape[1]
    lane = lax.broadcasted_iota(jnp.int32, (size, HEAD), 1)
    where = a * size + lax.broadcasted_iota(jnp.int32, (size, HEAD), 0)
    by_row = lane < HEAD // 2
    low = (lane < HEAD // 4) | ((lane >= HEAD // 2) & (lane < 3 * HEAD // 4))
    for px in range(2):
        pack = 2 * px + b

        def image(j, carry):
            start, begin, wide = carry
            inside = where >= start
            begin = jnp.where(inside, start, begin)
            wide = jnp.where(inside, widths_ref[pack, j], wide)
            return start + blocks_ref[pack, j] * BLOCK, begin, wide

        zero = jnp.zeros((size, HEAD), jnp.int32)
        _, begin, wide = lax.fori_loop(0, blocks_ref.shape[1], image, (jnp.int32(0), zero, zero + 1))
        offset = (where - begin).astype(jnp.float32)
        wide = wide.astype(jnp.float32)
        row = jnp.floor((offset + 0.5) / wide)
        col = offset - row * wide
        angle = jnp.where(by_row, row, col) * freq_ref[...]
        cos_ref[px] = jnp.cos(angle)
        sine = jnp.sin(angle)
        sin_ref[px] = jnp.where(low, -sine, sine)

    mine = [(x, 1 - b), (1 - x, b), (1 - x, 1 - b)]

    def share(k):
        spot = part(mine[k][0], mine[k][1], c)
        return remote(spot, spot, tok_send.at[3 + k], tok_recv.at[3 + k], 2 * x + 1 - c, s)

    def landed(k):
        spot = part(mine[k][0], mine[k][1], c)
        return remote(spot, spot, tok_send.at[3 + k], tok_recv.at[k], 2 * x + 1 - c, s)

    spot = part(x, 1 - b, c)
    relay = remote(spot, spot, tok_send.at[6], tok_recv.at[2], 2 * (1 - x) + c, s)
    def hop(d, carry):
        lower = a - d
        upper = a + d

        @pl.when(lower >= 0)
        def _():
            slot = jnp.maximum(2 * lower + b, 0)
            push(wall_ref.at[slot], slot, 0).wait_recv()
            spread(wall_ref.at[slot], slot, True, False)

        @pl.when(upper < planes)
        def _():
            slot = jnp.minimum(2 * upper + b, 2 * planes - 1)
            push(wall_ref.at[slot], slot, 1).wait_recv()
            spread(wall_ref.at[slot], slot, False, True)

        return carry

    lax.fori_loop(1, 2, hop, 0)
    landed(0).wait_recv()
    relay.start()
    share(0).start()
    lax.fori_loop(2, 3, hop, 0)

    @pl.when(lifts)
    def _():
        push(wall_ref.at[bottom], bottom, 0).wait_recv()
        push(wall_ref.at[bottom], bottom, 0).start()

    @pl.when(drops)
    def _():
        push(wall_ref.at[top], top, 1).wait_recv()
        push(wall_ref.at[top], top, 1).start()

    lax.fori_loop(3, planes, hop, 0)
    landed(1).wait_recv()
    share(1).start()
    landed(2).wait_recv()
    share(2).start()

    def finish(k, carry):
        slot = 2 * k + 1 - b
        early = ((k == 0) & lifts) | ((k == planes - 1) & drops)

        @pl.when(jnp.logical_not(early))
        def _():
            push(wall_ref.at[slot], slot, 2).wait_recv()

        sent = 2 * k + b

        @pl.when(crosses(k))
        def _():
            push(wall_ref.at[sent], sent, 2).wait_send()

        @pl.when((k <= a) & (a < planes - 1))
        def _():
            push(wall_ref.at[sent], sent, 0).wait_send()

        @pl.when((k >= a) & (a > 0))
        def _():
            push(wall_ref.at[sent], sent, 1).wait_send()

        return carry

    lax.fori_loop(0, planes, finish, 0)

    @pl.when(lifts)
    def _():
        push(wall_ref.at[bottom], bottom, 0).wait_send()

    @pl.when(drops)
    def _():
        push(wall_ref.at[top], top, 1).wait_send()

    keep_w.wait()

    @pl.when(home)
    def _():
        for copy in along:
            copy.wait_send()
        whole.wait_send()
        keep.wait()

    @pl.when(jnp.logical_not(home))
    def _():
        for copy in across:
            copy.wait_send()
        whole.wait_recv()

    relay.wait_send()
    for k in range(3):
        share(k).wait_send()
        spot = part(mine[k][0], mine[k][1], 1 - c)
        remote(spot, spot, tok_send.at[3 + k], tok_recv.at[3 + k], 2 * x + 1 - c, s).wait_recv()


def turn(raw, gain, cosine, sine):
    parts = HEAD // 4
    n = rms_norm(raw, gain)
    swapped = jnp.concatenate(
        [n[:, parts:2 * parts], n[:, :parts], n[:, 3 * parts:], n[:, 2 * parts:3 * parts]], axis=1)
    return (n * cosine + swapped * sine).astype(jnp.bfloat16)


def attend_kernel(planes, t_ref, wall_ref, cos_ref, sin_ref, qg_ref, kg_ref, blocks_ref, o_ref,
                  x_ref, w_ref, q_ref, low_win, high_win, mixed, landed, halo_send, halo_recv, out_send, out_recv,
                  local_sem, load_sem):
    x, c, a, b, f, s = place()
    size, width = q_ref.shape[1], q_ref.shape[2]
    rows = size // 2
    inner = size - HALO
    span = HALO + BLOCK
    wins = (low_win, high_win)
    home = c == b
    load_w = pltpu.make_async_copy(wall_ref, w_ref, load_sem.at[2])
    loads = [pltpu.make_async_copy(t_ref.at[p], x_ref.at[p], load_sem.at[p]) for p in range(2)]
    load_w.start()
    for load in loads:
        load.start()
    barrier = pltpu.get_barrier_semaphore()
    has_down, has_up = a > 0, a < planes - 1
    for core in range(4):
        @pl.when(jnp.logical_or(b != c, f != core))
        def _():
            signal(barrier, core, 2 * a + c)

    @pl.when(has_down)
    def _():
        signal(barrier, f, s - 2)

    @pl.when(has_up)
    def _():
        signal(barrier, f, s + 2)

    count = 4 - home.astype(jnp.int32) + has_down.astype(jnp.int32) + has_up.astype(jnp.int32)
    pl.semaphore_wait(barrier, count)

    def upward(p):
        return remote(wins[p].at[pl.ds(HALO + inner, HALO)], wins[p].at[pl.ds(0, HALO)],
                      halo_send.at[p, 0], halo_recv.at[p, 0], f, s + 2)

    def downward(p):
        return remote(wins[p].at[pl.ds(HALO, HALO)], wins[p].at[pl.ds(HALO + size, HALO)],
                      halo_send.at[p, 1], halo_recv.at[p, 1], f, s - 2)

    blank = jnp.zeros((HALO, 2 * width), jnp.bfloat16)

    @pl.when(jnp.logical_not(has_down))
    def _():
        for win in wins:
            win[:HALO] = blank

    @pl.when(jnp.logical_not(has_up))
    def _():
        for win in wins:
            win[HALO + size:] = blank

    heads = width // HEAD
    shift_q = 2 * width // 128 * 128

    def make_keys(p, i):
        first = i * rows
        at = slice(first, first + rows)
        raw = jnp.dot(x_ref[p, at], w_ref[:, :pl.cdiv(2 * width, 128) * 128], preferred_element_type=jnp.float32)
        keys = [turn(raw[:, h * HEAD:(h + 1) * HEAD], kg_ref[...], cos_ref[p, at], sin_ref[p, at])
                for h in range(heads)]
        done = jnp.concatenate(keys + [raw[:, width:2 * width].astype(jnp.bfloat16)], axis=1)
        wins[p][HALO + first:HALO + first + rows] = done

    def make_queries(p, i):
        at = slice(i * rows, (i + 1) * rows)
        raw = jnp.dot(x_ref[p, at], w_ref[:, shift_q:], preferred_element_type=jnp.float32)
        raw = raw[:, 2 * width - shift_q:]
        q_ref[p, at] = jnp.concatenate(
            [turn(raw[:, h * HEAD:(h + 1) * HEAD], qg_ref[...], cos_ref[p, at], sin_ref[p, at])
             for h in range(heads)], axis=1)

    load_w.wait()
    for load in loads:
        load.wait()
    for p in range(2):
        for i in range(2):
            make_keys(p, i)

        make_queries(p, 0)

        @pl.when(has_up)
        def _():
            upward(p).start()

        @pl.when(has_down)
        def _():
            downward(p).start()

    for p in range(2):
        make_queries(p, 1)

    scale = HEAD ** (-0.5) * 1.4426950408889634

    def deliver(p, yy):
        return remote(mixed.at[p, pl.ds(yy * rows, rows)], landed.at[f],
                      out_send.at[p, yy], out_recv.at[f], 2 * p + b, 2 * a + yy)

    def to_self(p, yy):
        return pltpu.make_async_copy(mixed.at[p, pl.ds(yy * rows, rows)], landed.at[f], local_sem.at[2])

    def is_self(p, yy):
        return home & (p == x) & (yy == b)

    for p in range(2):
        pack = 2 * p + b

        @pl.when(has_down)
        def _():
            upward(p).wait_recv()

        @pl.when(has_up)
        def _():
            downward(p).wait_recv()

        def block(i, carry):
            first = pl.multiple_of(i * BLOCK, BLOCK)
            where_q = a * size + i * BLOCK

            def image(j, state):
                start, begin, length = state
                inside = where_q >= start
                blocks = blocks_ref[pack, j] * BLOCK
                return start + blocks, jnp.where(inside, start, begin), jnp.where(inside, blocks, length)

            _, begin, length = lax.fori_loop(0, blocks_ref.shape[1], image,
                                             (jnp.int32(0), jnp.int32(0), jnp.int32(0)))
            back = where_q - begin
            chosen = wins[p][pl.ds(pl.multiple_of(first + HALO, BLOCK), span)]
            for shift in range(BLOCK, HALO + 1, BLOCK):
                earlier = wins[p][pl.ds(pl.multiple_of(first + HALO - shift, BLOCK), span)]
                chosen = jnp.where(back == shift, earlier, chosen)
            mask = lax.broadcasted_iota(jnp.int32, (BLOCK, span), 1) < length
            queries = q_ref[p, pl.ds(first, BLOCK)]
            outs = []
            for h in range(width // HEAD):
                keys = chosen[:, h * HEAD:(h + 1) * HEAD]
                vals = chosen[:, width + h * HEAD:width + (h + 1) * HEAD]
                scores = lax.dot_general(queries[:, h * HEAD:(h + 1) * HEAD], keys, (((1,), (1,)), ((), ())),
                                         preferred_element_type=jnp.float32)
                scores = jnp.where(mask, scores, -1e30)
                top = jnp.max(scores, axis=-1, keepdims=True)
                expo = jnp.exp2((scores - top) * scale)
                norm = jnp.sum(expo, axis=-1, keepdims=True)
                probs = (expo * (1.0 / norm)).astype(jnp.bfloat16)
                outs.append(jnp.dot(probs, vals, preferred_element_type=jnp.float32).astype(jnp.bfloat16))
            mixed[p, pl.ds(first, BLOCK)] = jnp.concatenate(outs, axis=1)
            return carry

        lax.fori_loop(0, size // BLOCK, block, 0)
        for yy in range(2):
            @pl.when(is_self(p, yy))
            def _():
                to_self(p, yy).start()

            @pl.when(jnp.logical_not(is_self(p, yy)))
            def _():
                deliver(p, yy).start()

    for p in range(2):
        for yy in range(2):
            @pl.when(is_self(p, yy))
            def _():
                to_self(p, yy).wait()

            @pl.when(jnp.logical_not(is_self(p, yy)))
            def _():
                deliver(p, yy).wait_send()

        @pl.when(has_up)
        def _():
            upward(p).wait_send()

        @pl.when(has_down)
        def _():
            downward(p).wait_send()

    for core in range(4):
        @pl.when(jnp.logical_or(b != c, f != core))
        def _():
            remote(mixed.at[0, pl.ds(0, rows)], landed.at[core], out_send.at[0, 0], out_recv.at[core], f, s).wait_recv()

    o_ref[0] = jnp.concatenate([landed[core] for core in range(4)], axis=1)


def fused_kernel(planes, raw_in, gain_in, parts_in, qg_in, kg_in, freq_in, blocks_ref, widths_ref, o_ref,
                 raw_ref, gain_ref, parts_ref, qg_ref, kg_ref, freq_ref, load_sem, own_ref, xa_ref, xb_ref, xd_ref, wkv_ref, wq_ref, okv_ref, oq_ref, cos_ref, sin_ref, q_ref, lead_ref, win_a, win_b, mixed,
                 land_y, land_x, land_d, tok_send, tok_recv, w_send, w_recv, pass_send, halo_send, halo_recv, out_send, out_recv,
                 local_sem):
    x, c, a, b, f, s = place()
    loads = [pltpu.make_async_copy(src, dst, load_sem.at[i]) for i, (src, dst) in enumerate((
        (parts_in, parts_ref), (raw_in, raw_ref), (gain_in, gain_ref), (qg_in, qg_ref), (kg_in, kg_ref),
        (freq_in, freq_ref)))]
    for load in loads:
        load.start()
    rows = raw_ref.shape[1]
    depth, width = parts_ref.shape[1], parts_ref.shape[2]
    size = 2 * rows
    heads = width // HEAD
    wide = wkv_ref.shape[2]
    extra = wide - 2 * width
    wins = (win_a, win_b)
    span = HALO + BLOCK
    home = c == b
    has_down, has_up = a > 0, a < planes - 1
    mate = 2 * x + 1 - c
    beside = 2 * (1 - x) + c
    other = s + 1 - 2 * b
    packs = (2 * x + c, 2 * (1 - x) + c)
    cut = rows * 6 // 8 // 32 * 32

    barrier = pltpu.get_barrier_semaphore()
    signal(barrier, mate, s)
    signal(barrier, beside, s)
    signal(barrier, f, other)
    signal(barrier, beside, other)

    @pl.when(jnp.logical_not(home))
    def _():
        signal(barrier, mate, other)

    @pl.when(has_down)
    def _():
        signal(barrier, f, s - 2)

    @pl.when(has_up)
    def _():
        signal(barrier, f, s + 2)

    loads[0].wait()
    okv_ref[...] = jnp.concatenate([parts_ref[1], parts_ref[2], parts_ref[0, :, :extra]], axis=1)
    oq_ref[...] = jnp.concatenate(
        [parts_ref[0, :, extra:], jnp.zeros((depth, oq_ref.shape[1] - width + extra), jnp.bfloat16)], axis=1)
    for load in loads[1:]:
        load.wait()
    step = 32

    def normalize(i, carry):
        at = pl.ds(pl.multiple_of(i * step, step), step)
        own_ref[at] = rms_norm(raw_ref[0, at].astype(jnp.float32), gain_ref[...][None]).astype(jnp.bfloat16)
        return carry

    lax.fori_loop(cut // step, rows // step, normalize, 0)
    count = 4 + jnp.logical_not(home).astype(jnp.int32) + has_down.astype(jnp.int32) + has_up.astype(jnp.int32)
    pl.semaphore_wait(barrier, count)


    def slot_of(plane):
        return 2 * plane + c

    def spot(slot, kind):
        return (wkv_ref, wq_ref)[kind].at[slot]

    def push(plane, kind, way, src=None):
        slot = slot_of(plane)
        target = ((f, s + 2), (f, s - 2), (mate, s))[way]
        return remote(spot(slot, kind) if src is None else src, spot(slot, kind), w_send.at[plane, kind, way], w_recv.at[slot, kind], *target)

    def pass_over(kind):
        return remote((okv_ref, oq_ref)[kind], spot(s, kind), pass_send.at[kind], w_recv.at[s, kind], mate, other)

    def spread(plane, kind, up, down, src=None):
        if up:
            @pl.when(has_up)
            def _():
                push(plane, kind, 0, src).start()
        if down:
            @pl.when(has_down)
            def _():
                push(plane, kind, 1, src).start()
        push(plane, kind, 2, src).start()

    def keep_own(kind):
        return pltpu.make_async_copy((okv_ref, oq_ref)[kind], spot(s, kind), local_sem.at[1 + kind])

    def begin_ring(kind):
        @pl.when(home)
        def _():
            spread(a, kind, True, True, (okv_ref, oq_ref)[kind])
            keep_own(kind).start()

        @pl.when(jnp.logical_not(home))
        def _():
            slot = slot_of(a)
            remote(spot(slot, kind), spot(slot, kind), pass_send.at[kind], w_recv.at[slot, kind], mate, other).wait_recv()
            spread(a, kind, True, True)

    def hop(d, kind):
        @pl.when(a >= d)
        def _():
            plane = jnp.maximum(a - d, 0)
            push(plane, kind, 0).wait_recv()
            spread(plane, kind, True, False)

        @pl.when(a + d < planes)
        def _():
            plane = jnp.minimum(a + d, planes - 1)
            push(plane, kind, 1).wait_recv()
            spread(plane, kind, False, True)

    def from_mate(kind):
        for plane in range(planes):
            slot = 2 * plane + 1 - c
            remote(spot(slot, kind), spot(slot, kind), w_send.at[plane, kind, 2], w_recv.at[slot, kind], mate, s).wait_recv()

    @pl.when(jnp.logical_not(home))
    def _():
        pass_over(0).start()
        pass_over(1).start()

    @pl.when(home)
    def _():
        spread(a, 0, True, True, okv_ref)
        keep_own(0).start()

    def piece(ref, k):
        first, length = ((0, cut), (cut, rows - cut))[k]
        return ref.at[pl.ds(first, length)]

    def along_x(k):
        return remote(piece(own_ref, k), piece(xb_ref, k), tok_send.at[0, k], tok_recv.at[0, k], beside, s)

    def along_y(k):
        return remote(piece(own_ref, k), piece(xa_ref, k), tok_send.at[1, k], tok_recv.at[1, k], f, other)

    def relay_x():
        return remote(piece(xa_ref, 0), piece(xd_ref, 0), tok_send.at[2, 0], tok_recv.at[2, 0], beside, s)

    def relay_y():
        return remote(piece(xb_ref, 1), piece(xd_ref, 1), tok_send.at[2, 1], tok_recv.at[2, 1], f, other)

    def shard_rows(p, mine, first, length):
        ref = ((xd_ref, xb_ref), (xa_ref, own_ref))[p == 0][mine]
        return ref[first:first + length]

    along_x(1).start()
    lax.fori_loop(0, cut // step, normalize, 0)
    along_y(0).start()
    along_x(0).start()
    along_y(1).start()

    lane = lax.broadcasted_iota(jnp.int32, (size, HEAD), 1)
    where = a * size + lax.broadcasted_iota(jnp.int32, (size, HEAD), 0)
    by_row = lane < HEAD // 2
    low = (lane < HEAD // 4) | ((lane >= HEAD // 2) & (lane < 3 * HEAD // 4))

    def tables(p):
        def image(j, carry):
            start, begin, columns = carry
            inside = where >= start
            begin = jnp.where(inside, start, begin)
            columns = jnp.where(inside, widths_ref[packs[p], j], columns)
            return start + blocks_ref[packs[p], j] * BLOCK, begin, columns

        zero = jnp.zeros((size, HEAD), jnp.int32)
        _, begin, columns = lax.fori_loop(0, blocks_ref.shape[1], image, (jnp.int32(0), zero, zero + 1))
        offset = (where - begin).astype(jnp.float32)
        columns = columns.astype(jnp.float32)
        row = jnp.floor((offset + 0.5) / columns)
        col = offset - row * columns
        angle = jnp.where(by_row, row, col) * freq_ref[...]
        cos_ref[p] = jnp.cos(angle)
        sine = jnp.sin(angle)
        sin_ref[p] = jnp.where(low, -sine, sine)

    tables(0)
    tables(1)

    @pl.when(jnp.logical_not(home))
    def _():
        slot = slot_of(a)
        remote(spot(slot, 0), spot(slot, 0), pass_send.at[0], w_recv.at[slot, 0], mate, other).wait_recv()
        spread(a, 0, True, True)

    hop(1, 0)

    blank = jnp.zeros((HALO, 2 * width), jnp.bfloat16)

    @pl.when(jnp.logical_not(has_down))
    def _():
        for win in wins:
            win[:HALO] = blank

    @pl.when(jnp.logical_not(has_up))
    def _():
        for win in wins:
            win[HALO + size:] = blank

    begin_ring(1)
    hop(2, 0)
    along_x(1).wait_recv()
    relay_y().start()
    hop(1, 1)
    along_y(0).wait_recv()
    relay_x().start()
    for d in range(3, planes):
        hop(d, 0)
        hop(d - 1, 1)
    from_mate(0)

    @pl.when(home)
    def _():
        keep_own(0).wait()
        keep_own(1).wait()

    wkv = lambda: wkv_ref[...].reshape(-1, wide)
    wq = lambda: wq_ref[...].reshape(-1, wq_ref.shape[2])

    def make_keys(p, mine, first, length):
        pos = b if mine else 1 - b
        at = pl.ds(pl.multiple_of(pos * rows + first, 16), length)
        raw = jnp.dot(shard_rows(p, mine, first, length), wkv(), preferred_element_type=jnp.float32)
        cosine, sine = cos_ref[p, at], sin_ref[p, at]
        keys = [turn(raw[:, h * HEAD:(h + 1) * HEAD], kg_ref[...], cosine, sine) for h in range(heads)]
        done = jnp.concatenate(keys + [raw[:, width:2 * width].astype(jnp.bfloat16)], axis=1)
        wins[p][pl.ds(pl.multiple_of(HALO + pos * rows + first, 16), length)] = done
        lead_ref[p, at] = raw[:, 2 * width:]

    def make_queries(p, mine, first, length):
        pos = b if mine else 1 - b
        at = pl.ds(pl.multiple_of(pos * rows + first, 16), length)
        raw = jnp.dot(shard_rows(p, mine, first, length), wq(), preferred_element_type=jnp.float32)
        raw = jnp.concatenate([lead_ref[p, at], raw[:, :width - extra]], axis=1)
        cosine, sine = cos_ref[p, at], sin_ref[p, at]
        q_ref[p, at] = jnp.concatenate(
            [turn(raw[:, h * HEAD:(h + 1) * HEAD], qg_ref[...], cosine, sine) for h in range(heads)], axis=1)

    def upward(p, k):
        return remote(wins[p].at[pl.ds(size + k * BLOCK, BLOCK)], wins[p].at[pl.ds(k * BLOCK, BLOCK)],
                      halo_send.at[p, 0, k], halo_recv.at[p, 0, k], f, s + 2)

    def downward(p, k):
        return remote(wins[p].at[pl.ds(HALO + k * BLOCK, BLOCK)], wins[p].at[pl.ds(HALO + size + k * BLOCK, BLOCK)],
                      halo_send.at[p, 1, k], halo_recv.at[p, 1, k], f, s - 2)

    per = rows // BLOCK
    reach = HALO // BLOCK
    total = size // BLOCK

    def send_block(p, i):
        if i >= total - reach:
            @pl.when(has_up)
            def _():
                upward(p, i - (total - reach)).start()
        if i < reach:
            @pl.when(has_down)
            def _():
                downward(p, i).start()

    def send_shard(p, pos):
        for q in range(2):
            @pl.when(pos == q)
            def _():
                for k in range(per):
                    send_block(p, q * per + k)

    make_keys(0, True, 0, rows)
    send_shard(0, b)
    hop(planes - 1, 1)
    along_y(1).wait_recv()
    make_keys(0, False, 0, rows)
    send_shard(0, 1 - b)
    along_x(0).wait_recv()
    make_keys(1, True, 0, rows)
    send_shard(1, b)
    from_mate(1)
    make_queries(0, True, 0, rows)
    make_queries(0, False, 0, rows)
    make_queries(1, True, 0, rows)

    scale = HEAD ** (-0.5) * 1.4426950408889634

    def attend_block(p, pos, k):
        i = pos * per + k
        first = pl.multiple_of(i * BLOCK, BLOCK)
        where_q = a * size + i * BLOCK

        def image(j, state):
            start, begin, length = state
            inside = where_q >= start
            blocks = blocks_ref[packs[p], j] * BLOCK
            return start + blocks, jnp.where(inside, start, begin), jnp.where(inside, blocks, length)

        _, begin, length = lax.fori_loop(0, blocks_ref.shape[1], image, (jnp.int32(0), jnp.int32(0), jnp.int32(0)))
        back = where_q - begin
        chosen = wins[p][pl.ds(pl.multiple_of(first + HALO, BLOCK), span)]
        for shift in range(BLOCK, HALO + 1, BLOCK):
            earlier = wins[p][pl.ds(pl.multiple_of(first + HALO - shift, BLOCK), span)]
            chosen = jnp.where(back == shift, earlier, chosen)
        mask = lax.broadcasted_iota(jnp.int32, (span, BLOCK), 0) < length
        queries = q_ref[p, pl.ds(first, BLOCK)]
        outs = []
        for h in range(heads):
            keys = chosen[:, h * HEAD:(h + 1) * HEAD]
            vals = chosen[:, width + h * HEAD:width + (h + 1) * HEAD]
            scores = lax.dot_general(keys, queries[:, h * HEAD:(h + 1) * HEAD], (((1,), (1,)), ((), ())),
                                     preferred_element_type=jnp.float32)
            scores = jnp.where(mask, scores, -1e30)
            top = jnp.max(scores, axis=0, keepdims=True)
            expo = jnp.exp2((scores - top) * scale)
            norm = jnp.sum(expo, axis=0, keepdims=True)
            probs = (expo * (1.0 / norm)).astype(jnp.bfloat16)
            outs.append(lax.dot_general(vals, probs, (((0,), (0,)), ((), ())),
                                        preferred_element_type=jnp.float32).astype(jnp.bfloat16))
        mixed[p, pos, k] = jnp.concatenate(outs, axis=0)

    def deliver(p, k, blk):
        pos, seat = (1 - b, other) if k == 0 else (b, s)
        owner = f if p == 0 else beside
        way = 0 if p == 0 else 2 - k
        return remote(mixed.at[p, pos, blk], (land_y, land_x, land_d)[way].at[blk],
                      out_send.at[way, blk], out_recv.at[way, blk], owner, seat)

    def attend(p, k):
        pos = 1 - b if k == 0 else b
        for i in range(per):
            attend_block(p, pos, i)
            if p == 1 or k == 0:
                deliver(p, k, i).start()

    def place_group(group, blocks):
        for g in range(4):
            @pl.when(group == g)
            def _():
                for i in range(per):
                    o_ref[0, i * BLOCK:(i + 1) * BLOCK, g * width:(g + 1) * width] = blocks(i).T

    def halo_wait(p):
        @pl.when(has_down)
        def _():
            for k in range(reach):
                upward(p, k).wait_recv()

        @pl.when(has_up)
        def _():
            for k in range(reach):
                downward(p, k).wait_recv()

    relay_x().wait_recv()
    relay_y().wait_recv()
    make_keys(1, False, 0, rows)
    send_shard(1, 1 - b)
    halo_wait(0)
    attend(0, 0)
    attend(0, 1)
    make_queries(1, False, 0, rows)
    place_group(2 * x + b, lambda i: mixed[0, b, i])
    for i in range(per):
        deliver(0, 0, i).wait_recv()
    place_group(2 * x + 1 - b, lambda i: land_y[i])
    halo_wait(1)
    attend(1, 0)
    attend(1, 1)

    def drain(plane, carry):
        for kind in range(2):
            @pl.when((plane <= a) & has_up)
            def _():
                push(plane, kind, 0).wait_send()

            @pl.when((plane >= a) & has_down)
            def _():
                push(plane, kind, 1).wait_send()

            push(plane, kind, 2).wait_send()
        return carry

    lax.fori_loop(0, planes, drain, 0)

    @pl.when(jnp.logical_not(home))
    def _():
        pass_over(0).wait_send()
        pass_over(1).wait_send()

    for k in range(2):
        along_x(k).wait_send()
        along_y(k).wait_send()
    relay_x().wait_send()
    relay_y().wait_send()
    for p in range(2):
        for k in range(reach):
            @pl.when(has_up)
            def _():
                upward(p, k).wait_send()

            @pl.when(has_down)
            def _():
                downward(p, k).wait_send()

    for i in range(per):
        deliver(1, 1, i).wait_recv()
    place_group(2 * (1 - x) + b, lambda i: land_x[i])
    for i in range(per):
        deliver(1, 0, i).wait_recv()
    place_group(2 * (1 - x) + 1 - b, lambda i: land_d[i])
    for i in range(per):
        deliver(0, 0, i).wait_send()
        deliver(1, 0, i).wait_send()
        deliver(1, 1, i).wait_send()


def fused(planes, tokens, norm_gain, w_qkv, q_gain, k_gain, img_blocks, img_width):
    row_count, model = tokens.shape[1], tokens.shape[2]
    depth, width = w_qkv.shape[1], w_qkv.shape[2]
    size = 2 * row_count
    wide = pl.cdiv(2 * width, 128) * 128
    tail = pl.cdiv(3 * width - wide, 128) * 128
    quarter = HEAD // 4
    freq = np.tile(np.float32(10000.0) ** (-np.arange(quarter, dtype=np.float32) / np.float32(quarter)), 4)[None]
    vmem = pl.BlockSpec(memory_space=pltpu.VMEM)
    smem = pl.BlockSpec(memory_space=pltpu.SMEM)
    anywhere = pl.BlockSpec(memory_space=pl.ANY)
    dma = pltpu.SemaphoreType.DMA
    return pl.pallas_call(
        functools.partial(fused_kernel, planes),
        out_shape=jax.ShapeDtypeStruct((1, row_count, 4 * width), jnp.bfloat16),
        in_specs=[anywhere] * 6 + [smem] * 2,
        out_specs=vmem,
        scratch_shapes=[
            pltpu.VMEM(tokens.shape, jnp.bfloat16),
            pltpu.VMEM(norm_gain.shape, jnp.float32),
            pltpu.VMEM(w_qkv.shape, jnp.bfloat16),
            pltpu.VMEM((1, HEAD), jnp.float32),
            pltpu.VMEM((1, HEAD), jnp.float32),
            pltpu.VMEM((1, HEAD), jnp.float32),
            dma((6,)),
            pltpu.VMEM((row_count, model), jnp.bfloat16),
            pltpu.VMEM((row_count, model), jnp.bfloat16),
            pltpu.VMEM((row_count, model), jnp.bfloat16),
            pltpu.VMEM((row_count, model), jnp.bfloat16),
            pltpu.VMEM((2 * planes, depth, wide), jnp.bfloat16),
            pltpu.VMEM((2 * planes, depth, tail), jnp.bfloat16),
            pltpu.VMEM((depth, wide), jnp.bfloat16),
            pltpu.VMEM((depth, tail), jnp.bfloat16),
            pltpu.VMEM((2, size, HEAD), jnp.float32),
            pltpu.VMEM((2, size, HEAD), jnp.float32),
            pltpu.VMEM((2, size, width), jnp.bfloat16),
            pltpu.VMEM((2, size, wide - 2 * width), jnp.float32),
            pltpu.VMEM((size + 2 * HALO, 2 * width), jnp.bfloat16),
            pltpu.VMEM((size + 2 * HALO, 2 * width), jnp.bfloat16),
            pltpu.VMEM((2, 2, row_count // BLOCK, width, BLOCK), jnp.bfloat16),
            pltpu.VMEM((row_count // BLOCK, width, BLOCK), jnp.bfloat16),
            pltpu.VMEM((row_count // BLOCK, width, BLOCK), jnp.bfloat16),
            pltpu.VMEM((row_count // BLOCK, width, BLOCK), jnp.bfloat16),
            dma((3, 2)),
            dma((3, 2)),
            dma((planes, 2, 3)),
            dma((2 * planes, 2)),
            dma((2,)),
            dma((2, 2, HALO // BLOCK)),
            dma((2, 2, HALO // BLOCK)),
            dma((3, row_count // BLOCK)),
            dma((3, row_count // BLOCK)),
            dma((3,)),
        ],
        compiler_params=pltpu.CompilerParams(
            collective_id=0, has_side_effects=True, vmem_limit_bytes=60 * 1024 * 1024),
        name="fused",
    )(tokens, norm_gain, w_qkv, q_gain[None], k_gain[None], jnp.asarray(freq), img_blocks, img_width)


def shards(planes, tokens, norm_gain, w_qkv, q_gain, k_gain, img_blocks, img_width):
    row_count, model = tokens.shape[1], tokens.shape[2]
    width = w_qkv.shape[2]
    size = 2 * row_count
    seqs = 2 * planes
    depth = w_qkv.shape[1]
    broad = pl.cdiv(3 * width, 128) * 128
    quarter = HEAD // 4
    freq = np.tile(np.float32(10000.0) ** (-np.arange(quarter, dtype=np.float32) / np.float32(quarter)), 4)[None]
    vmem = pl.BlockSpec(memory_space=pltpu.VMEM)
    smem = pl.BlockSpec(memory_space=pltpu.SMEM)
    anywhere = pl.BlockSpec(memory_space=pl.ANY)
    table = jax.ShapeDtypeStruct((2, size, HEAD), jnp.float32)
    gathered, weights, cosine, sine = pl.pallas_call(
        functools.partial(gather_kernel, planes),
        out_shape=(
            jax.ShapeDtypeStruct((2, 2, row_count, model), jnp.bfloat16),
            jax.ShapeDtypeStruct((seqs, depth, broad), jnp.bfloat16),
            table,
            table,
        ),
        in_specs=[vmem, vmem, vmem, smem, smem, vmem],
        out_specs=(anywhere, anywhere, vmem, vmem),
        scratch_shapes=[
            pltpu.VMEM((row_count, model), jnp.bfloat16),
            pltpu.VMEM((depth, broad), jnp.bfloat16),
            pltpu.SemaphoreType.DMA((7,)),
            pltpu.SemaphoreType.DMA((7,)),
            pltpu.SemaphoreType.DMA((seqs, 3)),
            pltpu.SemaphoreType.DMA((seqs,)),
            pltpu.SemaphoreType.DMA((2,)),
        ],
        compiler_params=pltpu.CompilerParams(collective_id=0, has_side_effects=True),
        name="gather",
    )(tokens, norm_gain, w_qkv, img_blocks, img_width, jnp.asarray(freq))
    attended = pl.pallas_call(
        functools.partial(attend_kernel, planes),
        out_shape=jax.ShapeDtypeStruct((1, row_count, 4 * width), jnp.bfloat16),
        in_specs=[anywhere, anywhere, vmem, vmem, vmem, vmem, smem],
        out_specs=vmem,
        scratch_shapes=[
            pltpu.VMEM((2, size, model), jnp.bfloat16),
            pltpu.VMEM((model, broad), jnp.bfloat16),
            pltpu.VMEM((2, size, width), jnp.bfloat16),
            pltpu.VMEM((size + 2 * HALO, 2 * width), jnp.bfloat16),
            pltpu.VMEM((size + 2 * HALO, 2 * width), jnp.bfloat16),
            pltpu.VMEM((2, size, width), jnp.bfloat16),
            pltpu.VMEM((4, row_count, width), jnp.bfloat16),
            pltpu.SemaphoreType.DMA((2, 2)),
            pltpu.SemaphoreType.DMA((2, 2)),
            pltpu.SemaphoreType.DMA((2, 2)),
            pltpu.SemaphoreType.DMA((4,)),
            pltpu.SemaphoreType.DMA((3,)),
            pltpu.SemaphoreType.DMA((3,)),
        ],
        compiler_params=pltpu.CompilerParams(collective_id=1, has_side_effects=True),
        name="attend",
    )(gathered.reshape(2, size, model), weights.reshape(model, broad), cosine, sine,
      q_gain[None], k_gain[None], img_blocks)
    return attended


def solution(mesh):
    assert mesh.shape["fsdp"] == 4 and mesh.shape["seq"] % 2 == 0
    planes = mesh.shape["seq"] // 2

    def body(tokens, norm_gain, w_qkv, *rest):
        whole_tiles = w_qkv.shape[1] % 16 == 0 and 2 * w_qkv.shape[2] % 128 != 0
        return (fused if whole_tiles else shards)(planes, tokens, norm_gain, w_qkv, *rest)

    return jax.shard_map(
        body,
        mesh=mesh,
        in_specs=(P("fsdp", "seq", None), P(), P(None, "seq", "fsdp"), P(), P(), P(), P()),
        out_specs=P("fsdp", "seq", None),
        check_vma=False,
    )
```

```python
import functools

import jax
import jax.numpy as jnp
import numpy as np
from jax import lax
from jax.experimental import pallas as pl
from jax.experimental.pallas import tpu as pltpu
from jax.sharding import PartitionSpec as P

HEAD = 96
BLOCK = 128
HALO = 3 * BLOCK
MESH = pl.DeviceIdType.MESH

eps_model = 1e-06


def rms_norm(values, gain):
    return values * lax.rsqrt(jnp.mean(values * values, axis=-1, keepdims=True) + eps_model) * gain


def place():
    f = lax.axis_index("fsdp")
    s = lax.axis_index("seq")
    return f // 2, f % 2, s // 2, s % 2, f, s


def remote(src, dst, send, recv, f, s):
    return pltpu.make_async_remote_copy(
        src_ref=src, dst_ref=dst, send_sem=send, recv_sem=recv,
        device_id={"fsdp": f, "seq": s}, device_id_type=MESH,
    )


def signal(sem, f, s):
    pl.semaphore_signal(sem, inc=1, device_id={"fsdp": f, "seq": s}, device_id_type=MESH)


def gather_kernel(planes, raw_ref, gain_ref, parts_ref, blocks_ref, widths_ref, freq_ref,
                  t_ref, wall_ref, cos_ref, sin_ref,
                  tok_ref, w_ref, tok_send, tok_recv, w_send, w_recv, local_sem):
    x, c, a, b, f, s = place()
    rows = tok_ref.shape[0]
    half = rows // 2
    other = s + 1 - 2 * b
    home = c == b
    barrier = pltpu.get_barrier_semaphore()
    signal(barrier, 2 * x + 1 - c, s)
    for core in range(2):
        signal(barrier, 2 * (1 - x) + core, s)
        signal(barrier, 2 * x + core, other)

    @pl.when(a > 0)
    def _():
        signal(barrier, f, s - 2)

    @pl.when(a < planes - 1)
    def _():
        signal(barrier, f, s + 2)

    step = 32

    @pl.loop(0, rows // step)
    def _(i):
        at = pl.ds(pl.multiple_of(i * step, step), step)
        tok_ref[at] = rms_norm(raw_ref[0, at].astype(jnp.float32), gain_ref[...][None]).astype(jnp.bfloat16)

    spare = jnp.zeros((w_ref.shape[0], w_ref.shape[1] - 3 * parts_ref.shape[2]), jnp.bfloat16)
    w_ref[...] = jnp.concatenate([parts_ref[1], parts_ref[2], parts_ref[0], spare], axis=1)
    pl.semaphore_wait(barrier, 5 + (a > 0).astype(jnp.int32) + (a < planes - 1).astype(jnp.int32))

    def part(xx, yy, h):
        return t_ref.at[xx, yy, pl.ds(pl.multiple_of(h * half, half), half)]

    keep = pltpu.make_async_copy(tok_ref, t_ref.at[x, b], local_sem.at[0])
    whole = remote(tok_ref, t_ref.at[x, b], tok_send.at[0], tok_recv.at[6], 2 * x + 1 - c, s)
    along = [remote(tok_ref.at[pl.ds(h * half, half)], part(x, b, h), tok_send.at[1 + h], tok_recv.at[1],
                    2 * (1 - x) + h, s) for h in range(2)]
    across = [remote(tok_ref.at[pl.ds(h * half, half)], part(x, b, h), tok_send.at[1 + h], tok_recv.at[0],
                     2 * x + h, other) for h in range(2)]

    @pl.when(home)
    def _():
        for copy in along:
            copy.start()
        whole.start()
        keep.start()

    @pl.when(jnp.logical_not(home))
    def _():
        for copy in across:
            copy.start()

    keep_w = pltpu.make_async_copy(w_ref, wall_ref.at[s], local_sem.at[1])
    keep_w.start()

    def push(src, slot, way):
        target = (s + 2, s - 2, other)[way]
        return remote(src, wall_ref.at[slot], w_send.at[slot, way], w_recv.at[slot], f, target)

    def spread(src, slot, up, down):
        if up:
            @pl.when(a < planes - 1)
            def _():
                push(src, slot, 0).start()
        if down:
            @pl.when(a > 0)
            def _():
                push(src, slot, 1).start()

        @pl.when(crosses(slot // 2))
        def _():
            push(src, slot, 2).start()

    middle = planes // 2
    bottom, top = 1 - b, 2 * (planes - 1) + 1 - b
    lifts = jnp.logical_not(home) & (a >= middle - 1) & (a < planes - 1)
    drops = jnp.logical_not(home) & (a <= middle) & (a > 0)

    def crosses(k):
        skipped = ((k == 0) & (a >= middle)) | ((k == planes - 1) & (a < middle))
        return jnp.logical_not(home & skipped)

    spread(w_ref, s, True, True)

    size = cos_ref.shape[1]
    lane = lax.broadcasted_iota(jnp.int32, (size, HEAD), 1)
    where = a * size + lax.broadcasted_iota(jnp.int32, (size, HEAD), 0)
    by_row = lane < HEAD // 2
    low = (lane < HEAD // 4) | ((lane >= HEAD // 2) & (lane < 3 * HEAD // 4))
    for px in range(2):
        pack = 2 * px + b

        def image(j, carry):
            start, begin, wide = carry
            inside = where >= start
            begin = jnp.where(inside, start, begin)
            wide = jnp.where(inside, widths_ref[pack, j], wide)
            return start + blocks_ref[pack, j] * BLOCK, begin, wide

        zero = jnp.zeros((size, HEAD), jnp.int32)
        _, begin, wide = lax.fori_loop(0, blocks_ref.shape[1], image, (jnp.int32(0), zero, zero + 1))
        offset = (where - begin).astype(jnp.float32)
        wide = wide.astype(jnp.float32)
        row = jnp.floor((offset + 0.5) / wide)
        col = offset - row * wide
        angle = jnp.where(by_row, row, col) * freq_ref[...]
        cos_ref[px] = jnp.cos(angle)
        sine = jnp.sin(angle)
        sin_ref[px] = jnp.where(low, -sine, sine)

    mine = [(x, 1 - b), (1 - x, b), (1 - x, 1 - b)]

    def share(k):
        spot = part(mine[k][0], mine[k][1], c)
        return remote(spot, spot, tok_send.at[3 + k], tok_recv.at[3 + k], 2 * x + 1 - c, s)

    def landed(k):
        spot = part(mine[k][0], mine[k][1], c)
        return remote(spot, spot, tok_send.at[3 + k], tok_recv.at[k], 2 * x + 1 - c, s)

    spot = part(x, 1 - b, c)
    relay = remote(spot, spot, tok_send.at[6], tok_recv.at[2], 2 * (1 - x) + c, s)
    def hop(d, carry):
        lower = a - d
        upper = a + d

        @pl.when(lower >= 0)
        def _():
            slot = jnp.maximum(2 * lower + b, 0)
            push(wall_ref.at[slot], slot, 0).wait_recv()
            spread(wall_ref.at[slot], slot, True, False)

        @pl.when(upper < planes)
        def _():
            slot = jnp.minimum(2 * upper + b, 2 * planes - 1)
            push(wall_ref.at[slot], slot, 1).wait_recv()
            spread(wall_ref.at[slot], slot, False, True)

        return carry

    lax.fori_loop(1, 2, hop, 0)
    landed(0).wait_recv()
    relay.start()
    share(0).start()
    lax.fori_loop(2, 3, hop, 0)

    @pl.when(lifts)
    def _():
        push(wall_ref.at[bottom], bottom, 0).wait_recv()
        push(wall_ref.at[bottom], bottom, 0).start()

    @pl.when(drops)
    def _():
        push(wall_ref.at[top], top, 1).wait_recv()
        push(wall_ref.at[top], top, 1).start()

    lax.fori_loop(3, planes, hop, 0)
    landed(1).wait_recv()
    share(1).start()
    landed(2).wait_recv()
    share(2).start()

    def finish(k, carry):
        slot = 2 * k + 1 - b
        early = ((k == 0) & lifts) | ((k == planes - 1) & drops)

        @pl.when(jnp.logical_not(early))
        def _():
            push(wall_ref.at[slot], slot, 2).wait_recv()

        sent = 2 * k + b

        @pl.when(crosses(k))
        def _():
            push(wall_ref.at[sent], sent, 2).wait_send()

        @pl.when((k <= a) & (a < planes - 1))
        def _():
            push(wall_ref.at[sent], sent, 0).wait_send()

        @pl.when((k >= a) & (a > 0))
        def _():
            push(wall_ref.at[sent], sent, 1).wait_send()

        return carry

    lax.fori_loop(0, planes, finish, 0)

    @pl.when(lifts)
    def _():
        push(wall_ref.at[bottom], bottom, 0).wait_send()

    @pl.when(drops)
    def _():
        push(wall_ref.at[top], top, 1).wait_send()

    keep_w.wait()

    @pl.when(home)
    def _():
        for copy in along:
            copy.wait_send()
        whole.wait_send()
        keep.wait()

    @pl.when(jnp.logical_not(home))
    def _():
        for copy in across:
            copy.wait_send()
        whole.wait_recv()

    relay.wait_send()
    for k in range(3):
        share(k).wait_send()
        spot = part(mine[k][0], mine[k][1], 1 - c)
        remote(spot, spot, tok_send.at[3 + k], tok_recv.at[3 + k], 2 * x + 1 - c, s).wait_recv()


def turn(raw, gain, cosine, sine):
    parts = HEAD // 4
    n = rms_norm(raw, gain)
    swapped = jnp.concatenate(
        [n[:, parts:2 * parts], n[:, :parts], n[:, 3 * parts:], n[:, 2 * parts:3 * parts]], axis=1)
    return (n * cosine + swapped * sine).astype(jnp.bfloat16)


def attend_kernel(planes, t_ref, wall_ref, cos_ref, sin_ref, qg_ref, kg_ref, blocks_ref, o_ref,
                  x_ref, w_ref, q_ref, low_win, high_win, mixed, landed, halo_send, halo_recv, out_send, out_recv,
                  local_sem, load_sem):
    x, c, a, b, f, s = place()
    size, width = q_ref.shape[1], q_ref.shape[2]
    rows = size // 2
    inner = size - HALO
    span = HALO + BLOCK
    wins = (low_win, high_win)
    home = c == b
    load_w = pltpu.make_async_copy(wall_ref, w_ref, load_sem.at[2])
    loads = [pltpu.make_async_copy(t_ref.at[p], x_ref.at[p], load_sem.at[p]) for p in range(2)]
    load_w.start()
    for load in loads:
        load.start()
    barrier = pltpu.get_barrier_semaphore()
    has_down, has_up = a > 0, a < planes - 1
    for core in range(4):
        @pl.when(jnp.logical_or(b != c, f != core))
        def _():
            signal(barrier, core, 2 * a + c)

    @pl.when(has_down)
    def _():
        signal(barrier, f, s - 2)

    @pl.when(has_up)
    def _():
        signal(barrier, f, s + 2)

    count = 4 - home.astype(jnp.int32) + has_down.astype(jnp.int32) + has_up.astype(jnp.int32)
    pl.semaphore_wait(barrier, count)

    def upward(p):
        return remote(wins[p].at[pl.ds(HALO + inner, HALO)], wins[p].at[pl.ds(0, HALO)],
                      halo_send.at[p, 0], halo_recv.at[p, 0], f, s + 2)

    def downward(p):
        return remote(wins[p].at[pl.ds(HALO, HALO)], wins[p].at[pl.ds(HALO + size, HALO)],
                      halo_send.at[p, 1], halo_recv.at[p, 1], f, s - 2)

    blank = jnp.zeros((HALO, 2 * width), jnp.bfloat16)

    @pl.when(jnp.logical_not(has_down))
    def _():
        for win in wins:
            win[:HALO] = blank

    @pl.when(jnp.logical_not(has_up))
    def _():
        for win in wins:
            win[HALO + size:] = blank

    heads = width // HEAD
    shift_q = 2 * width // 128 * 128

    def make_keys(p, i):
        first = i * rows
        at = slice(first, first + rows)
        raw = jnp.dot(x_ref[p, at], w_ref[:, :pl.cdiv(2 * width, 128) * 128], preferred_element_type=jnp.float32)
        keys = [turn(raw[:, h * HEAD:(h + 1) * HEAD], kg_ref[...], cos_ref[p, at], sin_ref[p, at])
                for h in range(heads)]
        done = jnp.concatenate(keys + [raw[:, width:2 * width].astype(jnp.bfloat16)], axis=1)
        wins[p][HALO + first:HALO + first + rows] = done

    def make_queries(p, i):
        at = slice(i * rows, (i + 1) * rows)
        raw = jnp.dot(x_ref[p, at], w_ref[:, shift_q:], preferred_element_type=jnp.float32)
        raw = raw[:, 2 * width - shift_q:]
        q_ref[p, at] = jnp.concatenate(
            [turn(raw[:, h * HEAD:(h + 1) * HEAD], qg_ref[...], cos_ref[p, at], sin_ref[p, at])
             for h in range(heads)], axis=1)

    load_w.wait()
    for load in loads:
        load.wait()
    for p in range(2):
        for i in range(2):
            make_keys(p, i)

        make_queries(p, 0)

        @pl.when(has_up)
        def _():
            upward(p).start()

        @pl.when(has_down)
        def _():
            downward(p).start()

    for p in range(2):
        make_queries(p, 1)

    scale = HEAD ** (-0.5) * 1.4426950408889634

    def deliver(p, yy):
        return remote(mixed.at[p, pl.ds(yy * rows, rows)], landed.at[f],
                      out_send.at[p, yy], out_recv.at[f], 2 * p + b, 2 * a + yy)

    def to_self(p, yy):
        return pltpu.make_async_copy(mixed.at[p, pl.ds(yy * rows, rows)], landed.at[f], local_sem.at[2])

    def is_self(p, yy):
        return home & (p == x) & (yy == b)

    for p in range(2):
        pack = 2 * p + b

        @pl.when(has_down)
        def _():
            upward(p).wait_recv()

        @pl.when(has_up)
        def _():
            downward(p).wait_recv()

        def block(i, carry):
            first = pl.multiple_of(i * BLOCK, BLOCK)
            where_q = a * size + i * BLOCK

            def image(j, state):
                start, begin, length = state
                inside = where_q >= start
                blocks = blocks_ref[pack, j] * BLOCK
                return start + blocks, jnp.where(inside, start, begin), jnp.where(inside, blocks, length)

            _, begin, length = lax.fori_loop(0, blocks_ref.shape[1], image,
                                             (jnp.int32(0), jnp.int32(0), jnp.int32(0)))
            back = where_q - begin
            chosen = wins[p][pl.ds(pl.multiple_of(first + HALO, BLOCK), span)]
            for shift in range(BLOCK, HALO + 1, BLOCK):
                earlier = wins[p][pl.ds(pl.multiple_of(first + HALO - shift, BLOCK), span)]
                chosen = jnp.where(back == shift, earlier, chosen)
            mask = lax.broadcasted_iota(jnp.int32, (BLOCK, span), 1) < length
            queries = q_ref[p, pl.ds(first, BLOCK)]
            outs = []
            for h in range(width // HEAD):
                keys = chosen[:, h * HEAD:(h + 1) * HEAD]
                vals = chosen[:, width + h * HEAD:width + (h + 1) * HEAD]
                scores = lax.dot_general(queries[:, h * HEAD:(h + 1) * HEAD], keys, (((1,), (1,)), ((), ())),
                                         preferred_element_type=jnp.float32)
                scores = jnp.where(mask, scores, -1e30)
                top = jnp.max(scores, axis=-1, keepdims=True)
                expo = jnp.exp2((scores - top) * scale)
                norm = jnp.sum(expo, axis=-1, keepdims=True)
                probs = (expo * (1.0 / norm)).astype(jnp.bfloat16)
                outs.append(jnp.dot(probs, vals, preferred_element_type=jnp.float32).astype(jnp.bfloat16))
            mixed[p, pl.ds(first, BLOCK)] = jnp.concatenate(outs, axis=1)
            return carry

        lax.fori_loop(0, size // BLOCK, block, 0)
        for yy in range(2):
            @pl.when(is_self(p, yy))
            def _():
                to_self(p, yy).start()

            @pl.when(jnp.logical_not(is_self(p, yy)))
            def _():
                deliver(p, yy).start()

    for p in range(2):
        for yy in range(2):
            @pl.when(is_self(p, yy))
            def _():
                to_self(p, yy).wait()

            @pl.when(jnp.logical_not(is_self(p, yy)))
            def _():
                deliver(p, yy).wait_send()

        @pl.when(has_up)
        def _():
            upward(p).wait_send()

        @pl.when(has_down)
        def _():
            downward(p).wait_send()

    for core in range(4):
        @pl.when(jnp.logical_or(b != c, f != core))
        def _():
            remote(mixed.at[0, pl.ds(0, rows)], landed.at[core], out_send.at[0, 0], out_recv.at[core], f, s).wait_recv()

    o_ref[0] = jnp.concatenate([landed[core] for core in range(4)], axis=1)


def fused_kernel(planes, raw_in, gain_in, parts_in, qg_in, kg_in, freq_in, blocks_ref, widths_ref, o_ref,
                 raw_ref, gain_ref, parts_ref, qg_ref, kg_ref, freq_ref, load_sem, own_ref, xa_ref, xb_ref, xd_ref, wkv_ref, wq_ref, okv_ref, oq_ref, cos_ref, sin_ref, q_ref, lead_ref, win_a, win_b, mixed,
                 land_y, land_x, land_d, tok_send, tok_recv, w_send, w_recv, pass_send, halo_send, halo_recv, out_send, out_recv,
                 local_sem):
    x, c, a, b, f, s = place()
    loads = [pltpu.make_async_copy(src, dst, load_sem.at[i]) for i, (src, dst) in enumerate((
        (parts_in, parts_ref), (raw_in, raw_ref), (gain_in, gain_ref), (qg_in, qg_ref), (kg_in, kg_ref),
        (freq_in, freq_ref)))]
    for load in loads:
        load.start()
    rows = raw_ref.shape[1]
    depth, width = parts_ref.shape[1], parts_ref.shape[2]
    size = 2 * rows
    heads = width // HEAD
    wide = wkv_ref.shape[2]
    extra = wide - 2 * width
    wins = (win_a, win_b)
    span = HALO + BLOCK
    home = c == b
    has_down, has_up = a > 0, a < planes - 1
    mate = 2 * x + 1 - c
    beside = 2 * (1 - x) + c
    other = s + 1 - 2 * b
    packs = (2 * x + c, 2 * (1 - x) + c)
    cut = rows * 6 // 8 // 32 * 32

    barrier = pltpu.get_barrier_semaphore()
    signal(barrier, mate, s)
    signal(barrier, beside, s)
    signal(barrier, f, other)
    signal(barrier, beside, other)

    @pl.when(jnp.logical_not(home))
    def _():
        signal(barrier, mate, other)

    @pl.when(has_down)
    def _():
        signal(barrier, f, s - 2)

    @pl.when(has_up)
    def _():
        signal(barrier, f, s + 2)

    loads[0].wait()
    okv_ref[...] = jnp.concatenate([parts_ref[1], parts_ref[2], parts_ref[0, :, :extra]], axis=1)
    oq_ref[...] = jnp.concatenate(
        [parts_ref[0, :, extra:], jnp.zeros((depth, oq_ref.shape[1] - width + extra), jnp.bfloat16)], axis=1)
    for load in loads[1:]:
        load.wait()
    step = 32

    def normalize(i, carry):
        at = pl.ds(pl.multiple_of(i * step, step), step)
        own_ref[at] = rms_norm(raw_ref[0, at].astype(jnp.float32), gain_ref[...][None]).astype(jnp.bfloat16)
        return carry

    lax.fori_loop(cut // step, rows // step, normalize, 0)
    count = 4 + jnp.logical_not(home).astype(jnp.int32) + has_down.astype(jnp.int32) + has_up.astype(jnp.int32)
    pl.semaphore_wait(barrier, count)


    def slot_of(plane):
        return 2 * plane + c

    def spot(slot, kind):
        return (wkv_ref, wq_ref)[kind].at[slot]

    def push(plane, kind, way, src=None):
        slot = slot_of(plane)
        target = ((f, s + 2), (f, s - 2), (mate, s))[way]
        return remote(spot(slot, kind) if src is None else src, spot(slot, kind), w_send.at[plane, kind, way], w_recv.at[slot, kind], *target)

    def pass_over(kind):
        return remote((okv_ref, oq_ref)[kind], spot(s, kind), pass_send.at[kind], w_recv.at[s, kind], mate, other)

    def spread(plane, kind, up, down, src=None):
        if up:
            @pl.when(has_up)
            def _():
                push(plane, kind, 0, src).start()
        if down:
            @pl.when(has_down)
            def _():
                push(plane, kind, 1, src).start()
        push(plane, kind, 2, src).start()

    def keep_own(kind):
        return pltpu.make_async_copy((okv_ref, oq_ref)[kind], spot(s, kind), local_sem.at[1 + kind])

    def begin_ring(kind):
        @pl.when(home)
        def _():
            spread(a, kind, True, True, (okv_ref, oq_ref)[kind])
            keep_own(kind).start()

        @pl.when(jnp.logical_not(home))
        def _():
            slot = slot_of(a)
            remote(spot(slot, kind), spot(slot, kind), pass_send.at[kind], w_recv.at[slot, kind], mate, other).wait_recv()
            spread(a, kind, True, True)

    def hop(d, kind):
        @pl.when(a >= d)
        def _():
            plane = jnp.maximum(a - d, 0)
            push(plane, kind, 0).wait_recv()
            spread(plane, kind, True, False)

        @pl.when(a + d < planes)
        def _():
            plane = jnp.minimum(a + d, planes - 1)
            push(plane, kind, 1).wait_recv()
            spread(plane, kind, False, True)

    def from_mate(kind):
        for plane in range(planes):
            slot = 2 * plane + 1 - c
            remote(spot(slot, kind), spot(slot, kind), w_send.at[plane, kind, 2], w_recv.at[slot, kind], mate, s).wait_recv()

    @pl.when(jnp.logical_not(home))
    def _():
        pass_over(0).start()
        pass_over(1).start()

    @pl.when(home)
    def _():
        spread(a, 0, True, True, okv_ref)
        keep_own(0).start()

    def piece(ref, k):
        first, length = ((0, cut), (cut, rows - cut))[k]
        return ref.at[pl.ds(first, length)]

    def along_x(k):
        return remote(piece(own_ref, k), piece(xb_ref, k), tok_send.at[0, k], tok_recv.at[0, k], beside, s)

    def along_y(k):
        return remote(piece(own_ref, k), piece(xa_ref, k), tok_send.at[1, k], tok_recv.at[1, k], f, other)

    def relay_x():
        return remote(piece(xa_ref, 0), piece(xd_ref, 0), tok_send.at[2, 0], tok_recv.at[2, 0], beside, s)

    def relay_y():
        return remote(piece(xb_ref, 1), piece(xd_ref, 1), tok_send.at[2, 1], tok_recv.at[2, 1], f, other)

    def shard_rows(p, mine, first, length):
        ref = ((xd_ref, xb_ref), (xa_ref, own_ref))[p == 0][mine]
        return ref[first:first + length]

    along_x(1).start()
    lax.fori_loop(0, cut // step, normalize, 0)
    along_y(0).start()
    along_x(0).start()
    along_y(1).start()

    lane = lax.broadcasted_iota(jnp.int32, (size, HEAD), 1)
    where = a * size + lax.broadcasted_iota(jnp.int32, (size, HEAD), 0)
    by_row = lane < HEAD // 2
    low = (lane < HEAD // 4) | ((lane >= HEAD // 2) & (lane < 3 * HEAD // 4))

    padded = cos_ref.shape[2]
    copies = padded // HEAD

    def tables(p):
        def image(j, carry):
            start, begin, columns = carry
            inside = where >= start
            begin = jnp.where(inside, start, begin)
            columns = jnp.where(inside, widths_ref[packs[p], j], columns)
            return start + blocks_ref[packs[p], j] * BLOCK, begin, columns

        zero = jnp.zeros((size, HEAD), jnp.int32)
        _, begin, columns = lax.fori_loop(0, blocks_ref.shape[1], image, (jnp.int32(0), zero, zero + 1))
        offset = (where - begin).astype(jnp.float32)
        columns = columns.astype(jnp.float32)
        row = jnp.floor((offset + 0.5) / columns)
        col = offset - row * columns
        angle = jnp.where(by_row, row, col) * freq_ref[...]
        cos_ref[p] = jnp.concatenate([jnp.cos(angle)] * copies, axis=1)
        sine = jnp.sin(angle)
        sin_ref[p] = jnp.concatenate([jnp.where(low, -sine, sine)] * copies, axis=1)

    tables(0)
    tables(1)

    @pl.when(jnp.logical_not(home))
    def _():
        slot = slot_of(a)
        remote(spot(slot, 0), spot(slot, 0), pass_send.at[0], w_recv.at[slot, 0], mate, other).wait_recv()
        spread(a, 0, True, True)

    hop(1, 0)

    blank = jnp.zeros((HALO, 2 * width), jnp.bfloat16)

    @pl.when(jnp.logical_not(has_down))
    def _():
        for win in wins:
            win[:HALO] = blank

    @pl.when(jnp.logical_not(has_up))
    def _():
        for win in wins:
            win[HALO + size:] = blank

    begin_ring(1)
    hop(2, 0)
    along_x(1).wait_recv()
    relay_y().start()
    hop(1, 1)
    along_y(0).wait_recv()
    relay_x().start()
    for d in range(3, planes):
        hop(d, 0)
        hop(d - 1, 1)
    from_mate(0)

    @pl.when(home)
    def _():
        keep_own(0).wait()
        keep_own(1).wait()

    wkv = lambda: wkv_ref[...].reshape(-1, wide)
    wq = lambda: wq_ref[...].reshape(-1, wq_ref.shape[2])

    def turn_heads(raw, gain, at, p):
        along = lax.broadcasted_iota(jnp.int32, raw.shape, 1)
        head = along // HEAD
        first_part = along % (HEAD // 2) < HEAD // 4
        square = raw * raw
        factor = jnp.zeros_like(raw)
        for h in range(heads):
            mean = jnp.sum(jnp.where(head == h, square, 0.0), axis=-1, keepdims=True) * (1.0 / HEAD)
            factor = jnp.where(head == h, lax.rsqrt(mean + eps_model), factor)
        n = raw * factor * jnp.concatenate([gain] * copies, axis=1)
        swapped = jnp.where(first_part, pltpu.roll(n, padded - HEAD // 4, 1), pltpu.roll(n, HEAD // 4, 1))
        return (n * cos_ref[p, at] + swapped * sin_ref[p, at]).astype(jnp.bfloat16)[:, :width]

    def make_keys(p, mine, first, length):
        pos = b if mine else 1 - b
        at = pl.ds(pl.multiple_of(pos * rows + first, 16), length)
        raw = jnp.dot(shard_rows(p, mine, first, length), wkv(), preferred_element_type=jnp.float32)
        done = jnp.concatenate([turn_heads(raw[:, :padded], kg_ref[...], at, p),
                                raw[:, width:2 * width].astype(jnp.bfloat16)], axis=1)
        wins[p][pl.ds(pl.multiple_of(HALO + pos * rows + first, 16), length)] = done
        lead_ref[p, at] = raw[:, 2 * width:]

    def make_queries(p, mine, first, length):
        pos = b if mine else 1 - b
        at = pl.ds(pl.multiple_of(pos * rows + first, 16), length)
        raw = jnp.dot(shard_rows(p, mine, first, length), wq(), preferred_element_type=jnp.float32)
        raw = jnp.concatenate(
            [lead_ref[p, at], raw[:, :width - extra], jnp.zeros((length, padded - width), jnp.float32)], axis=1)
        q_ref[p, at] = turn_heads(raw, qg_ref[...], at, p)

    def upward(p, k):
        return remote(wins[p].at[pl.ds(size + k * BLOCK, BLOCK)], wins[p].at[pl.ds(k * BLOCK, BLOCK)],
                      halo_send.at[p, 0, k], halo_recv.at[p, 0, k], f, s + 2)

    def downward(p, k):
        return remote(wins[p].at[pl.ds(HALO + k * BLOCK, BLOCK)], wins[p].at[pl.ds(HALO + size + k * BLOCK, BLOCK)],
                      halo_send.at[p, 1, k], halo_recv.at[p, 1, k], f, s - 2)

    per = rows // BLOCK
    reach = HALO // BLOCK
    total = size // BLOCK

    def send_block(p, i):
        if i >= total - reach:
            @pl.when(has_up)
            def _():
                upward(p, i - (total - reach)).start()
        if i < reach:
            @pl.when(has_down)
            def _():
                downward(p, i).start()

    def send_shard(p, pos):
        for q in range(2):
            @pl.when(pos == q)
            def _():
                for k in range(per):
                    send_block(p, q * per + k)

    make_keys(0, True, 0, rows)
    send_shard(0, b)
    hop(planes - 1, 1)
    along_y(1).wait_recv()
    make_keys(0, False, 0, rows)
    send_shard(0, 1 - b)
    along_x(0).wait_recv()
    make_keys(1, True, 0, rows)
    send_shard(1, b)
    from_mate(1)
    make_queries(0, True, 0, rows)
    make_queries(0, False, 0, rows)
    make_queries(1, True, 0, rows)

    scale = HEAD ** (-0.5) * 1.4426950408889634

    def attend_block(p, pos, k):
        i = pos * per + k
        first = pl.multiple_of(i * BLOCK, BLOCK)
        where_q = a * size + i * BLOCK

        def image(j, state):
            start, begin, length = state
            inside = where_q >= start
            blocks = blocks_ref[packs[p], j] * BLOCK
            return start + blocks, jnp.where(inside, start, begin), jnp.where(inside, blocks, length)

        _, begin, length = lax.fori_loop(0, blocks_ref.shape[1], image, (jnp.int32(0), jnp.int32(0), jnp.int32(0)))
        back = where_q - begin
        chosen = wins[p][pl.ds(pl.multiple_of(first + HALO, BLOCK), span)]
        for shift in range(BLOCK, HALO + 1, BLOCK):
            earlier = wins[p][pl.ds(pl.multiple_of(first + HALO - shift, BLOCK), span)]
            chosen = jnp.where(back == shift, earlier, chosen)
        mask = lax.broadcasted_iota(jnp.int32, (span, BLOCK), 0) < length
        queries = q_ref[p, pl.ds(first, BLOCK)]
        outs = []
        for h in range(heads):
            keys = chosen[:, h * HEAD:(h + 1) * HEAD]
            vals = chosen[:, width + h * HEAD:width + (h + 1) * HEAD]
            scores = lax.dot_general(keys, queries[:, h * HEAD:(h + 1) * HEAD], (((1,), (1,)), ((), ())),
                                     preferred_element_type=jnp.float32)
            scores = jnp.where(mask, scores, -1e30)
            top = jnp.max(scores, axis=0, keepdims=True)
            expo = jnp.exp2((scores - top) * scale)
            norm = jnp.sum(expo, axis=0, keepdims=True)
            probs = (expo * (1.0 / norm)).astype(jnp.bfloat16)
            outs.append(lax.dot_general(vals, probs, (((0,), (0,)), ((), ())),
                                        preferred_element_type=jnp.float32).astype(jnp.bfloat16))
        mixed[p, pos, k] = jnp.concatenate(outs, axis=0)

    def deliver(p, k, blk):
        pos, seat = (1 - b, other) if k == 0 else (b, s)
        owner = f if p == 0 else beside
        way = 0 if p == 0 else 2 - k
        return remote(mixed.at[p, pos, blk], (land_y, land_x, land_d)[way].at[blk],
                      out_send.at[way, blk], out_recv.at[way, blk], owner, seat)

    def attend(p, k):
        pos = 1 - b if k == 0 else b
        for i in range(per):
            attend_block(p, pos, i)
            if p == 1 or k == 0:
                deliver(p, k, i).start()

    def place_group(group, blocks):
        for g in range(4):
            @pl.when(group == g)
            def _():
                for i in range(per):
                    o_ref[0, i * BLOCK:(i + 1) * BLOCK, g * width:(g + 1) * width] = blocks(i).T

    def halo_wait(p):
        @pl.when(has_down)
        def _():
            for k in range(reach):
                upward(p, k).wait_recv()

        @pl.when(has_up)
        def _():
            for k in range(reach):
                downward(p, k).wait_recv()

    relay_x().wait_recv()
    relay_y().wait_recv()
    make_keys(1, False, 0, rows)
    send_shard(1, 1 - b)
    halo_wait(0)
    attend(0, 0)
    attend(0, 1)
    make_queries(1, False, 0, rows)
    place_group(2 * x + b, lambda i: mixed[0, b, i])
    for i in range(per):
        deliver(0, 0, i).wait_recv()
    place_group(2 * x + 1 - b, lambda i: land_y[i])
    halo_wait(1)
    attend(1, 0)
    attend(1, 1)

    def drain(plane, carry):
        for kind in range(2):
            @pl.when((plane <= a) & has_up)
            def _():
                push(plane, kind, 0).wait_send()

            @pl.when((plane >= a) & has_down)
            def _():
                push(plane, kind, 1).wait_send()

            push(plane, kind, 2).wait_send()
        return carry

    lax.fori_loop(0, planes, drain, 0)

    @pl.when(jnp.logical_not(home))
    def _():
        pass_over(0).wait_send()
        pass_over(1).wait_send()

    for k in range(2):
        along_x(k).wait_send()
        along_y(k).wait_send()
    relay_x().wait_send()
    relay_y().wait_send()
    for p in range(2):
        for k in range(reach):
            @pl.when(has_up)
            def _():
                upward(p, k).wait_send()

            @pl.when(has_down)
            def _():
                downward(p, k).wait_send()

    for i in range(per):
        deliver(1, 1, i).wait_recv()
    place_group(2 * (1 - x) + b, lambda i: land_x[i])
    for i in range(per):
        deliver(1, 0, i).wait_recv()
    place_group(2 * (1 - x) + 1 - b, lambda i: land_d[i])
    for i in range(per):
        deliver(0, 0, i).wait_send()
        deliver(1, 0, i).wait_send()
        deliver(1, 1, i).wait_send()


def fused(planes, tokens, norm_gain, w_qkv, q_gain, k_gain, img_blocks, img_width):
    row_count, model = tokens.shape[1], tokens.shape[2]
    depth, width = w_qkv.shape[1], w_qkv.shape[2]
    size = 2 * row_count
    wide = pl.cdiv(2 * width, 128) * 128
    tail = pl.cdiv(3 * width - wide, 128) * 128
    quarter = HEAD // 4
    freq = np.tile(np.float32(10000.0) ** (-np.arange(quarter, dtype=np.float32) / np.float32(quarter)), 4)[None]
    vmem = pl.BlockSpec(memory_space=pltpu.VMEM)
    smem = pl.BlockSpec(memory_space=pltpu.SMEM)
    anywhere = pl.BlockSpec(memory_space=pl.ANY)
    dma = pltpu.SemaphoreType.DMA
    return pl.pallas_call(
        functools.partial(fused_kernel, planes),
        out_shape=jax.ShapeDtypeStruct((1, row_count, 4 * width), jnp.bfloat16),
        in_specs=[anywhere] * 6 + [smem] * 2,
        out_specs=vmem,
        scratch_shapes=[
            pltpu.VMEM(tokens.shape, jnp.bfloat16),
            pltpu.VMEM(norm_gain.shape, jnp.float32),
            pltpu.VMEM(w_qkv.shape, jnp.bfloat16),
            pltpu.VMEM((1, HEAD), jnp.float32),
            pltpu.VMEM((1, HEAD), jnp.float32),
            pltpu.VMEM((1, HEAD), jnp.float32),
            dma((6,)),
            pltpu.VMEM((row_count, model), jnp.bfloat16),
            pltpu.VMEM((row_count, model), jnp.bfloat16),
            pltpu.VMEM((row_count, model), jnp.bfloat16),
            pltpu.VMEM((row_count, model), jnp.bfloat16),
            pltpu.VMEM((2 * planes, depth, wide), jnp.bfloat16),
            pltpu.VMEM((2 * planes, depth, tail), jnp.bfloat16),
            pltpu.VMEM((depth, wide), jnp.bfloat16),
            pltpu.VMEM((depth, tail), jnp.bfloat16),
            pltpu.VMEM((2, size, pl.cdiv(width, 128) * 128), jnp.float32),
            pltpu.VMEM((2, size, pl.cdiv(width, 128) * 128), jnp.float32),
            pltpu.VMEM((2, size, width), jnp.bfloat16),
            pltpu.VMEM((2, size, wide - 2 * width), jnp.float32),
            pltpu.VMEM((size + 2 * HALO, 2 * width), jnp.bfloat16),
            pltpu.VMEM((size + 2 * HALO, 2 * width), jnp.bfloat16),
            pltpu.VMEM((2, 2, row_count // BLOCK, width, BLOCK), jnp.bfloat16),
            pltpu.VMEM((row_count // BLOCK, width, BLOCK), jnp.bfloat16),
            pltpu.VMEM((row_count // BLOCK, width, BLOCK), jnp.bfloat16),
            pltpu.VMEM((row_count // BLOCK, width, BLOCK), jnp.bfloat16),
            dma((3, 2)),
            dma((3, 2)),
            dma((planes, 2, 3)),
            dma((2 * planes, 2)),
            dma((2,)),
            dma((2, 2, HALO // BLOCK)),
            dma((2, 2, HALO // BLOCK)),
            dma((3, row_count // BLOCK)),
            dma((3, row_count // BLOCK)),
            dma((3,)),
        ],
        compiler_params=pltpu.CompilerParams(
            collective_id=0, has_side_effects=True, vmem_limit_bytes=60 * 1024 * 1024),
        name="fused",
    )(tokens, norm_gain, w_qkv, q_gain[None], k_gain[None], jnp.asarray(freq), img_blocks, img_width)


def shards(planes, tokens, norm_gain, w_qkv, q_gain, k_gain, img_blocks, img_width):
    row_count, model = tokens.shape[1], tokens.shape[2]
    width = w_qkv.shape[2]
    size = 2 * row_count
    seqs = 2 * planes
    depth = w_qkv.shape[1]
    broad = pl.cdiv(3 * width, 128) * 128
    quarter = HEAD // 4
    freq = np.tile(np.float32(10000.0) ** (-np.arange(quarter, dtype=np.float32) / np.float32(quarter)), 4)[None]
    vmem = pl.BlockSpec(memory_space=pltpu.VMEM)
    smem = pl.BlockSpec(memory_space=pltpu.SMEM)
    anywhere = pl.BlockSpec(memory_space=pl.ANY)
    table = jax.ShapeDtypeStruct((2, size, HEAD), jnp.float32)
    gathered, weights, cosine, sine = pl.pallas_call(
        functools.partial(gather_kernel, planes),
        out_shape=(
            jax.ShapeDtypeStruct((2, 2, row_count, model), jnp.bfloat16),
            jax.ShapeDtypeStruct((seqs, depth, broad), jnp.bfloat16),
            table,
            table,
        ),
        in_specs=[vmem, vmem, vmem, smem, smem, vmem],
        out_specs=(anywhere, anywhere, vmem, vmem),
        scratch_shapes=[
            pltpu.VMEM((row_count, model), jnp.bfloat16),
            pltpu.VMEM((depth, broad), jnp.bfloat16),
            pltpu.SemaphoreType.DMA((7,)),
            pltpu.SemaphoreType.DMA((7,)),
            pltpu.SemaphoreType.DMA((seqs, 3)),
            pltpu.SemaphoreType.DMA((seqs,)),
            pltpu.SemaphoreType.DMA((2,)),
        ],
        compiler_params=pltpu.CompilerParams(collective_id=0, has_side_effects=True),
        name="gather",
    )(tokens, norm_gain, w_qkv, img_blocks, img_width, jnp.asarray(freq))
    attended = pl.pallas_call(
        functools.partial(attend_kernel, planes),
        out_shape=jax.ShapeDtypeStruct((1, row_count, 4 * width), jnp.bfloat16),
        in_specs=[anywhere, anywhere, vmem, vmem, vmem, vmem, smem],
        out_specs=vmem,
        scratch_shapes=[
            pltpu.VMEM((2, size, model), jnp.bfloat16),
            pltpu.VMEM((model, broad), jnp.bfloat16),
            pltpu.VMEM((2, size, width), jnp.bfloat16),
            pltpu.VMEM((size + 2 * HALO, 2 * width), jnp.bfloat16),
            pltpu.VMEM((size + 2 * HALO, 2 * width), jnp.bfloat16),
            pltpu.VMEM((2, size, width), jnp.bfloat16),
            pltpu.VMEM((4, row_count, width), jnp.bfloat16),
            pltpu.SemaphoreType.DMA((2, 2)),
            pltpu.SemaphoreType.DMA((2, 2)),
            pltpu.SemaphoreType.DMA((2, 2)),
            pltpu.SemaphoreType.DMA((4,)),
            pltpu.SemaphoreType.DMA((3,)),
            pltpu.SemaphoreType.DMA((3,)),
        ],
        compiler_params=pltpu.CompilerParams(collective_id=1, has_side_effects=True),
        name="attend",
    )(gathered.reshape(2, size, model), weights.reshape(model, broad), cosine, sine,
      q_gain[None], k_gain[None], img_blocks)
    return attended


def solution(mesh):
    assert mesh.shape["fsdp"] == 4 and mesh.shape["seq"] % 2 == 0
    planes = mesh.shape["seq"] // 2

    def body(tokens, norm_gain, w_qkv, *rest):
        whole_tiles = w_qkv.shape[1] % 16 == 0 and 2 * w_qkv.shape[2] % 128 != 0 and -w_qkv.shape[2] % 128 == HEAD
        return (fused if whole_tiles else shards)(planes, tokens, norm_gain, w_qkv, *rest)

    return jax.shard_map(
        body,
        mesh=mesh,
        in_specs=(P("fsdp", "seq", None), P(), P(None, "seq", "fsdp"), P(), P(), P(), P()),
        out_specs=P("fsdp", "seq", None),
        check_vma=False,
    )
```

```python
import functools

import jax
import jax.numpy as jnp
import numpy as np
from jax import lax
from jax.experimental import pallas as pl
from jax.experimental.pallas import tpu as pltpu
from jax.sharding import PartitionSpec as P

HEAD = 96
BLOCK = 128
HALO = 3 * BLOCK
MESH = pl.DeviceIdType.MESH

eps_model = 1e-06


def rms_norm(values, gain):
    return values * lax.rsqrt(jnp.mean(values * values, axis=-1, keepdims=True) + eps_model) * gain


def place():
    f = lax.axis_index("fsdp")
    s = lax.axis_index("seq")
    return f // 2, f % 2, s // 2, s % 2, f, s


def remote(src, dst, send, recv, f, s):
    return pltpu.make_async_remote_copy(
        src_ref=src, dst_ref=dst, send_sem=send, recv_sem=recv,
        device_id={"fsdp": f, "seq": s}, device_id_type=MESH,
    )


def signal(sem, f, s):
    pl.semaphore_signal(sem, inc=1, device_id={"fsdp": f, "seq": s}, device_id_type=MESH)


def gather_kernel(planes, raw_ref, gain_ref, parts_ref, blocks_ref, widths_ref, freq_ref,
                  t_ref, wall_ref, cos_ref, sin_ref,
                  tok_ref, w_ref, tok_send, tok_recv, w_send, w_recv, local_sem):
    x, c, a, b, f, s = place()
    rows = tok_ref.shape[0]
    half = rows // 2
    other = s + 1 - 2 * b
    home = c == b
    barrier = pltpu.get_barrier_semaphore()
    signal(barrier, 2 * x + 1 - c, s)
    for core in range(2):
        signal(barrier, 2 * (1 - x) + core, s)
        signal(barrier, 2 * x + core, other)

    @pl.when(a > 0)
    def _():
        signal(barrier, f, s - 2)

    @pl.when(a < planes - 1)
    def _():
        signal(barrier, f, s + 2)

    step = 32

    @pl.loop(0, rows // step)
    def _(i):
        at = pl.ds(pl.multiple_of(i * step, step), step)
        tok_ref[at] = rms_norm(raw_ref[0, at].astype(jnp.float32), gain_ref[...][None]).astype(jnp.bfloat16)

    spare = jnp.zeros((w_ref.shape[0], w_ref.shape[1] - 3 * parts_ref.shape[2]), jnp.bfloat16)
    w_ref[...] = jnp.concatenate([parts_ref[1], parts_ref[2], parts_ref[0], spare], axis=1)
    pl.semaphore_wait(barrier, 5 + (a > 0).astype(jnp.int32) + (a < planes - 1).astype(jnp.int32))

    def part(xx, yy, h):
        return t_ref.at[xx, yy, pl.ds(pl.multiple_of(h * half, half), half)]

    keep = pltpu.make_async_copy(tok_ref, t_ref.at[x, b], local_sem.at[0])
    whole = remote(tok_ref, t_ref.at[x, b], tok_send.at[0], tok_recv.at[6], 2 * x + 1 - c, s)
    along = [remote(tok_ref.at[pl.ds(h * half, half)], part(x, b, h), tok_send.at[1 + h], tok_recv.at[1],
                    2 * (1 - x) + h, s) for h in range(2)]
    across = [remote(tok_ref.at[pl.ds(h * half, half)], part(x, b, h), tok_send.at[1 + h], tok_recv.at[0],
                     2 * x + h, other) for h in range(2)]

    @pl.when(home)
    def _():
        for copy in along:
            copy.start()
        whole.start()
        keep.start()

    @pl.when(jnp.logical_not(home))
    def _():
        for copy in across:
            copy.start()

    keep_w = pltpu.make_async_copy(w_ref, wall_ref.at[s], local_sem.at[1])
    keep_w.start()

    def push(src, slot, way):
        target = (s + 2, s - 2, other)[way]
        return remote(src, wall_ref.at[slot], w_send.at[slot, way], w_recv.at[slot], f, target)

    def spread(src, slot, up, down):
        if up:
            @pl.when(a < planes - 1)
            def _():
                push(src, slot, 0).start()
        if down:
            @pl.when(a > 0)
            def _():
                push(src, slot, 1).start()

        @pl.when(crosses(slot // 2))
        def _():
            push(src, slot, 2).start()

    middle = planes // 2
    bottom, top = 1 - b, 2 * (planes - 1) + 1 - b
    lifts = jnp.logical_not(home) & (a >= middle - 1) & (a < planes - 1)
    drops = jnp.logical_not(home) & (a <= middle) & (a > 0)

    def crosses(k):
        skipped = ((k == 0) & (a >= middle)) | ((k == planes - 1) & (a < middle))
        return jnp.logical_not(home & skipped)

    spread(w_ref, s, True, True)

    size = cos_ref.shape[1]
    lane = lax.broadcasted_iota(jnp.int32, (size, HEAD), 1)
    where = a * size + lax.broadcasted_iota(jnp.int32, (size, HEAD), 0)
    by_row = lane < HEAD // 2
    low = (lane < HEAD // 4) | ((lane >= HEAD // 2) & (lane < 3 * HEAD // 4))
    for px in range(2):
        pack = 2 * px + b

        def image(j, carry):
            start, begin, wide = carry
            inside = where >= start
            begin = jnp.where(inside, start, begin)
            wide = jnp.where(inside, widths_ref[pack, j], wide)
            return start + blocks_ref[pack, j] * BLOCK, begin, wide

        zero = jnp.zeros((size, HEAD), jnp.int32)
        _, begin, wide = lax.fori_loop(0, blocks_ref.shape[1], image, (jnp.int32(0), zero, zero + 1))
        offset = (where - begin).astype(jnp.float32)
        wide = wide.astype(jnp.float32)
        row = jnp.floor((offset + 0.5) / wide)
        col = offset - row * wide
        angle = jnp.where(by_row, row, col) * freq_ref[...]
        cos_ref[px] = jnp.cos(angle)
        sine = jnp.sin(angle)
        sin_ref[px] = jnp.where(low, -sine, sine)

    mine = [(x, 1 - b), (1 - x, b), (1 - x, 1 - b)]

    def share(k):
        spot = part(mine[k][0], mine[k][1], c)
        return remote(spot, spot, tok_send.at[3 + k], tok_recv.at[3 + k], 2 * x + 1 - c, s)

    def landed(k):
        spot = part(mine[k][0], mine[k][1], c)
        return remote(spot, spot, tok_send.at[3 + k], tok_recv.at[k], 2 * x + 1 - c, s)

    spot = part(x, 1 - b, c)
    relay = remote(spot, spot, tok_send.at[6], tok_recv.at[2], 2 * (1 - x) + c, s)
    def hop(d, carry):
        lower = a - d
        upper = a + d

        @pl.when(lower >= 0)
        def _():
            slot = jnp.maximum(2 * lower + b, 0)
            push(wall_ref.at[slot], slot, 0).wait_recv()
            spread(wall_ref.at[slot], slot, True, False)

        @pl.when(upper < planes)
        def _():
            slot = jnp.minimum(2 * upper + b, 2 * planes - 1)
            push(wall_ref.at[slot], slot, 1).wait_recv()
            spread(wall_ref.at[slot], slot, False, True)

        return carry

    lax.fori_loop(1, 2, hop, 0)
    landed(0).wait_recv()
    relay.start()
    share(0).start()
    lax.fori_loop(2, 3, hop, 0)

    @pl.when(lifts)
    def _():
        push(wall_ref.at[bottom], bottom, 0).wait_recv()
        push(wall_ref.at[bottom], bottom, 0).start()

    @pl.when(drops)
    def _():
        push(wall_ref.at[top], top, 1).wait_recv()
        push(wall_ref.at[top], top, 1).start()

    lax.fori_loop(3, planes, hop, 0)
    landed(1).wait_recv()
    share(1).start()
    landed(2).wait_recv()
    share(2).start()

    def finish(k, carry):
        slot = 2 * k + 1 - b
        early = ((k == 0) & lifts) | ((k == planes - 1) & drops)

        @pl.when(jnp.logical_not(early))
        def _():
            push(wall_ref.at[slot], slot, 2).wait_recv()

        sent = 2 * k + b

        @pl.when(crosses(k))
        def _():
            push(wall_ref.at[sent], sent, 2).wait_send()

        @pl.when((k <= a) & (a < planes - 1))
        def _():
            push(wall_ref.at[sent], sent, 0).wait_send()

        @pl.when((k >= a) & (a > 0))
        def _():
            push(wall_ref.at[sent], sent, 1).wait_send()

        return carry

    lax.fori_loop(0, planes, finish, 0)

    @pl.when(lifts)
    def _():
        push(wall_ref.at[bottom], bottom, 0).wait_send()

    @pl.when(drops)
    def _():
        push(wall_ref.at[top], top, 1).wait_send()

    keep_w.wait()

    @pl.when(home)
    def _():
        for copy in along:
            copy.wait_send()
        whole.wait_send()
        keep.wait()

    @pl.when(jnp.logical_not(home))
    def _():
        for copy in across:
            copy.wait_send()
        whole.wait_recv()

    relay.wait_send()
    for k in range(3):
        share(k).wait_send()
        spot = part(mine[k][0], mine[k][1], 1 - c)
        remote(spot, spot, tok_send.at[3 + k], tok_recv.at[3 + k], 2 * x + 1 - c, s).wait_recv()


def turn(raw, gain, cosine, sine):
    parts = HEAD // 4
    n = rms_norm(raw, gain)
    swapped = jnp.concatenate(
        [n[:, parts:2 * parts], n[:, :parts], n[:, 3 * parts:], n[:, 2 * parts:3 * parts]], axis=1)
    return (n * cosine + swapped * sine).astype(jnp.bfloat16)


def attend_kernel(planes, t_ref, wall_ref, cos_ref, sin_ref, qg_ref, kg_ref, blocks_ref, o_ref,
                  x_ref, w_ref, q_ref, low_win, high_win, mixed, landed, halo_send, halo_recv, out_send, out_recv,
                  local_sem, load_sem):
    x, c, a, b, f, s = place()
    size, width = q_ref.shape[1], q_ref.shape[2]
    rows = size // 2
    inner = size - HALO
    span = HALO + BLOCK
    wins = (low_win, high_win)
    home = c == b
    load_w = pltpu.make_async_copy(wall_ref, w_ref, load_sem.at[2])
    loads = [pltpu.make_async_copy(t_ref.at[p], x_ref.at[p], load_sem.at[p]) for p in range(2)]
    load_w.start()
    for load in loads:
        load.start()
    barrier = pltpu.get_barrier_semaphore()
    has_down, has_up = a > 0, a < planes - 1
    for core in range(4):
        @pl.when(jnp.logical_or(b != c, f != core))
        def _():
            signal(barrier, core, 2 * a + c)

    @pl.when(has_down)
    def _():
        signal(barrier, f, s - 2)

    @pl.when(has_up)
    def _():
        signal(barrier, f, s + 2)

    count = 4 - home.astype(jnp.int32) + has_down.astype(jnp.int32) + has_up.astype(jnp.int32)
    pl.semaphore_wait(barrier, count)

    def upward(p):
        return remote(wins[p].at[pl.ds(HALO + inner, HALO)], wins[p].at[pl.ds(0, HALO)],
                      halo_send.at[p, 0], halo_recv.at[p, 0], f, s + 2)

    def downward(p):
        return remote(wins[p].at[pl.ds(HALO, HALO)], wins[p].at[pl.ds(HALO + size, HALO)],
                      halo_send.at[p, 1], halo_recv.at[p, 1], f, s - 2)

    blank = jnp.zeros((HALO, 2 * width), jnp.bfloat16)

    @pl.when(jnp.logical_not(has_down))
    def _():
        for win in wins:
            win[:HALO] = blank

    @pl.when(jnp.logical_not(has_up))
    def _():
        for win in wins:
            win[HALO + size:] = blank

    heads = width // HEAD
    shift_q = 2 * width // 128 * 128

    def make_keys(p, i):
        first = i * rows
        at = slice(first, first + rows)
        raw = jnp.dot(x_ref[p, at], w_ref[:, :pl.cdiv(2 * width, 128) * 128], preferred_element_type=jnp.float32)
        keys = [turn(raw[:, h * HEAD:(h + 1) * HEAD], kg_ref[...], cos_ref[p, at], sin_ref[p, at])
                for h in range(heads)]
        done = jnp.concatenate(keys + [raw[:, width:2 * width].astype(jnp.bfloat16)], axis=1)
        wins[p][HALO + first:HALO + first + rows] = done

    def make_queries(p, i):
        at = slice(i * rows, (i + 1) * rows)
        raw = jnp.dot(x_ref[p, at], w_ref[:, shift_q:], preferred_element_type=jnp.float32)
        raw = raw[:, 2 * width - shift_q:]
        q_ref[p, at] = jnp.concatenate(
            [turn(raw[:, h * HEAD:(h + 1) * HEAD], qg_ref[...], cos_ref[p, at], sin_ref[p, at])
             for h in range(heads)], axis=1)

    load_w.wait()
    for load in loads:
        load.wait()
    for p in range(2):
        for i in range(2):
            make_keys(p, i)

        make_queries(p, 0)

        @pl.when(has_up)
        def _():
            upward(p).start()

        @pl.when(has_down)
        def _():
            downward(p).start()

    for p in range(2):
        make_queries(p, 1)

    scale = HEAD ** (-0.5) * 1.4426950408889634

    def deliver(p, yy):
        return remote(mixed.at[p, pl.ds(yy * rows, rows)], landed.at[f],
                      out_send.at[p, yy], out_recv.at[f], 2 * p + b, 2 * a + yy)

    def to_self(p, yy):
        return pltpu.make_async_copy(mixed.at[p, pl.ds(yy * rows, rows)], landed.at[f], local_sem.at[2])

    def is_self(p, yy):
        return home & (p == x) & (yy == b)

    for p in range(2):
        pack = 2 * p + b

        @pl.when(has_down)
        def _():
            upward(p).wait_recv()

        @pl.when(has_up)
        def _():
            downward(p).wait_recv()

        def block(i, carry):
            first = pl.multiple_of(i * BLOCK, BLOCK)
            where_q = a * size + i * BLOCK

            def image(j, state):
                start, begin, length = state
                inside = where_q >= start
                blocks = blocks_ref[pack, j] * BLOCK
                return start + blocks, jnp.where(inside, start, begin), jnp.where(inside, blocks, length)

            _, begin, length = lax.fori_loop(0, blocks_ref.shape[1], image,
                                             (jnp.int32(0), jnp.int32(0), jnp.int32(0)))
            back = where_q - begin
            chosen = wins[p][pl.ds(pl.multiple_of(first + HALO, BLOCK), span)]
            for shift in range(BLOCK, HALO + 1, BLOCK):
                earlier = wins[p][pl.ds(pl.multiple_of(first + HALO - shift, BLOCK), span)]
                chosen = jnp.where(back == shift, earlier, chosen)
            mask = lax.broadcasted_iota(jnp.int32, (BLOCK, span), 1) < length
            queries = q_ref[p, pl.ds(first, BLOCK)]
            outs = []
            for h in range(width // HEAD):
                keys = chosen[:, h * HEAD:(h + 1) * HEAD]
                vals = chosen[:, width + h * HEAD:width + (h + 1) * HEAD]
                scores = lax.dot_general(queries[:, h * HEAD:(h + 1) * HEAD], keys, (((1,), (1,)), ((), ())),
                                         preferred_element_type=jnp.float32)
                scores = jnp.where(mask, scores, -1e30)
                top = jnp.max(scores, axis=-1, keepdims=True)
                expo = jnp.exp2((scores - top) * scale)
                norm = jnp.sum(expo, axis=-1, keepdims=True)
                probs = (expo * (1.0 / norm)).astype(jnp.bfloat16)
                outs.append(jnp.dot(probs, vals, preferred_element_type=jnp.float32).astype(jnp.bfloat16))
            mixed[p, pl.ds(first, BLOCK)] = jnp.concatenate(outs, axis=1)
            return carry

        lax.fori_loop(0, size // BLOCK, block, 0)
        for yy in range(2):
            @pl.when(is_self(p, yy))
            def _():
                to_self(p, yy).start()

            @pl.when(jnp.logical_not(is_self(p, yy)))
            def _():
                deliver(p, yy).start()

    for p in range(2):
        for yy in range(2):
            @pl.when(is_self(p, yy))
            def _():
                to_self(p, yy).wait()

            @pl.when(jnp.logical_not(is_self(p, yy)))
            def _():
                deliver(p, yy).wait_send()

        @pl.when(has_up)
        def _():
            upward(p).wait_send()

        @pl.when(has_down)
        def _():
            downward(p).wait_send()

    for core in range(4):
        @pl.when(jnp.logical_or(b != c, f != core))
        def _():
            remote(mixed.at[0, pl.ds(0, rows)], landed.at[core], out_send.at[0, 0], out_recv.at[core], f, s).wait_recv()

    o_ref[0] = jnp.concatenate([landed[core] for core in range(4)], axis=1)


def fused_kernel(planes, raw_in, gain_in, parts_in, qg_in, kg_in, freq_in, blocks_ref, widths_ref, o_ref,
                 raw_ref, gain_ref, parts_ref, qg_ref, kg_ref, freq_ref, load_sem, own_ref, xa_ref, xb_ref, xd_ref, wkv_ref, wq_ref, okv_ref, oq_ref, cos_ref, sin_ref, q_ref, lead_ref, win_a, win_b, mixed,
                 land_y, land_x, land_d, tok_send, tok_recv, w_send, w_recv, pass_send, halo_send, halo_recv, out_send, out_recv,
                 local_sem):
    x, c, a, b, f, s = place()
    loads = [pltpu.make_async_copy(src, dst, load_sem.at[i]) for i, (src, dst) in enumerate((
        (parts_in, parts_ref), (raw_in, raw_ref), (gain_in, gain_ref), (qg_in, qg_ref), (kg_in, kg_ref),
        (freq_in, freq_ref)))]
    for load in loads:
        load.start()
    rows = raw_ref.shape[1]
    depth, width = parts_ref.shape[1], parts_ref.shape[2]
    size = 2 * rows
    heads = width // HEAD
    wide = wkv_ref.shape[2]
    extra = wide - 2 * width
    wins = (win_a, win_b)
    span = HALO + BLOCK
    home = c == b
    has_down, has_up = a > 0, a < planes - 1
    mate = 2 * x + 1 - c
    beside = 2 * (1 - x) + c
    other = s + 1 - 2 * b
    packs = (2 * x + c, 2 * (1 - x) + c)
    cut = rows * 6 // 8 // 32 * 32

    barrier = pltpu.get_barrier_semaphore()
    signal(barrier, mate, s)
    signal(barrier, beside, s)
    signal(barrier, f, other)
    signal(barrier, beside, other)

    @pl.when(jnp.logical_not(home))
    def _():
        signal(barrier, mate, other)

    @pl.when(has_down)
    def _():
        signal(barrier, f, s - 2)

    @pl.when(has_up)
    def _():
        signal(barrier, f, s + 2)

    loads[0].wait()
    okv_ref[...] = jnp.concatenate([parts_ref[1], parts_ref[2], parts_ref[0, :, :extra]], axis=1)
    oq_ref[...] = jnp.concatenate(
        [parts_ref[0, :, extra:], jnp.zeros((depth, oq_ref.shape[1] - width + extra), jnp.bfloat16)], axis=1)
    for load in loads[1:]:
        load.wait()
    step = 32

    def normalize(i, carry):
        at = pl.ds(pl.multiple_of(i * step, step), step)
        own_ref[at] = rms_norm(raw_ref[0, at].astype(jnp.float32), gain_ref[...][None]).astype(jnp.bfloat16)
        return carry

    lax.fori_loop(cut // step, rows // step, normalize, 0)
    count = 4 + jnp.logical_not(home).astype(jnp.int32) + has_down.astype(jnp.int32) + has_up.astype(jnp.int32)
    pl.semaphore_wait(barrier, count)


    def slot_of(plane):
        return 2 * plane + c

    def spot(slot, kind):
        return (wkv_ref, wq_ref)[kind].at[slot]

    def push(plane, kind, way, src=None):
        slot = slot_of(plane)
        target = ((f, s + 2), (f, s - 2), (mate, s))[way]
        return remote(spot(slot, kind) if src is None else src, spot(slot, kind), w_send.at[plane, kind, way], w_recv.at[slot, kind], *target)

    def pass_over(kind):
        return remote((okv_ref, oq_ref)[kind], spot(s, kind), pass_send.at[kind], w_recv.at[s, kind], mate, other)

    def spread(plane, kind, up, down, src=None):
        if up:
            @pl.when(has_up)
            def _():
                push(plane, kind, 0, src).start()
        if down:
            @pl.when(has_down)
            def _():
                push(plane, kind, 1, src).start()
        push(plane, kind, 2, src).start()

    def keep_own(kind):
        return pltpu.make_async_copy((okv_ref, oq_ref)[kind], spot(s, kind), local_sem.at[1 + kind])

    def begin_ring(kind):
        @pl.when(home)
        def _():
            spread(a, kind, True, True, (okv_ref, oq_ref)[kind])
            keep_own(kind).start()

        @pl.when(jnp.logical_not(home))
        def _():
            slot = slot_of(a)
            remote(spot(slot, kind), spot(slot, kind), pass_send.at[kind], w_recv.at[slot, kind], mate, other).wait_recv()
            spread(a, kind, True, True)

    def hop(d, kind):
        @pl.when(a >= d)
        def _():
            plane = jnp.maximum(a - d, 0)
            push(plane, kind, 0).wait_recv()
            spread(plane, kind, True, False)

        @pl.when(a + d < planes)
        def _():
            plane = jnp.minimum(a + d, planes - 1)
            push(plane, kind, 1).wait_recv()
            spread(plane, kind, False, True)

    def from_mate(kind):
        for plane in range(planes):
            slot = 2 * plane + 1 - c
            remote(spot(slot, kind), spot(slot, kind), w_send.at[plane, kind, 2], w_recv.at[slot, kind], mate, s).wait_recv()

    @pl.when(jnp.logical_not(home))
    def _():
        pass_over(0).start()
        pass_over(1).start()

    @pl.when(home)
    def _():
        spread(a, 0, True, True, okv_ref)
        keep_own(0).start()

    def piece(ref, k):
        first, length = ((0, cut), (cut, rows - cut))[k]
        return ref.at[pl.ds(first, length)]

    def along_x(k):
        return remote(piece(own_ref, k), piece(xb_ref, k), tok_send.at[0, k], tok_recv.at[0, k], beside, s)

    def along_y(k):
        return remote(piece(own_ref, k), piece(xa_ref, k), tok_send.at[1, k], tok_recv.at[1, k], f, other)

    def relay_x():
        return remote(piece(xa_ref, 0), piece(xd_ref, 0), tok_send.at[2, 0], tok_recv.at[2, 0], beside, s)

    def relay_y():
        return remote(piece(xb_ref, 1), piece(xd_ref, 1), tok_send.at[2, 1], tok_recv.at[2, 1], f, other)

    def shard_rows(p, mine, first, length):
        ref = ((xd_ref, xb_ref), (xa_ref, own_ref))[p == 0][mine]
        return ref[first:first + length]

    along_x(1).start()
    lax.fori_loop(0, cut // step, normalize, 0)
    along_x(0).start()
    along_y(0).start()

    lane = lax.broadcasted_iota(jnp.int32, (size, HEAD), 1)
    where = a * size + lax.broadcasted_iota(jnp.int32, (size, HEAD), 0)
    by_row = lane < HEAD // 2
    low = (lane < HEAD // 4) | ((lane >= HEAD // 2) & (lane < 3 * HEAD // 4))

    padded = cos_ref.shape[2]
    copies = padded // HEAD

    def tables(p):
        def image(j, carry):
            start, begin, columns = carry
            inside = where >= start
            begin = jnp.where(inside, start, begin)
            columns = jnp.where(inside, widths_ref[packs[p], j], columns)
            return start + blocks_ref[packs[p], j] * BLOCK, begin, columns

        zero = jnp.zeros((size, HEAD), jnp.int32)
        _, begin, columns = lax.fori_loop(0, blocks_ref.shape[1], image, (jnp.int32(0), zero, zero + 1))
        offset = (where - begin).astype(jnp.float32)
        columns = columns.astype(jnp.float32)
        row = jnp.floor((offset + 0.5) / columns)
        col = offset - row * columns
        angle = jnp.where(by_row, row, col) * freq_ref[...]
        cos_ref[p] = jnp.concatenate([jnp.cos(angle)] * copies, axis=1)
        sine = jnp.sin(angle)
        sin_ref[p] = jnp.concatenate([jnp.where(low, -sine, sine)] * copies, axis=1)

    tables(0)
    tables(1)

    @pl.when(jnp.logical_not(home))
    def _():
        slot = slot_of(a)
        remote(spot(slot, 0), spot(slot, 0), pass_send.at[0], w_recv.at[slot, 0], mate, other).wait_recv()
        spread(a, 0, True, True)

    hop(1, 0)

    blank = jnp.zeros((HALO, 2 * width), jnp.bfloat16)

    @pl.when(jnp.logical_not(has_down))
    def _():
        for win in wins:
            win[:HALO] = blank

    @pl.when(jnp.logical_not(has_up))
    def _():
        for win in wins:
            win[HALO + size:] = blank

    begin_ring(1)
    hop(2, 0)
    along_x(1).wait_recv()
    along_y(1).start()
    relay_y().start()
    hop(1, 1)
    along_y(0).wait_recv()
    relay_x().start()
    for d in range(3, planes):
        hop(d - 1, 1)
        hop(d, 0)
    from_mate(0)

    @pl.when(home)
    def _():
        keep_own(0).wait()
        keep_own(1).wait()

    wkv = lambda: wkv_ref[...].reshape(-1, wide)
    wq = lambda: wq_ref[...].reshape(-1, wq_ref.shape[2])

    def turn_heads(raw, gain, at, p):
        along = lax.broadcasted_iota(jnp.int32, raw.shape, 1)
        head = along // HEAD
        first_part = along % (HEAD // 2) < HEAD // 4
        square = raw * raw
        factor = jnp.zeros_like(raw)
        for h in range(heads):
            mean = jnp.sum(jnp.where(head == h, square, 0.0), axis=-1, keepdims=True) * (1.0 / HEAD)
            factor = jnp.where(head == h, lax.rsqrt(mean + eps_model), factor)
        n = raw * factor * jnp.concatenate([gain] * copies, axis=1)
        swapped = jnp.where(first_part, pltpu.roll(n, padded - HEAD // 4, 1), pltpu.roll(n, HEAD // 4, 1))
        return (n * cos_ref[p, at] + swapped * sin_ref[p, at]).astype(jnp.bfloat16)[:, :width]

    def make_keys(p, mine, first, length):
        pos = b if mine else 1 - b
        at = pl.ds(pl.multiple_of(pos * rows + first, 16), length)
        raw = jnp.dot(shard_rows(p, mine, first, length), wkv(), preferred_element_type=jnp.float32)
        done = jnp.concatenate([turn_heads(raw[:, :padded], kg_ref[...], at, p),
                                raw[:, width:2 * width].astype(jnp.bfloat16)], axis=1)
        wins[p][pl.ds(pl.multiple_of(HALO + pos * rows + first, 16), length)] = done
        lead_ref[p, at] = raw[:, 2 * width:]

    def make_queries(p, mine, first, length):
        pos = b if mine else 1 - b
        at = pl.ds(pl.multiple_of(pos * rows + first, 16), length)
        raw = jnp.dot(shard_rows(p, mine, first, length), wq(), preferred_element_type=jnp.float32)
        raw = jnp.concatenate(
            [lead_ref[p, at], raw[:, :width - extra], jnp.zeros((length, padded - width), jnp.float32)], axis=1)
        q_ref[p, at] = turn_heads(raw, qg_ref[...], at, p)

    def upward(p, k):
        return remote(wins[p].at[pl.ds(size + k * BLOCK, BLOCK)], wins[p].at[pl.ds(k * BLOCK, BLOCK)],
                      halo_send.at[p, 0, k], halo_recv.at[p, 0, k], f, s + 2)

    def downward(p, k):
        return remote(wins[p].at[pl.ds(HALO + k * BLOCK, BLOCK)], wins[p].at[pl.ds(HALO + size + k * BLOCK, BLOCK)],
                      halo_send.at[p, 1, k], halo_recv.at[p, 1, k], f, s - 2)

    per = rows // BLOCK
    reach = HALO // BLOCK
    total = size // BLOCK

    def send_block(p, i):
        if i >= total - reach:
            @pl.when(has_up)
            def _():
                upward(p, i - (total - reach)).start()
        if i < reach:
            @pl.when(has_down)
            def _():
                downward(p, i).start()

    def send_shard(p, pos):
        for q in range(2):
            @pl.when(pos == q)
            def _():
                for k in range(per):
                    send_block(p, q * per + k)

    make_keys(0, True, 0, rows)
    send_shard(0, b)
    hop(planes - 1, 1)
    along_y(1).wait_recv()
    make_keys(0, False, 0, rows)
    send_shard(0, 1 - b)
    along_x(0).wait_recv()
    make_keys(1, True, 0, rows)
    send_shard(1, b)
    from_mate(1)
    make_queries(0, True, 0, rows)
    make_queries(0, False, 0, rows)
    make_queries(1, True, 0, rows)

    scale = HEAD ** (-0.5) * 1.4426950408889634

    def attend_block(p, pos, k):
        i = pos * per + k
        first = pl.multiple_of(i * BLOCK, BLOCK)
        where_q = a * size + i * BLOCK

        def image(j, state):
            start, begin, length = state
            inside = where_q >= start
            blocks = blocks_ref[packs[p], j] * BLOCK
            return start + blocks, jnp.where(inside, start, begin), jnp.where(inside, blocks, length)

        _, begin, length = lax.fori_loop(0, blocks_ref.shape[1], image, (jnp.int32(0), jnp.int32(0), jnp.int32(0)))
        back = where_q - begin
        chosen = wins[p][pl.ds(pl.multiple_of(first + HALO, BLOCK), span)]
        for shift in range(BLOCK, HALO + 1, BLOCK):
            earlier = wins[p][pl.ds(pl.multiple_of(first + HALO - shift, BLOCK), span)]
            chosen = jnp.where(back == shift, earlier, chosen)
        mask = lax.broadcasted_iota(jnp.int32, (span, BLOCK), 0) < length
        queries = q_ref[p, pl.ds(first, BLOCK)]
        outs = []
        for h in range(heads):
            keys = chosen[:, h * HEAD:(h + 1) * HEAD]
            vals = chosen[:, width + h * HEAD:width + (h + 1) * HEAD]
            scores = lax.dot_general(keys, queries[:, h * HEAD:(h + 1) * HEAD], (((1,), (1,)), ((), ())),
                                     preferred_element_type=jnp.float32)
            scores = jnp.where(mask, scores, -1e30)
            top = jnp.max(scores, axis=0, keepdims=True)
            expo = jnp.exp2((scores - top) * scale)
            norm = jnp.sum(expo, axis=0, keepdims=True)
            probs = (expo * (1.0 / norm)).astype(jnp.bfloat16)
            outs.append(lax.dot_general(vals, probs, (((0,), (0,)), ((), ())),
                                        preferred_element_type=jnp.float32).astype(jnp.bfloat16))
        mixed[p, pos, k] = jnp.concatenate(outs, axis=0)

    def deliver(p, k, blk):
        pos, seat = (1 - b, other) if k == 0 else (b, s)
        owner = f if p == 0 else beside
        way = 0 if p == 0 else 2 - k
        return remote(mixed.at[p, pos, blk], (land_y, land_x, land_d)[way].at[blk],
                      out_send.at[way, blk], out_recv.at[way, blk], owner, seat)

    def attend(p, k):
        pos = 1 - b if k == 0 else b
        for i in range(per):
            attend_block(p, pos, i)
            if p == 1 or k == 0:
                deliver(p, k, i).start()

    def place_group(group, blocks):
        for g in range(4):
            @pl.when(group == g)
            def _():
                for i in range(per):
                    o_ref[0, i * BLOCK:(i + 1) * BLOCK, g * width:(g + 1) * width] = blocks(i).T

    def halo_wait(p):
        @pl.when(has_down)
        def _():
            for k in range(reach):
                upward(p, k).wait_recv()

        @pl.when(has_up)
        def _():
            for k in range(reach):
                downward(p, k).wait_recv()

    relay_x().wait_recv()
    relay_y().wait_recv()
    make_keys(1, False, 0, rows)
    send_shard(1, 1 - b)
    halo_wait(0)
    attend(0, 0)
    attend(0, 1)
    make_queries(1, False, 0, rows)
    place_group(2 * x + b, lambda i: mixed[0, b, i])
    for i in range(per):
        deliver(0, 0, i).wait_recv()
    place_group(2 * x + 1 - b, lambda i: land_y[i])
    halo_wait(1)
    attend(1, 0)
    attend(1, 1)

    def drain(plane, carry):
        for kind in range(2):
            @pl.when((plane <= a) & has_up)
            def _():
                push(plane, kind, 0).wait_send()

            @pl.when((plane >= a) & has_down)
            def _():
                push(plane, kind, 1).wait_send()

            push(plane, kind, 2).wait_send()
        return carry

    lax.fori_loop(0, planes, drain, 0)

    @pl.when(jnp.logical_not(home))
    def _():
        pass_over(0).wait_send()
        pass_over(1).wait_send()

    for k in range(2):
        along_x(k).wait_send()
        along_y(k).wait_send()
    relay_x().wait_send()
    relay_y().wait_send()
    for p in range(2):
        for k in range(reach):
            @pl.when(has_up)
            def _():
                upward(p, k).wait_send()

            @pl.when(has_down)
            def _():
                downward(p, k).wait_send()

    for i in range(per):
        deliver(1, 1, i).wait_recv()
    place_group(2 * (1 - x) + b, lambda i: land_x[i])
    for i in range(per):
        deliver(1, 0, i).wait_recv()
    place_group(2 * (1 - x) + 1 - b, lambda i: land_d[i])
    for i in range(per):
        deliver(0, 0, i).wait_send()
        deliver(1, 0, i).wait_send()
        deliver(1, 1, i).wait_send()


def fused(planes, tokens, norm_gain, w_qkv, q_gain, k_gain, img_blocks, img_width):
    row_count, model = tokens.shape[1], tokens.shape[2]
    depth, width = w_qkv.shape[1], w_qkv.shape[2]
    size = 2 * row_count
    wide = pl.cdiv(2 * width, 128) * 128
    tail = pl.cdiv(3 * width - wide, 128) * 128
    quarter = HEAD // 4
    freq = np.tile(np.float32(10000.0) ** (-np.arange(quarter, dtype=np.float32) / np.float32(quarter)), 4)[None]
    vmem = pl.BlockSpec(memory_space=pltpu.VMEM)
    smem = pl.BlockSpec(memory_space=pltpu.SMEM)
    anywhere = pl.BlockSpec(memory_space=pl.ANY)
    dma = pltpu.SemaphoreType.DMA
    return pl.pallas_call(
        functools.partial(fused_kernel, planes),
        out_shape=jax.ShapeDtypeStruct((1, row_count, 4 * width), jnp.bfloat16),
        in_specs=[anywhere] * 6 + [smem] * 2,
        out_specs=vmem,
        scratch_shapes=[
            pltpu.VMEM(tokens.shape, jnp.bfloat16),
            pltpu.VMEM(norm_gain.shape, jnp.float32),
            pltpu.VMEM(w_qkv.shape, jnp.bfloat16),
            pltpu.VMEM((1, HEAD), jnp.float32),
            pltpu.VMEM((1, HEAD), jnp.float32),
            pltpu.VMEM((1, HEAD), jnp.float32),
            dma((6,)),
            pltpu.VMEM((row_count, model), jnp.bfloat16),
            pltpu.VMEM((row_count, model), jnp.bfloat16),
            pltpu.VMEM((row_count, model), jnp.bfloat16),
            pltpu.VMEM((row_count, model), jnp.bfloat16),
            pltpu.VMEM((2 * planes, depth, wide), jnp.bfloat16),
            pltpu.VMEM((2 * planes, depth, tail), jnp.bfloat16),
            pltpu.VMEM((depth, wide), jnp.bfloat16),
            pltpu.VMEM((depth, tail), jnp.bfloat16),
            pltpu.VMEM((2, size, pl.cdiv(width, 128) * 128), jnp.float32),
            pltpu.VMEM((2, size, pl.cdiv(width, 128) * 128), jnp.float32),
            pltpu.VMEM((2, size, width), jnp.bfloat16),
            pltpu.VMEM((2, size, wide - 2 * width), jnp.float32),
            pltpu.VMEM((size + 2 * HALO, 2 * width), jnp.bfloat16),
            pltpu.VMEM((size + 2 * HALO, 2 * width), jnp.bfloat16),
            pltpu.VMEM((2, 2, row_count // BLOCK, width, BLOCK), jnp.bfloat16),
            pltpu.VMEM((row_count // BLOCK, width, BLOCK), jnp.bfloat16),
            pltpu.VMEM((row_count // BLOCK, width, BLOCK), jnp.bfloat16),
            pltpu.VMEM((row_count // BLOCK, width, BLOCK), jnp.bfloat16),
            dma((3, 2)),
            dma((3, 2)),
            dma((planes, 2, 3)),
            dma((2 * planes, 2)),
            dma((2,)),
            dma((2, 2, HALO // BLOCK)),
            dma((2, 2, HALO // BLOCK)),
            dma((3, row_count // BLOCK)),
            dma((3, row_count // BLOCK)),
            dma((3,)),
        ],
        compiler_params=pltpu.CompilerParams(
            collective_id=0, has_side_effects=True, vmem_limit_bytes=60 * 1024 * 1024),
        name="fused",
    )(tokens, norm_gain, w_qkv, q_gain[None], k_gain[None], jnp.asarray(freq), img_blocks, img_width)


def shards(planes, tokens, norm_gain, w_qkv, q_gain, k_gain, img_blocks, img_width):
    row_count, model = tokens.shape[1], tokens.shape[2]
    width = w_qkv.shape[2]
    size = 2 * row_count
    seqs = 2 * planes
    depth = w_qkv.shape[1]
    broad = pl.cdiv(3 * width, 128) * 128
    quarter = HEAD // 4
    freq = np.tile(np.float32(10000.0) ** (-np.arange(quarter, dtype=np.float32) / np.float32(quarter)), 4)[None]
    vmem = pl.BlockSpec(memory_space=pltpu.VMEM)
    smem = pl.BlockSpec(memory_space=pltpu.SMEM)
    anywhere = pl.BlockSpec(memory_space=pl.ANY)
    table = jax.ShapeDtypeStruct((2, size, HEAD), jnp.float32)
    gathered, weights, cosine, sine = pl.pallas_call(
        functools.partial(gather_kernel, planes),
        out_shape=(
            jax.ShapeDtypeStruct((2, 2, row_count, model), jnp.bfloat16),
            jax.ShapeDtypeStruct((seqs, depth, broad), jnp.bfloat16),
            table,
            table,
        ),
        in_specs=[vmem, vmem, vmem, smem, smem, vmem],
        out_specs=(anywhere, anywhere, vmem, vmem),
        scratch_shapes=[
            pltpu.VMEM((row_count, model), jnp.bfloat16),
            pltpu.VMEM((depth, broad), jnp.bfloat16),
            pltpu.SemaphoreType.DMA((7,)),
            pltpu.SemaphoreType.DMA((7,)),
            pltpu.SemaphoreType.DMA((seqs, 3)),
            pltpu.SemaphoreType.DMA((seqs,)),
            pltpu.SemaphoreType.DMA((2,)),
        ],
        compiler_params=pltpu.CompilerParams(collective_id=0, has_side_effects=True),
        name="gather",
    )(tokens, norm_gain, w_qkv, img_blocks, img_width, jnp.asarray(freq))
    attended = pl.pallas_call(
        functools.partial(attend_kernel, planes),
        out_shape=jax.ShapeDtypeStruct((1, row_count, 4 * width), jnp.bfloat16),
        in_specs=[anywhere, anywhere, vmem, vmem, vmem, vmem, smem],
        out_specs=vmem,
        scratch_shapes=[
            pltpu.VMEM((2, size, model), jnp.bfloat16),
            pltpu.VMEM((model, broad), jnp.bfloat16),
            pltpu.VMEM((2, size, width), jnp.bfloat16),
            pltpu.VMEM((size + 2 * HALO, 2 * width), jnp.bfloat16),
            pltpu.VMEM((size + 2 * HALO, 2 * width), jnp.bfloat16),
            pltpu.VMEM((2, size, width), jnp.bfloat16),
            pltpu.VMEM((4, row_count, width), jnp.bfloat16),
            pltpu.SemaphoreType.DMA((2, 2)),
            pltpu.SemaphoreType.DMA((2, 2)),
            pltpu.SemaphoreType.DMA((2, 2)),
            pltpu.SemaphoreType.DMA((4,)),
            pltpu.SemaphoreType.DMA((3,)),
            pltpu.SemaphoreType.DMA((3,)),
        ],
        compiler_params=pltpu.CompilerParams(collective_id=1, has_side_effects=True),
        name="attend",
    )(gathered.reshape(2, size, model), weights.reshape(model, broad), cosine, sine,
      q_gain[None], k_gain[None], img_blocks)
    return attended


def solution(mesh):
    assert mesh.shape["fsdp"] == 4 and mesh.shape["seq"] % 2 == 0
    planes = mesh.shape["seq"] // 2

    def body(tokens, norm_gain, w_qkv, *rest):
        whole_tiles = w_qkv.shape[1] % 16 == 0 and 2 * w_qkv.shape[2] % 128 != 0 and -w_qkv.shape[2] % 128 == HEAD
        return (fused if whole_tiles else shards)(planes, tokens, norm_gain, w_qkv, *rest)

    return jax.shard_map(
        body,
        mesh=mesh,
        in_specs=(P("fsdp", "seq", None), P(), P(None, "seq", "fsdp"), P(), P(), P(), P()),
        out_specs=P("fsdp", "seq", None),
        check_vma=False,
    )
```
